128 devices in a mesh: cam: 16 (over y, x), pts: 8 (over z, core).
Axes of the slice: x: 4, y: 4, z: 4, core: 2. Of those that a mesh axis runs over, the one named last changes fastest.
Arguments:
- rhs: float32 [9, 131072], P(None, 'cam'), may hold values from -6 to 6
- cam_block: float32 [9, 9, 131072], P(None, None, 'cam'), as said below
- coupling: bfloat16 [512, 144, 12288], P('pts', None, 'cam'), may hold values from -0.03125 to 0.03125
- point_inverse: float32 [3, 3, 32768], P(None, None, 'pts'), as said below
- precond: float32 [9, 9, 131072], P(None, None, 'cam'), as said below
- tile_index: int32 [512, 64], P('pts', 'cam'), may hold values from 0 to 511
- tile_count: int32 [512, 16], P('pts', 'cam'), may hold values from 1 to 4, as said below
Outputs:
- solution: float32 [9, 131072], P(None, 'cam')
- residual: float32 [9, 131072], P(None, 'cam')
The draws below stay inside these ranges and needn't reach their ends.
Inputs may be any that keep to these rules, and one draw needn't show every extreme that they name: `tile_count`: every entry is at least 1 and at most 4; both ends occur. `cam_block`: symmetric with a dominant positive diagonal for each camera. `precond`: symmetric with a dominant positive diagonal for each camera. `point_inverse`: symmetric with a dominant positive diagonal for each point.
All inputs are finite; a program needn't handle non-finite values.
Results may differ from the reference program's by a relative error of at most 0.0024.
Values may be sent and summed in bfloat16 or wider, within the bound.
A program may use at most 128 MiB of HBM per device.

```python
import jax
import jax.numpy as jnp
from jax import lax

CAM_TILES = 512
PT_TILES = 64
SLOTS = 4
ITERS = 3
CAMS = 131072
POINT_TILES = 512
POINTS = 32768
SLOT_COLS = 64
N_CAM = 16
N_PTS = 8


def dominant_block(key, size, count, diag_lo, diag_hi, off_size):
    first, second = jax.random.split(key)
    diagonal = jax.random.uniform(first, (size, count), jnp.float32, diag_lo, diag_hi)
    offdiag = jax.random.uniform(second, (size, size, count), jnp.float32, -off_size, off_size)
    symmetric = (offdiag + offdiag.transpose(1, 0, 2)) * 0.5
    square_eye = jnp.arange(size)[:, None] == jnp.arange(size)[None, :]
    return jnp.where(square_eye[:, :, None], diagonal[:, None, :], symmetric)


def draw_cam_block(key, part):
    return dominant_block(key, 9, CAMS, 2.0, 4.0, 0.15)


def draw_precond(key, part):
    return dominant_block(key, 9, CAMS, 0.25, 0.5, 0.02)


def draw_point_inverse(key, part):
    return dominant_block(key, 3, POINTS, 0.5, 2.0, 0.2)


def draw_tile_count(key, part):
    counts = jax.random.randint(key, (POINT_TILES * N_CAM,), 1, SLOTS + 1, dtype=jnp.int32)
    counts = counts.at[0].set(SLOTS).at[1].set(1)
    return counts.reshape(POINT_TILES, N_CAM)


def touch_ends(drawn, own_key, low, largest):
    longest = drawn.shape.index(max(drawn.shape))
    spots = []
    for shift in (0, 1):
        where = [jax.random.randint(jax.random.fold_in(own_key, axis), (), 0, length) for axis, length in enumerate(drawn.shape)]
        where[longest] = (where[longest] + shift) % drawn.shape[longest]
        spots.append(tuple(where))
    return drawn.at[spots[0]].set(low).at[spots[1]].set(largest)


def block_levels(own_key, extent, cuts, low, high):
    gain, own = 1.0, jax.random.fold_in(own_key, 6)
    for axis_at, blocks in cuts:
        steps = jnp.exp(jax.random.uniform(jax.random.fold_in(own, axis_at), (blocks,), jnp.float32, low / len(cuts), high / len(cuts)))
        gain = gain * jnp.repeat(steps, extent[axis_at] // blocks).reshape([-1 if axis == axis_at else 1 for axis in range(len(extent))])
    return gain


def gaussian(key, shape, scale, reach, cuts=(), kind=jnp.bfloat16):
    result = jax.random.normal(key, shape, jnp.float32) * scale
    if len(cuts) > 0:
        result = block_levels(key, shape, cuts, -0.22, 0.18) * result
    return jnp.clip(result, min=-reach, max=reach).astype(kind)


def setup_inputs(seed: int = 0) -> dict:
    arg_keys = jax.random.split(jax.random.key(seed), 8)
    rhs = gaussian(arg_keys[0], (9, CAMS), 1.0, 6.0, ((1, 16),), jnp.float32)
    cam_block = draw_cam_block(jax.random.fold_in(arg_keys[7], 71), 0)
    coupling = gaussian(arg_keys[2], (POINT_TILES, 144, SLOT_COLS * 192), (4 * (N_CAM * SLOTS * 144 + PT_TILES * SLOTS * N_PTS * 192 // CAM_TILES)) ** -0.5, 0.03125, ((0, 8), (2, 16)))
    point_inverse = draw_point_inverse(jax.random.fold_in(arg_keys[7], 71), 0)
    precond = draw_precond(jax.random.fold_in(arg_keys[7], 71), 0)
    tile_index = touch_ends(jax.random.randint(arg_keys[5], (POINT_TILES, SLOT_COLS), 0, CAM_TILES), jax.random.fold_in(arg_keys[5], 1), 0, CAM_TILES - 1).astype(jnp.int32)
    tile_count = draw_tile_count(jax.random.fold_in(arg_keys[7], 71), 0)
    return {"rhs": rhs, "cam_block": cam_block, "coupling": coupling, "point_inverse": point_inverse, "precond": precond, "tile_index": tile_index, "tile_count": tile_count}


def to_tiles(vector, width):
    comps, count = vector.shape
    return vector.reshape(comps, count // width, width).transpose(1, 0, 2).reshape(count // width, comps * width)


def from_tiles(tiles, comps):
    count, cols = tiles.shape
    width = cols // comps
    return tiles.reshape(count, comps, width).transpose(1, 0, 2).reshape(comps, count * width)


def reference(rhs, cam_block, coupling, point_inverse, precond, tile_index, tile_count):
    slot_cols = tile_index.shape[1]
    slot_pos = jnp.arange(slot_cols, dtype=jnp.int32)
    slot_group = slot_pos // SLOTS
    within = slot_pos % SLOTS
    global_tile = slot_group[None, :] * CAM_TILES + tile_index
    usable = (within[None, :] < tile_count[:, slot_group]).astype(jnp.float32)
    grouped = coupling.reshape(N_PTS, PT_TILES, 144, slot_cols, 192)

    def forward_block(pair):
        block, dir_rows = pair
        return jnp.einsum("sckp,skc->sp", block.astype(jnp.float32), dir_rows.astype(jnp.float32), precision=lax.Precision.HIGHEST)

    def backward_block(pair):
        block, solved_rows = pair
        return jnp.einsum("sckp,sp->skc", block.astype(jnp.float32), solved_rows.astype(jnp.float32), precision=lax.Precision.HIGHEST)

    def schur_apply(direction):
        dir_half = direction.astype(jnp.bfloat16)
        dir_tiles = to_tiles(dir_half, 16)
        dir_rows = dir_tiles[global_tile] * usable[:, :, None].astype(jnp.bfloat16)
        point_sum = lax.map(forward_block, (grouped, dir_rows.reshape(N_PTS, PT_TILES, slot_cols, 144)))
        point_sum = from_tiles(point_sum.reshape(N_PTS * PT_TILES, 192), 3)
        solved = jnp.sum(point_inverse * point_sum[None, :, :], axis=1).astype(jnp.bfloat16)
        solved_tiles = to_tiles(solved, 64).reshape(N_PTS, PT_TILES, 192)
        contrib = lax.map(backward_block, (grouped, solved_tiles))
        contrib = contrib.reshape(-1, 144) * usable.reshape(-1, 1)
        cam_tiles = jax.ops.segment_sum(contrib, global_tile.reshape(-1), num_segments=CAM_TILES * N_CAM)
        cam_term = from_tiles(cam_tiles, 9)
        return jnp.sum(cam_block * direction[None, :, :], axis=1) - cam_term

    solution = jnp.zeros_like(rhs)
    residual = rhs
    precond_res = jnp.sum(precond * residual[None, :, :], axis=1)
    direction = precond_res
    inner_now = jnp.sum(residual * precond_res)
    for iteration in range(ITERS):
        image = schur_apply(direction)
        step_size = inner_now / jnp.sum(direction * image)
        solution = solution + step_size * direction
        residual = residual - step_size * image
        if iteration + 1 < ITERS:
            precond_res = jnp.sum(precond * residual[None, :, :], axis=1)
            inner_new = jnp.sum(residual * precond_res)
            direction = precond_res + (inner_new / inner_now) * direction
            inner_now = inner_new
    return solution, residual
```

```python
import functools

import jax
import jax.numpy as jnp
from jax import lax
from jax.experimental import pallas as pl
from jax.experimental.pallas import tpu as pltpu
from jax.sharding import PartitionSpec as P

ITERS = 3
F32 = jnp.float32
BF16 = jnp.bfloat16
CHUNKS = 16
MESH = pl.DeviceIdType.MESH


def iota(shape, axis):
    return lax.broadcasted_iota(jnp.int32, shape, axis)


def kernel(
    n_cam, n_pts,
    rhs_ref, inv_ref, idx_col_ref, idx_row_ref, cam_hbm, pre_hbm, blk_hbm,
    sol_out, res_out,
    blk, cam_nat, pre_nat, cam_d, pre_d,
    r_ref, z_ref, d_ref, s_ref, q_ref, u_ref, cd_ref,
    pick, place, mask, fold, fold_t, group,
    gath, rows, mid, contrib,
    p_send, p_recv, solved, t_send, t_recv, term, dots,
    blk_sem, cam_sem, pre_sem,
    ps_s, ps_r, so_s, so_r, ts_s, ts_r, te_s, te_r, do_s, do_r,
):
    me_c = lax.axis_index("cam")
    me_p = lax.axis_index("pts")
    blocks = d_ref.shape[0] // 9
    steps = blocks // 8
    tiles = blk.shape[0]
    per_chunk = tiles // CHUNKS

    pre_copy = pltpu.make_async_copy(pre_hbm, pre_nat, pre_sem)
    cam_copy = pltpu.make_async_copy(cam_hbm, cam_nat, cam_sem)

    def blk_copy(c):
        part = pl.ds(c * per_chunk, per_chunk)
        return pltpu.make_async_copy(blk_hbm.at[part], blk.at[part], blk_sem.at[c])

    pre_copy.start()

    def start_chunk(c, carry):
        blk_copy(c).start()
        return carry

    lax.fori_loop(0, CHUNKS, start_chunk, 0)
    cam_copy.start()

    barrier = pltpu.get_barrier_semaphore()

    def cam_peer(k):
        return lax.rem(me_c + k, n_cam)

    def pts_peer(k):
        return lax.rem(me_p + k, n_pts)

    def greet_cam(k, carry):
        pl.semaphore_signal(barrier, inc=1, device_id=(cam_peer(k), me_p), device_id_type=MESH)
        return carry

    def greet_pts(k, carry):
        pl.semaphore_signal(barrier, inc=1, device_id=(me_c, pts_peer(k)), device_id_type=MESH)
        return carry

    lax.fori_loop(1, n_cam, greet_cam, 0)
    lax.fori_loop(1, n_pts, greet_pts, 0)

    def cam_send(k, src, dst, ssem, rsem):
        peer = cam_peer(k)
        return pltpu.make_async_remote_copy(
            src_ref=src(peer), dst_ref=dst.at[me_c], send_sem=ssem.at[peer],
            recv_sem=rsem.at[me_c], device_id=(peer, me_p), device_id_type=MESH,
        )

    def cam_arrive(k, src, dst, ssem, rsem):
        peer = cam_peer(k)
        return pltpu.make_async_remote_copy(
            src_ref=src(peer), dst_ref=dst.at[peer], send_sem=ssem.at[peer],
            recv_sem=rsem.at[peer], device_id=(peer, me_p), device_id_type=MESH,
        )

    def pts_send(k, src, dst, ssem, rsem):
        peer = pts_peer(k)
        return pltpu.make_async_remote_copy(
            src_ref=src(peer), dst_ref=dst.at[me_p], send_sem=ssem.at[peer],
            recv_sem=rsem.at[me_p], device_id=(me_c, peer), device_id_type=MESH,
        )

    def pts_arrive(k, src, dst, ssem, rsem):
        peer = pts_peer(k)
        return pltpu.make_async_remote_copy(
            src_ref=src(peer), dst_ref=dst.at[peer], send_sem=ssem.at[peer],
            recv_sem=rsem.at[peer], device_id=(me_c, peer), device_id_type=MESH,
        )

    def start_all(n, send, *args):
        def body(k, carry):
            send(k, *args).start()
            return carry

        lax.fori_loop(1, n, body, 0)

    def wait_all(n, arrive, *args):
        def body(k, carry):
            copy = arrive(k, *args)
            copy.wait_recv()
            copy.wait_send()
            return carry

        lax.fori_loop(1, n, body, 0)

    idx_col = idx_col_ref[...]
    idx_row = idx_row_ref[...]
    pairs = idx_col.shape[0]
    pick[...] = jnp.where(iota((pairs, blocks), 1) == idx_col // 8, 1.0, 0.0).astype(BF16)
    place[...] = jnp.where(iota((blocks, pairs), 0) == idx_row // 8, 1.0, 0.0).astype(BF16)
    mask[...] = jnp.where(iota((pairs, 128), 1) // 16 == lax.rem(idx_col + 8, 8), 1.0, 0.0)
    at = iota((9 * 128, 144), 0)
    fold[...] = jnp.where(
        iota((9 * 128, 144), 1) == (at // 128) * 16 + lax.rem(at, 16), 1.0, 0.0
    ).astype(BF16)
    at = iota((144, 9 * 128), 1)
    fold_t[...] = jnp.where(
        iota((144, 9 * 128), 0) == (at // 128) * 16 + lax.rem(at, 16), 1.0, 0.0
    ).astype(BF16)
    group[...] = jnp.where(iota((tiles, pairs), 1) // 4 == iota((tiles, pairs), 0), 1.0, 0.0).astype(
        BF16
    )

    def to_dense(src, dst):
        def body(b, carry):
            dst[pl.ds(b, 9, stride=blocks), :] = src[:, pl.ds(pl.multiple_of(b * 128, 128), 128)]
            return carry

        lax.fori_loop(0, blocks, body, 0, unroll=4)

    def to_dense_blocks(src, dst):
        def body(b, carry):
            for i in range(9):
                dst[i, pl.ds(b, 9, stride=blocks), :] = src[
                    i, :, pl.ds(pl.multiple_of(b * 128, 128), 128)
                ]
            return carry

        lax.fori_loop(0, blocks, body, 0)

    def at_rows(j, step):
        return pl.ds(pl.multiple_of(j * blocks + step * 8, 8), 8)

    def apply_rows(mat, vec, i, step):
        total = mat[i, at_rows(0, step), :] * vec[0]
        for j in range(1, 9):
            total = total + mat[i, at_rows(j, step), :] * vec[j]
        return total

    to_dense(rhs_ref, r_ref)
    pre_copy.wait()
    to_dense_blocks(pre_nat, pre_d)

    def first(step, acc):
        r = [r_ref[at_rows(j, step), :] for j in range(9)]
        for i in range(9):
            z = apply_rows(pre_d, r, i, step)
            z_ref[at_rows(i, step), :] = z
            d_ref[at_rows(i, step), :] = z
            acc = acc + r[i] * z
        return acc

    rz = lax.fori_loop(0, steps, first, jnp.zeros((8, 128), F32))
    pl.semaphore_wait(barrier, n_cam + n_pts - 2)

    row8 = iota((8, 768), 0)
    diag = iota((8, 768), 1) // 192 == lax.rem(row8, 4)
    upper = row8 < 4

    inner = None
    for it in range(ITERS):
        last = it + 1 == ITERS
        for j in range(9):
            part = d_ref[j * blocks : (j + 1) * blocks, :].astype(BF16)
            picked = jnp.dot(pick[...], part, preferred_element_type=F32)
            gath[:, j * 128 : (j + 1) * 128] = (picked * mask[...]).astype(BF16)
        rows[...] = jnp.dot(gath[...], fold[...], preferred_element_type=F32)

        def forward(j):
            left = rows[pl.ds(pl.multiple_of(8 * j, 8), 8), :].astype(BF16)
            one = jnp.dot(left, blk[2 * j], preferred_element_type=F32)
            two = jnp.dot(left, blk[2 * j + 1], preferred_element_type=F32)
            mid[pl.ds(pl.multiple_of(8 * j, 8), 8), :] = jnp.where(
                diag, jnp.where(upper, one, two), 0.0
            )

        def forward_chunk(c, carry):
            if it == 0:
                blk_copy(c).wait()
            for k in range(per_chunk // 2):
                forward(c * (per_chunk // 2) + k)
            return carry

        lax.fori_loop(0, CHUNKS, forward_chunk, 0, unroll=1 if it == 0 else 2)
        full = mid[...]
        high = full.astype(BF16)
        low = (full - high.astype(F32)).astype(BF16)
        summed = jnp.dot(group[...], high, preferred_element_type=F32) + jnp.dot(
            group[...], low, preferred_element_type=F32
        )
        summed = summed[:, :384] + summed[:, 384:]
        summed = summed + pltpu.roll(summed, 192, 1)
        slab = tiles // n_cam
        for o in range(n_cam):
            p_send[o] = summed[o * slab : (o + 1) * slab, :]
        own = (lambda peer: p_send.at[peer], p_recv, ps_s, ps_r)
        start_all(n_cam, cam_send, *own)

        if it == 0:
            cam_copy.wait()
            to_dense_blocks(cam_nat, cam_d)

        def cam_apply(step, carry):
            d = [d_ref[at_rows(j, step), :] for j in range(9)]
            for i in range(9):
                cd_ref[at_rows(i, step), :] = apply_rows(cam_d, d, i, step)
            return carry

        lax.fori_loop(0, steps, cam_apply, 0)

        wait_all(n_cam, cam_arrive, *own)
        total = p_send[me_c]
        for k in range(1, n_cam):
            total = total + p_recv[cam_peer(k)]
        answer = inv_ref[0] * total
        for k in (1, 2):
            answer = answer + inv_ref[k] * pltpu.roll(total, 384 - 64 * k, 1)
        solved[me_c] = answer.astype(BF16).astype(F32)
        own = (lambda peer: solved.at[me_c], solved, so_s, so_r)
        start_all(n_cam, cam_send, *own)
        wait_all(n_cam, cam_arrive, *own)

        def backward(j, carry):
            q4 = lax.rem(j, 2) * 2
            one = jnp.broadcast_to(solved[j // 2, pl.ds(q4, 1), :], (8, 384))
            two = jnp.broadcast_to(solved[j // 2, pl.ds(q4 + 1, 1), :], (8, 384))
            both = jnp.where(upper[:, :384], one, two)
            left = jnp.where(diag, jnp.concatenate([both, both], axis=1), 0.0).astype(BF16)
            contract = (((1,), (1,)), ((), ()))
            one = lax.dot_general(left, blk[2 * j], contract, preferred_element_type=F32)
            two = lax.dot_general(left, blk[2 * j + 1], contract, preferred_element_type=F32)
            contrib[pl.ds(pl.multiple_of(8 * j, 8), 8), :] = jnp.where(
                upper[:, :144], one, two
            )
            return carry

        lax.fori_loop(0, tiles // 2, backward, 0, unroll=4)
        contrib_half = contrib[...].astype(BF16)
        for j in range(9):
            lanes = slice(j * 128, (j + 1) * 128)
            wide = jnp.dot(contrib_half, fold_t[:, lanes], preferred_element_type=F32)
            wide = (wide * mask[...]).astype(BF16)
            put = jnp.dot(place[...], wide, preferred_element_type=F32)
            for o in range(n_pts):
                t_send[o, :, lanes] = put[o * 8 : (o + 1) * 8, :].astype(BF16)
        own = (lambda peer: t_send.at[peer], t_recv, ts_s, ts_r)
        start_all(n_pts, pts_send, *own)
        wait_all(n_pts, pts_arrive, *own)
        total = t_send[me_p].astype(F32)
        for k in range(1, n_pts):
            total = total + t_recv[pts_peer(k)].astype(F32)
        term[me_p] = total.astype(BF16)
        own = (lambda peer: term.at[me_p], term, te_s, te_r)
        start_all(n_pts, pts_send, *own)
        wait_all(n_pts, pts_arrive, *own)

        def image(step, acc):
            dq, zq, uq = acc
            q = []
            for i in range(9):
                value = cd_ref[at_rows(i, step), :] - term[step, :, i * 128 : (i + 1) * 128].astype(
                    F32
                )
                q_ref[at_rows(i, step), :] = value
                q.append(value)
                dq = dq + d_ref[at_rows(i, step), :] * value
            if not last:
                for i in range(9):
                    u = apply_rows(pre_d, q, i, step)
                    u_ref[at_rows(i, step), :] = u
                    zq = zq + z_ref[at_rows(i, step), :] * q[i]
                    uq = uq + u * q[i]
            return dq, zq, uq

        zero = jnp.zeros((8, 128), F32)
        dq, zq, uq = lax.fori_loop(0, steps, image, (zero, zero, zero))
        dots[me_c, 0:1, :] = jnp.sum(dq, axis=0, keepdims=True)
        dots[me_c, 1:2, :] = jnp.sum(zq, axis=0, keepdims=True)
        dots[me_c, 2:3, :] = jnp.sum(uq, axis=0, keepdims=True)
        dots[me_c, 3:4, :] = jnp.sum(rz, axis=0, keepdims=True)
        own = (lambda peer: dots.at[me_c], dots, do_s, do_r)
        start_all(n_cam, cam_send, *own)
        wait_all(n_cam, cam_arrive, *own)
        total = dots[0]
        for k in range(1, n_cam):
            total = total + dots[k]
        total = jnp.sum(total, axis=1, keepdims=True)
        if it == 0:
            inner = total[3:4]
        size = inner / total[0:1]
        alpha = jnp.broadcast_to(size, (8, 128))
        if not last:
            inner_new = inner - 2.0 * size * total[1:2] + size * size * total[2:3]
            beta = jnp.broadcast_to(inner_new / inner, (8, 128))
            inner = inner_new

        def update(step, carry):
            for i in range(9):
                at_i = at_rows(i, step)
                d = d_ref[at_i, :]
                s = alpha * d
                if it > 0:
                    s = s_ref[at_i, :] + s
                s_ref[at_i, :] = s
                r_ref[at_i, :] = r_ref[at_i, :] - alpha * q_ref[at_i, :]
                if not last:
                    z = z_ref[at_i, :] - alpha * u_ref[at_i, :]
                    z_ref[at_i, :] = z
                    d_ref[at_i, :] = z + beta * d
            return carry

        lax.fori_loop(0, steps, update, 0)

    def from_dense(b, carry):
        lanes = pl.ds(pl.multiple_of(b * 128, 128), 128)
        sol_out[:, lanes] = s_ref[pl.ds(b, 9, stride=blocks), :]
        res_out[:, lanes] = r_ref[pl.ds(b, 9, stride=blocks), :]
        return carry

    lax.fori_loop(0, blocks, from_dense, 0, unroll=4)


def per_device(n_cam, n_pts, rhs, cam_block, coupling, point_inverse, precond, tile_index, tile_count):
    tiles, slots = tile_index.shape
    cams = rhs.shape[1]
    blocks = cams // 128
    slab = tiles // n_cam
    used = jnp.arange(slots)[None, :] < tile_count
    index = jnp.where(used, tile_index, -8)
    pairs = tiles * slots
    own = lax.dynamic_slice_in_dim(point_inverse, lax.axis_index("cam") * slab * 64, slab * 64, 2)
    own = own.reshape(3, 3, slab, 64)
    turned = [
        jnp.concatenate([own[i % 3, (i + k) % 3] for i in range(6)], axis=1) for k in range(3)
    ]
    inv = jnp.stack(turned)
    vec = pltpu.VMEM((9 * blocks, 128), F32)
    whole = pl.BlockSpec(memory_space=pltpu.VMEM)
    hbm = pl.BlockSpec(memory_space=pl.ANY)
    dma = pltpu.SemaphoreType.DMA
    return pl.pallas_call(
        functools.partial(kernel, n_cam, n_pts),
        out_shape=(jax.ShapeDtypeStruct(rhs.shape, F32), jax.ShapeDtypeStruct(rhs.shape, F32)),
        in_specs=[whole, whole, whole, whole, hbm, hbm, hbm],
        out_specs=(whole, whole),
        scratch_shapes=[
            pltpu.VMEM(coupling.shape, BF16),
            pltpu.VMEM(cam_block.shape, F32),
            pltpu.VMEM(precond.shape, F32),
            pltpu.VMEM((9, 9 * blocks, 128), F32),
            pltpu.VMEM((9, 9 * blocks, 128), F32),
            vec, vec, vec, vec, vec, vec, vec,
            pltpu.VMEM((pairs, blocks), BF16),
            pltpu.VMEM((blocks, pairs), BF16),
            pltpu.VMEM((pairs, 128), F32),
            pltpu.VMEM((9 * 128, 144), BF16),
            pltpu.VMEM((144, 9 * 128), BF16),
            pltpu.VMEM((tiles, pairs), BF16),
            pltpu.VMEM((pairs, 9 * 128), BF16),
            pltpu.VMEM((pairs, 144), F32),
            pltpu.VMEM((pairs, 768), F32),
            pltpu.VMEM((pairs, 144), F32),
            pltpu.VMEM((n_cam, slab, 384), F32),
            pltpu.VMEM((n_cam, slab, 384), F32),
            pltpu.VMEM((n_cam, slab, 384), F32),
            pltpu.VMEM((n_pts, blocks // n_pts, 9 * 128), BF16),
            pltpu.VMEM((n_pts, blocks // n_pts, 9 * 128), BF16),
            pltpu.VMEM((n_pts, blocks // n_pts, 9 * 128), BF16),
            pltpu.VMEM((n_cam, 4, 128), F32),
            dma((CHUNKS,)), dma, dma,
            dma((n_cam,)), dma((n_cam,)), dma((n_cam,)), dma((n_cam,)),
            dma((n_pts,)), dma((n_pts,)), dma((n_pts,)), dma((n_pts,)),
            dma((n_cam,)), dma((n_cam,)),
        ],
        compiler_params=pltpu.CompilerParams(
            collective_id=0, has_side_effects=True, vmem_limit_bytes=58 * 2**20
        ),
    )(rhs, inv, index.reshape(pairs, 1), index.reshape(1, pairs), cam_block, precond, coupling)


def solution(mesh):
    in_specs = (
        P(None, "cam"),
        P(None, None, "cam"),
        P("pts", None, "cam"),
        P(None, None, "pts"),
        P(None, None, "cam"),
        P("pts", "cam"),
        P("pts", "cam"),
    )
    out_specs = (P(None, "cam"), P(None, "cam"))
    body = functools.partial(per_device, mesh.shape["cam"], mesh.shape["pts"])
    return jax.shard_map(body, mesh=mesh, in_specs=in_specs, out_specs=out_specs, check_vma=False)
```

```python
import functools

import jax
import jax.numpy as jnp
from jax import lax
from jax.experimental import pallas as pl
from jax.experimental.pallas import tpu as pltpu
from jax.sharding import PartitionSpec as P

ITERS = 3
F32 = jnp.float32
BF16 = jnp.bfloat16
CHUNKS = 16
HALVES = 2
MESH = pl.DeviceIdType.MESH


def iota(shape, axis):
    return lax.broadcasted_iota(jnp.int32, shape, axis)


def one_hot(where):
    return jnp.where(where, 1.0, 0.0).astype(BF16)


def kernel(
    n_cam, n_pts,
    idx_ref, count_ref, rhs_hbm, inv_hbm, cam_hbm, pre_hbm, blk_hbm,
    sol_out, res_out,
    blk, cam_nat, pre_nat, rhs_nat, inv_nat, cam_d, pre_d, inv_d,
    r_ref, z_ref, d_ref, s_ref, q_ref, cz_ref,
    pick, place, mask, fold, fold_t, group,
    gath, rows, mid, contrib, even, odd,
    p_send, p_recv, z_all, t_send, t_recv, dots_c, dots_p, out_nat,
    blk_sem, cam_sem, pre_sem, rhs_sem, inv_sem,
    ps_s, ps_r, z_s, z_r, t_s, t_r, dc_s, dc_r, dp_s, dp_r, so_s, so_r, re_s, re_r,
):
    me_c = lax.axis_index("cam")
    me_p = lax.axis_index("pts")
    tiles = blk.shape[0]
    pairs = tiles // 2
    slots = 4 * tiles
    per_half = pairs // HALVES
    per_chunk = tiles // CHUNKS
    blocks = place.shape[0]
    own = rhs_nat.shape[1]
    lanes_here = pl.ds(pl.multiple_of(me_p * own, own), own)

    pre_copy = pltpu.make_async_copy(pre_hbm.at[:, :, lanes_here], pre_nat, pre_sem)
    cam_copy = pltpu.make_async_copy(cam_hbm.at[:, :, lanes_here], cam_nat, cam_sem)
    rhs_copy = pltpu.make_async_copy(rhs_hbm.at[:, lanes_here], rhs_nat, rhs_sem)
    inv_copy = pltpu.make_async_copy(inv_hbm, inv_nat, inv_sem)

    def blk_copy(c):
        part = pl.ds(c * per_chunk, per_chunk)
        return pltpu.make_async_copy(blk_hbm.at[part], blk.at[part], blk_sem.at[c])

    rhs_copy.start()
    pre_copy.start()

    def start_chunk(c, carry):
        blk_copy(c).start()
        return carry

    lax.fori_loop(0, CHUNKS, start_chunk, 0)
    inv_copy.start()
    cam_copy.start()

    barrier = pltpu.get_barrier_semaphore()

    def cam_peer(k):
        return lax.rem(me_c + k, n_cam)

    def pts_peer(k):
        return lax.rem(me_p + k, n_pts)

    def greet_cam(k, carry):
        pl.semaphore_signal(barrier, inc=1, device_id=(cam_peer(k), me_p), device_id_type=MESH)
        return carry

    def greet_pts(k, carry):
        pl.semaphore_signal(barrier, inc=1, device_id=(me_c, pts_peer(k)), device_id_type=MESH)
        return carry

    lax.fori_loop(1, n_cam, greet_cam, 0)
    lax.fori_loop(1, n_pts, greet_pts, 0)

    def cam_copy_to(peer, slot, src, dst, ssem, rsem):
        return pltpu.make_async_remote_copy(
            src_ref=src(peer), dst_ref=dst(slot), send_sem=ssem.at[peer],
            recv_sem=rsem.at[slot], device_id=(peer, me_p), device_id_type=MESH,
        )

    def pts_copy_to(peer, slot, src, dst, ssem, rsem):
        return pltpu.make_async_remote_copy(
            src_ref=src(peer), dst_ref=dst(slot), send_sem=ssem.at[peer],
            recv_sem=rsem.at[slot], device_id=(me_c, peer), device_id_type=MESH,
        )

    def start_cam(*args):
        def body(k, carry):
            cam_copy_to(cam_peer(k), me_c, *args).start()
            return carry

        lax.fori_loop(1, n_cam, body, 0)

    def wait_cam(*args):
        def body(k, carry):
            copy = cam_copy_to(cam_peer(k), cam_peer(k), *args)
            copy.wait_recv()
            copy.wait_send()
            return carry

        lax.fori_loop(1, n_cam, body, 0)

    def start_pts(*args):
        def body(k, carry):
            pts_copy_to(pts_peer(k), me_p, *args).start()
            return carry

        lax.fori_loop(1, n_pts, body, 0)

    def wait_pts(*args):
        def body(k, carry):
            copy = pts_copy_to(pts_peer(k), pts_peer(k), *args)
            copy.wait_recv()
            copy.wait_send()
            return carry

        lax.fori_loop(1, n_pts, body, 0)

    def part(j):
        return slice(8 * j, 8 * j + 8)

    def to_dense(src, dst):
        for b in range(8):
            dst[pl.ds(b, 9, stride=8), :] = src[:, 128 * b : 128 * b + 128]

    def to_dense_blocks(src, dst):
        def body(i, carry):
            for b in range(8):
                dst[i, pl.ds(b, 9, stride=8), :] = src[i, :, 128 * b : 128 * b + 128]
            return carry

        lax.fori_loop(0, 9, body, 0)

    def apply_block(mat, vec):
        out = []
        for i in range(9):
            total = mat[i, part(0), :] * vec[0]
            for j in range(1, 9):
                total = total + mat[i, part(j), :] * vec[j]
            out.append(total)
        return out

    def precondition(r):
        z = apply_block(pre_d, r)
        gamma = r[0] * z[0]
        for j in range(1, 9):
            gamma = gamma + r[j] * z[j]
        for j in range(9):
            z_ref[part(j), :] = z[j]
            z_all[me_p, :, 128 * j : 128 * j + 128] = z[j].astype(BF16)
        return gamma

    z_args = (lambda peer: z_all.at[me_p], lambda slot: z_all.at[slot], z_s, z_r)

    rhs_copy.wait()
    to_dense(rhs_nat, r_ref)
    pre_copy.wait()
    to_dense_blocks(pre_nat, pre_d)
    gamma = precondition([r_ref[part(j), :] for j in range(9)])
    pl.semaphore_wait(barrier, n_cam + n_pts - 2)
    start_pts(*z_args)

    index = idx_ref[...]
    used = iota((tiles, 4), 1) < count_ref[...]
    spread = one_hot(iota((slots, tiles), 0) // 4 == iota((slots, tiles), 1))
    here = iota((slots, 4), 1) == lax.rem(iota((slots, 4), 0), 4)

    def column(value):
        wide = jnp.dot(spread, value.astype(F32).astype(BF16), preferred_element_type=F32)
        return jnp.sum(jnp.where(here, wide, 0.0), axis=1, keepdims=True)

    chosen = jnp.where(
        iota((slots, blocks), 1).astype(F32) == column(jnp.where(used, index // 8, -1)), 1.0, 0.0
    )
    pick[...] = chosen.astype(BF16)
    place[...] = jnp.transpose(chosen).astype(BF16)
    mask[...] = jnp.where(
        (iota((slots, 128), 1) // 16).astype(F32) == column(lax.rem(index, 8)), 1.0, 0.0
    )
    at = iota((9 * 128, 144), 0)
    fold[...] = one_hot(iota((9 * 128, 144), 1) == (at // 128) * 16 + lax.rem(at, 16))
    at = iota((144, 9 * 128), 1)
    fold_t[...] = one_hot(iota((144, 9 * 128), 0) == (at // 128) * 16 + lax.rem(at, 16))
    row = iota((2 * per_half, 8 * per_half), 0)
    col = iota((2 * per_half, 8 * per_half), 1)
    group[...] = one_hot(
        (col // 8 == lax.rem(row, per_half)) & (lax.rem(col, 8) // 4 == row // per_half)
    )
    inv_copy.wait()

    def inv_dense(b, carry):
        for i in range(3):
            inv_d[i, pl.ds(b, 3, stride=pairs), :] = inv_nat[
                i, :, pl.ds(pl.multiple_of(b * 128, 128), 128)
            ]
        return carry

    lax.fori_loop(0, pairs, inv_dense, 0, unroll=4)
    cam_copy.wait()
    to_dense_blocks(cam_nat, cam_d)

    row8 = iota((8, 768), 0)
    diag = iota((8, 768), 1) // 192 == lax.rem(row8, 4)
    upper = row8 < 4
    first_tile = lax.rem(iota((per_half, 384), 1), 128) < 64
    order = (0, 2, 1)

    gamma_old = None
    alpha_old = None
    for it in range(ITERS):
        last = it + 1 == ITERS
        parity = it % 2
        wait_pts(*z_args)
        for j in range(9):
            wide = z_all[:, :, 128 * j : 128 * j + 128].astype(F32).reshape(blocks, 128)
            picked = jnp.dot(pick[...], wide.astype(BF16), preferred_element_type=F32)
            gath[:, 128 * j : 128 * j + 128] = (picked * mask[...]).astype(BF16)
        rows[...] = jnp.dot(gath[...], fold[...], preferred_element_type=F32)

        def forward(j, h):
            left = rows[pl.ds(pl.multiple_of(8 * j, 8), 8), :].astype(BF16)
            one = jnp.dot(left, blk[2 * j], preferred_element_type=F32)
            two = jnp.dot(left, blk[2 * j + 1], preferred_element_type=F32)
            both = jnp.where(diag, jnp.where(upper, one, two), 0.0)
            mid[pl.ds(pl.multiple_of(8 * (j - h * per_half), 8), 8), :] = (
                both[:, :384] + both[:, 384:]
            )

        def p_args(h):
            return (
                lambda peer: p_send.at[h],
                lambda slot: p_recv.at[parity, h, slot],
                ps_s.at[h],
                ps_r.at[parity, h],
            )

        for h in range(HALVES):
            if it == 0:

                def forward_chunk(c, carry):
                    blk_copy(c).wait()
                    for k in range(per_chunk // 2):
                        forward(c * (per_chunk // 2) + k, h)
                    return carry

                some = CHUNKS // HALVES
                lax.fori_loop(h * some, (h + 1) * some, forward_chunk, 0)
            else:

                def forward_four(c, carry):
                    for k in range(4):
                        forward(4 * c + k, h)
                    return carry

                some = per_half // 4
                lax.fori_loop(h * some, (h + 1) * some, forward_four, 0)
            full = mid[...]
            high = full.astype(BF16)
            low = (full - high.astype(F32)).astype(BF16)
            summed = jnp.dot(group[...], high, preferred_element_type=F32) + jnp.dot(
                group[...], low, preferred_element_type=F32
            )
            summed = summed + pltpu.roll(summed, 192, 1)
            p_send[h] = jnp.where(
                first_tile, summed[:per_half], pltpu.roll(summed[per_half:], 64, 1)
            ).astype(BF16)
            start_cam(*p_args(h))

        z = [z_ref[part(j), :] for j in range(9)]
        cz = apply_block(cam_d, z)
        curve = z[0] * cz[0]
        for j in range(1, 9):
            curve = curve + z[j] * cz[j]
        for j in range(9):
            cz_ref[part(j), :] = cz[j]
        dots_c[parity, me_c, 0:1, :] = jnp.sum(gamma, axis=0, keepdims=True)
        dots_c[parity, me_c, 1:2, :] = jnp.sum(curve, axis=0, keepdims=True)
        dc_args = (
            lambda peer: dots_c.at[parity, me_c],
            lambda slot: dots_c.at[parity, slot],
            dc_s,
            dc_r.at[parity],
        )
        start_cam(*dc_args)

        def backward(j):
            both = jnp.where(
                upper[:, :384],
                jnp.broadcast_to(even[pl.ds(j, 1), :], (8, 384)),
                jnp.broadcast_to(odd[pl.ds(j, 1), :], (8, 384)),
            )
            left = jnp.where(diag, jnp.concatenate([both, both], axis=1), 0.0).astype(BF16)
            contract = (((1,), (1,)), ((), ()))
            one = lax.dot_general(left, blk[2 * j], contract, preferred_element_type=F32)
            two = lax.dot_general(left, blk[2 * j + 1], contract, preferred_element_type=F32)
            contrib[pl.ds(pl.multiple_of(8 * j, 8), 8), :] = jnp.where(upper[:, :144], one, two)

        energy = jnp.zeros((per_half, 128), F32)
        for h in range(HALVES):
            wait_cam(*p_args(h))
            total = p_send[h].astype(F32)
            for k in range(1, n_cam):
                total = total + p_recv[parity, h, cam_peer(k)].astype(F32)
            sums = [None] * 3
            for place_i, i in enumerate(order):
                sums[i] = total[:, 128 * place_i : 128 * place_i + 128]
            here_h = slice(h * per_half, (h + 1) * per_half)
            answers = []
            for i in order:
                answer = jnp.zeros((per_half, 128), F32)
                for j in range(3):
                    at_j = slice(j * pairs + h * per_half, j * pairs + (h + 1) * per_half)
                    answer = answer + inv_d[i, at_j, :] * sums[j]
                answer = answer.astype(BF16).astype(F32)
                energy = energy + answer * sums[i]
                answers.append(answer)
            answer = jnp.concatenate(answers, axis=1)
            a = jnp.where(first_tile, answer, 0.0)
            even[here_h, :] = a + pltpu.roll(a, 192, 1)
            a = pltpu.roll(jnp.where(first_tile, 0.0, answer), 320, 1)
            odd[here_h, :] = a + pltpu.roll(a, 192, 1)
            if h + 1 == HALVES:
                wait_cam(*dc_args)
                total = dots_c[parity, 0]
                for k in range(1, n_cam):
                    total = total + dots_c[parity, k]
                dots_p[me_p, 0:2, :] = total[0:2]
                dots_p[me_p, 2:3, :] = jnp.sum(energy, axis=0, keepdims=True)
                dp_args = (
                    lambda peer: dots_p.at[me_p],
                    lambda slot: dots_p.at[slot],
                    dp_s,
                    dp_r,
                )
                start_pts(*dp_args)

            def backward_four(c, carry):
                for k in range(4):
                    backward(4 * c + k)
                return carry

            some = per_half // 4
            lax.fori_loop(h * some, (h + 1) * some, backward_four, 0)

        contrib_half = contrib[...].astype(BF16)
        for j in range(9):
            lanes = slice(j * 128, (j + 1) * 128)
            wide = jnp.dot(contrib_half, fold_t[:, lanes], preferred_element_type=F32)
            wide = (wide * mask[...]).astype(BF16)
            put = jnp.dot(place[...], wide, preferred_element_type=F32)
            for o in range(n_pts):
                t_send[o, :, lanes] = put[o * 8 : (o + 1) * 8, :].astype(BF16)
        t_args = (lambda peer: t_send.at[peer], lambda slot: t_recv.at[slot], t_s, t_r)
        start_pts(*t_args)

        wait_pts(*dp_args)
        total = dots_p[0, 0:3]
        for k in range(1, n_pts):
            total = total + dots_p[k, 0:3]
        total = jnp.sum(total, axis=1, keepdims=True)
        gamma_now = total[0:1]
        curve_now = total[1:2] - total[2:3]
        if it == 0:
            alpha = gamma_now / curve_now
        else:
            beta = gamma_now / gamma_old
            alpha = gamma_now / (curve_now - beta * gamma_now / alpha_old)
            beta_all = jnp.broadcast_to(beta, (8, 128))
        gamma_old, alpha_old = gamma_now, alpha
        alpha_all = jnp.broadcast_to(alpha, (8, 128))
        for j in range(9):
            if it == 0:
                d = z[j]
                s = alpha_all * d
                q = cz[j]
            else:
                d = z_ref[part(j), :] + beta_all * d_ref[part(j), :]
                s = s_ref[part(j), :] + alpha_all * d
                q = cz_ref[part(j), :] + beta_all * q_ref[part(j), :]
            d_ref[part(j), :] = d
            s_ref[part(j), :] = s
            q_ref[part(j), :] = q

        def to_native(src, which, out):
            for b in range(8):
                out_nat[which, :, 128 * b : 128 * b + 128] = src[pl.ds(b, 9, stride=8), :]
            out[:, lanes_here] = out_nat[which]

        def out_args(which, out, ssem, rsem):
            return (
                lambda peer: out_nat.at[which],
                lambda slot: out.at[:, pl.ds(pl.multiple_of(slot * own, own), own)],
                ssem,
                rsem,
            )

        if last:
            to_native(s_ref, 0, sol_out)
            start_pts(*out_args(0, sol_out, so_s, so_r))

        wait_pts(*t_args)
        r = []
        for j in range(9):
            lanes = slice(j * 128, (j + 1) * 128)
            total = t_send[me_p, :, lanes].astype(F32)
            for k in range(1, n_pts):
                total = total + t_recv[pts_peer(k), :, lanes].astype(F32)
            q = q_ref[part(j), :] - total
            q_ref[part(j), :] = q
            value = r_ref[part(j), :] - alpha_all * q
            r_ref[part(j), :] = value
            r.append(value)
        if not last:
            gamma = precondition(r)
            start_pts(*z_args)
        else:
            to_native(r_ref, 1, res_out)
            start_pts(*out_args(1, res_out, re_s, re_r))
            wait_pts(*out_args(0, sol_out, so_s, so_r))
            wait_pts(*out_args(1, res_out, re_s, re_r))


def per_device(n_cam, n_pts, rhs, cam_block, coupling, point_inverse, precond, tile_index, tile_count):
    tiles, slots = tile_index.shape
    cams = rhs.shape[1]
    blocks = cams // 128
    here = cams // n_pts
    pairs = tiles * slots
    half = tiles // 2 // HALVES
    vec = pltpu.VMEM((72, 128), F32)
    whole = pl.BlockSpec(memory_space=pltpu.VMEM)
    hbm = pl.BlockSpec(memory_space=pl.ANY)
    dma = pltpu.SemaphoreType.DMA
    slab = pltpu.VMEM((n_pts, 8, 9 * 128), BF16)
    return pl.pallas_call(
        functools.partial(kernel, n_cam, n_pts),
        out_shape=(jax.ShapeDtypeStruct(rhs.shape, F32), jax.ShapeDtypeStruct(rhs.shape, F32)),
        in_specs=[whole, whole, hbm, hbm, hbm, hbm, hbm],
        out_specs=(whole, whole),
        scratch_shapes=[
            pltpu.VMEM(coupling.shape, BF16),
            pltpu.VMEM((9, 9, here), F32),
            pltpu.VMEM((9, 9, here), F32),
            pltpu.VMEM((9, here), F32),
            pltpu.VMEM(point_inverse.shape, F32),
            pltpu.VMEM((9, 72, 128), F32),
            pltpu.VMEM((9, 72, 128), F32),
            pltpu.VMEM((3, 3 * tiles // 2, 128), F32),
            vec, vec, vec, vec, vec, vec,
            pltpu.VMEM((pairs, blocks), BF16),
            pltpu.VMEM((blocks, pairs), BF16),
            pltpu.VMEM((pairs, 128), F32),
            pltpu.VMEM((9 * 128, 144), BF16),
            pltpu.VMEM((144, 9 * 128), BF16),
            pltpu.VMEM((2 * half, 8 * half), BF16),
            pltpu.VMEM((pairs, 9 * 128), BF16),
            pltpu.VMEM((pairs, 144), F32),
            pltpu.VMEM((8 * half, 384), F32),
            pltpu.VMEM((pairs, 144), F32),
            pltpu.VMEM((tiles // 2, 384), F32),
            pltpu.VMEM((tiles // 2, 384), F32),
            pltpu.VMEM((HALVES, half, 384), BF16),
            pltpu.VMEM((2, HALVES, n_cam, half, 384), BF16),
            slab, slab, slab,
            pltpu.VMEM((2, n_cam, 2, 128), F32),
            pltpu.VMEM((n_pts, 4, 128), F32),
            pltpu.VMEM((2, 9, here), F32),
            dma((CHUNKS,)), dma, dma, dma, dma,
            dma((HALVES, n_cam)), dma((2, HALVES, n_cam)),
            dma((n_pts,)), dma((n_pts,)),
            dma((n_pts,)), dma((n_pts,)),
            dma((n_cam,)), dma((2, n_cam)),
            dma((n_pts,)), dma((n_pts,)),
            dma((n_pts,)), dma((n_pts,)),
            dma((n_pts,)), dma((n_pts,)),
        ],
        compiler_params=pltpu.CompilerParams(
            collective_id=0, has_side_effects=True, vmem_limit_bytes=48 * 2**20
        ),
    )(tile_index, tile_count, rhs, point_inverse, cam_block, precond, coupling)


def solution(mesh):
    in_specs = (
        P(None, "cam"),
        P(None, None, "cam"),
        P("pts", None, "cam"),
        P(None, None, "pts"),
        P(None, None, "cam"),
        P("pts", "cam"),
        P("pts", "cam"),
    )
    out_specs = (P(None, "cam"), P(None, "cam"))
    body = functools.partial(per_device, mesh.shape["cam"], mesh.shape["pts"])
    return jax.shard_map(body, mesh=mesh, in_specs=in_specs, out_specs=out_specs, check_vma=False)
```

```python
import functools

import jax
import jax.numpy as jnp
from jax import lax
from jax.experimental import pallas as pl
from jax.experimental.pallas import tpu as pltpu
from jax.sharding import PartitionSpec as P

ITERS = 3
F32 = jnp.float32
BF16 = jnp.bfloat16
CHUNKS = 16
HALVES = 2
UNROLL = 8
GROUPS = 3
MESH = pl.DeviceIdType.MESH


def iota(shape, axis):
    return lax.broadcasted_iota(jnp.int32, shape, axis)


def one_hot(where):
    return jnp.where(where, 1.0, 0.0).astype(BF16)


def kernel(
    n_cam, n_pts,
    idx_ref, count_ref, rhs_hbm, inv_hbm, cam_hbm, pre_hbm, blk_hbm,
    sol_out, res_out,
    blk, cam_nat, pre_nat, rhs_nat, inv_nat, cam_d, pre_d, inv_d,
    z_first, r_ref, z_ref, d_ref, s_ref, q_ref, cz_ref,
    pick, place, mask, fold, fold_t, group,
    gath, rows, mid, contrib, even, odd,
    p_send, p_recv, z_all, t_send, t_recv, w_all, dots_c, dots_p,
    blk_sem, cam_sem, pre_sem, rhs_sem, inv_sem,
    ps_s, ps_r, z_sem, t_s, t_r, w_s, w_r, dc_s, dc_r, dp_s, dp_r, out_sem,
):
    me_c = lax.axis_index("cam")
    me_p = lax.axis_index("pts")
    tiles = blk.shape[0]
    pairs = tiles // 2
    slots = 4 * tiles
    per_half = pairs // HALVES
    per_chunk = tiles // CHUNKS
    blocks = place.shape[0]
    core = lax.rem(me_p, 2)
    me_z = me_p // 2
    n_z = n_pts // 2
    mine = blocks // 2
    first_block = core * mine
    lanes_here = pl.ds(pl.multiple_of(first_block * 128, mine * 128), mine * 128)

    pre_copy = pltpu.make_async_copy(pre_hbm, pre_nat, pre_sem)
    cam_copy = pltpu.make_async_copy(cam_hbm.at[:, :, lanes_here], cam_nat, cam_sem)
    rhs_copy = pltpu.make_async_copy(rhs_hbm, rhs_nat, rhs_sem)
    inv_copy = pltpu.make_async_copy(inv_hbm, inv_nat, inv_sem)

    def blk_copy(c):
        part = pl.ds(c * per_chunk, per_chunk)
        return pltpu.make_async_copy(blk_hbm.at[part], blk.at[part], blk_sem.at[c])

    rhs_copy.start()
    pre_copy.start()

    def start_chunk(c, carry):
        blk_copy(c).start()
        return carry

    lax.fori_loop(0, CHUNKS, start_chunk, 0)
    inv_copy.start()
    cam_copy.start()

    barrier = pltpu.get_barrier_semaphore()

    def cam_peer(k):
        return lax.rem(me_c + k, n_cam)

    def pts_peer(k):
        return lax.rem(me_p + k, n_pts)

    def greet_cam(k, carry):
        pl.semaphore_signal(barrier, inc=1, device_id=(cam_peer(k), me_p), device_id_type=MESH)
        return carry

    def greet_pts(k, carry):
        pl.semaphore_signal(barrier, inc=1, device_id=(me_c, pts_peer(k)), device_id_type=MESH)
        return carry

    lax.fori_loop(1, n_cam, greet_cam, 0)
    lax.fori_loop(1, n_pts, greet_pts, 0)

    def cam_copy_to(peer, slot, src, dst, ssem, rsem):
        return pltpu.make_async_remote_copy(
            src_ref=src(peer), dst_ref=dst(slot), send_sem=ssem.at[peer],
            recv_sem=rsem.at[slot], device_id=(peer, me_p), device_id_type=MESH,
        )

    def pts_copy_to(peer, slot, src, dst, ssem, rsem):
        return pltpu.make_async_remote_copy(
            src_ref=src(peer), dst_ref=dst(slot), send_sem=ssem.at[peer],
            recv_sem=rsem.at[slot], device_id=(me_c, peer), device_id_type=MESH,
        )

    def start_cam(*args):
        def body(k, carry):
            cam_copy_to(cam_peer(k), me_c, *args).start()
            return carry

        lax.fori_loop(1, n_cam, body, 0)

    def wait_cam(*args):
        def body(k, carry):
            copy = cam_copy_to(cam_peer(k), cam_peer(k), *args)
            copy.wait_recv()
            copy.wait_send()
            return carry

        lax.fori_loop(1, n_cam, body, 0)

    def start_pts(*args):
        def body(k, carry):
            pts_copy_to(pts_peer(k), me_p, *args).start()
            return carry

        lax.fori_loop(1, n_pts, body, 0)

    def wait_pts(*args):
        def body(k, carry):
            copy = pts_copy_to(pts_peer(k), pts_peer(k), *args)
            copy.wait_recv()
            copy.wait_send()
            return carry

        lax.fori_loop(1, n_pts, body, 0)

    def swap(src, dst, ssem, rsem):
        return pltpu.make_async_remote_copy(
            src_ref=src, dst_ref=dst, send_sem=ssem, recv_sem=rsem,
            device_id=(me_c, me_z * 2 + 1 - core), device_id_type=MESH,
        )

    def z_peer(k):
        return lax.rem(me_z + k, n_z)

    def along_z(k, slot, src, dst, ssem, rsem):
        return pltpu.make_async_remote_copy(
            src_ref=src, dst_ref=dst(slot), send_sem=ssem.at[k], recv_sem=rsem.at[slot],
            device_id=(me_c, z_peer(k) * 2 + core), device_id_type=MESH,
        )

    def at_rows(j, step):
        return pl.ds(pl.multiple_of(j * mine + step * 8, 8), 8)

    def to_dense_blocks(src, start, dst):
        def body(b, carry):
            lanes = pl.ds(pl.multiple_of((start + b) * 128, 128), 128)
            for i in range(9):
                dst[i, pl.ds(b, 9, stride=mine), :] = src[i, :, lanes]
            return carry

        lax.fori_loop(0, mine, body, 0)

    def apply_row(mat, vec, i, step):
        total = mat[i, at_rows(0, step), :] * vec[0]
        for j in range(1, 9):
            total = total + mat[i, at_rows(j, step), :] * vec[j]
        return total

    z_swap = swap(z_all.at[core], z_all.at[core], z_sem.at[0], z_sem.at[1])

    index = idx_ref[...]
    used = iota((4, tiles), 0) < count_ref[...]
    spread = one_hot(iota((slots, tiles), 0) // 4 == iota((slots, tiles), 1))
    here = iota((slots, 4), 1) == lax.rem(iota((slots, 4), 0), 4)

    def column(value):
        wide = lax.dot_general(
            spread, value.astype(F32).astype(BF16), (((1,), (1,)), ((), ())),
            preferred_element_type=F32,
        )
        return jnp.sum(jnp.where(here, wide, 0.0), axis=1, keepdims=True)

    chosen = jnp.where(
        iota((slots, blocks), 1).astype(F32) == column(jnp.where(used, index // 8, -1)), 1.0, 0.0
    )
    pick[...] = chosen.astype(BF16)
    place[...] = jnp.transpose(chosen).astype(BF16)
    mask[...] = jnp.where(
        (iota((slots, 128), 1) // 16).astype(F32) == column(lax.rem(index, 8)), 1.0, 0.0
    )
    at = iota((9 * 128, 144), 0)
    fold[...] = one_hot(iota((9 * 128, 144), 1) == (at // 128) * 16 + lax.rem(at, 16))
    at = iota((144, 9 * 128), 1)
    fold_t[...] = one_hot(iota((144, 9 * 128), 0) == (at // 128) * 16 + lax.rem(at, 16))
    row = iota((2 * per_half, 8 * per_half), 0)
    col = iota((2 * per_half, 8 * per_half), 1)
    group[...] = one_hot(
        (col // 8 == lax.rem(row, per_half)) & (lax.rem(col, 8) // 4 == row // per_half)
    )

    rhs_copy.wait()
    pre_copy.wait()

    def first(b, carry):
        lanes = pl.ds(pl.multiple_of(b * 128, 128), 128)
        total = pre_nat[0, :, lanes] * rhs_nat[pl.ds(0, 1), lanes]
        for j in range(1, 9):
            total = total + pre_nat[j, :, lanes] * rhs_nat[pl.ds(j, 1), lanes]
        z_first[pl.ds(b, 9, stride=blocks), :] = total
        return carry

    lax.fori_loop(0, blocks, first, 0, unroll=2)
    for j in range(9):
        for o in range(2):
            at = j * blocks + o * mine
            z_all[o, :, 128 * j : 128 * j + 128] = z_first[at : at + mine, :].astype(BF16)

    row8 = iota((8, 768), 0)
    diag = iota((8, 768), 1) // 192 == lax.rem(row8, 4)
    upper = row8 < 4
    first_tile = lax.rem(iota((per_half, 384), 1), 128) < 64
    order = (0, 2, 1)

    gamma_old = None
    alpha_old = None
    for it in range(ITERS):
        last = it + 1 == ITERS
        parity = it % 2
        if it > 0:
            z_swap.wait()
        for j in range(9):
            wide = z_all[:, :, 128 * j : 128 * j + 128].astype(F32).reshape(blocks, 128)
            picked = jnp.dot(pick[...], wide.astype(BF16), preferred_element_type=F32)
            gath[:, 128 * j : 128 * j + 128] = (picked * mask[...]).astype(BF16)
        rows[...] = jnp.dot(gath[...], fold[...], preferred_element_type=F32)

        def forward(j, h):
            left = rows[pl.ds(pl.multiple_of(8 * j, 8), 8), :].astype(BF16)
            one = jnp.dot(left, blk[2 * j], preferred_element_type=F32)
            two = jnp.dot(left, blk[2 * j + 1], preferred_element_type=F32)
            both = jnp.where(diag, jnp.where(upper, one, two), 0.0)
            mid[pl.ds(pl.multiple_of(8 * (j - h * per_half), 8), 8), :] = (
                both[:, :384] + both[:, 384:]
            )

        def p_args(h):
            return (
                lambda peer: p_send.at[h],
                lambda slot: p_recv.at[parity, h, slot],
                ps_s.at[h],
                ps_r.at[parity, h],
            )

        for h in range(HALVES):
            if it == 0:

                def forward_chunk(c, carry):
                    blk_copy(c).wait()
                    for k in range(per_chunk // 2):
                        forward(c * (per_chunk // 2) + k, h)
                    return carry

                some = CHUNKS // HALVES
                lax.fori_loop(h * some, (h + 1) * some, forward_chunk, 0)
            else:

                def forward_some(c, carry):
                    for k in range(UNROLL):
                        forward(UNROLL * c + k, h)
                    return carry

                some = per_half // UNROLL
                lax.fori_loop(h * some, (h + 1) * some, forward_some, 0)
            full = mid[...]
            high = full.astype(BF16)
            low = (full - high.astype(F32)).astype(BF16)
            summed = jnp.dot(group[...], high, preferred_element_type=F32) + jnp.dot(
                group[...], low, preferred_element_type=F32
            )
            summed = summed + pltpu.roll(summed, 192, 1)
            p_send[h] = jnp.where(
                first_tile, summed[:per_half], pltpu.roll(summed[per_half:], 64, 1)
            ).astype(BF16)
            if it == 0 and h == 0:
                pl.semaphore_wait(barrier, n_cam + n_pts - 2)
            start_cam(*p_args(h))

        if it == 0:

            def inv_dense(b, carry):
                for i in range(3):
                    inv_d[i, pl.ds(b, 3, stride=pairs), :] = inv_nat[
                        i, :, pl.ds(pl.multiple_of(b * 128, 128), 128)
                    ]
                return carry

            inv_copy.wait()
            lax.fori_loop(0, pairs, inv_dense, 0, unroll=4)
            for j in range(9):
                rows_j = pl.ds(pl.multiple_of(j * blocks + first_block, 8), mine)
                z_ref[j * mine : (j + 1) * mine, :] = z_first[rows_j, :]

            def rhs_dense(b, carry):
                lanes = pl.ds(pl.multiple_of((first_block + b) * 128, 128), 128)
                r_ref[pl.ds(b, 9, stride=mine), :] = rhs_nat[:, lanes]
                return carry

            lax.fori_loop(0, mine, rhs_dense, 0, unroll=4)
            cam_copy.wait()
            to_dense_blocks(cam_nat, 0, cam_d)

        def shares(step, carry):
            gamma, curve = carry
            z = [z_ref[at_rows(j, step), :] for j in range(9)]
            for i in range(9):
                cz = apply_row(cam_d, z, i, step)
                cz_ref[at_rows(i, step), :] = cz
                curve = curve + z[i] * cz
                gamma = gamma + z[i] * r_ref[at_rows(i, step), :]
            return gamma, curve

        zero = jnp.zeros((8, 128), F32)
        gamma, curve = lax.fori_loop(0, mine // 8, shares, (zero, zero))
        dots_c[parity, me_c, 0:1, :] = jnp.sum(gamma, axis=0, keepdims=True)
        dots_c[parity, me_c, 1:2, :] = jnp.sum(curve, axis=0, keepdims=True)
        dc_args = (
            lambda peer: dots_c.at[parity, me_c],
            lambda slot: dots_c.at[parity, slot],
            dc_s,
            dc_r.at[parity],
        )
        start_cam(*dc_args)

        def backward(j):
            both = jnp.where(
                upper[:, :384],
                jnp.broadcast_to(even[pl.ds(j, 1), :], (8, 384)),
                jnp.broadcast_to(odd[pl.ds(j, 1), :], (8, 384)),
            )
            left = jnp.where(diag, jnp.concatenate([both, both], axis=1), 0.0).astype(BF16)
            contract = (((1,), (1,)), ((), ()))
            one = lax.dot_general(left, blk[2 * j], contract, preferred_element_type=F32)
            two = lax.dot_general(left, blk[2 * j + 1], contract, preferred_element_type=F32)
            contrib[pl.ds(pl.multiple_of(8 * j, 8), 8), :] = jnp.where(upper[:, :144], one, two)

        energy = jnp.zeros((per_half, 128), F32)
        for h in range(HALVES):
            wait_cam(*p_args(h))
            total = p_send[h].astype(F32)
            for k in range(1, n_cam):
                total = total + p_recv[parity, h, cam_peer(k)].astype(F32)
            sums = [None] * 3
            for place_i, i in enumerate(order):
                sums[i] = total[:, 128 * place_i : 128 * place_i + 128]
            here_h = slice(h * per_half, (h + 1) * per_half)
            answers = []
            for i in order:
                answer = jnp.zeros((per_half, 128), F32)
                for j in range(3):
                    at_j = slice(j * pairs + h * per_half, j * pairs + (h + 1) * per_half)
                    answer = answer + inv_d[i, at_j, :] * sums[j]
                answer = answer.astype(BF16).astype(F32)
                energy = energy + answer * sums[i]
                answers.append(answer)
            answer = jnp.concatenate(answers, axis=1)
            a = jnp.where(first_tile, answer, 0.0)
            even[here_h, :] = a + pltpu.roll(a, 192, 1)
            a = pltpu.roll(jnp.where(first_tile, 0.0, answer), 320, 1)
            odd[here_h, :] = a + pltpu.roll(a, 192, 1)
            if h + 1 == HALVES:
                wait_cam(*dc_args)
                total = dots_c[parity, 0]
                for k in range(1, n_cam):
                    total = total + dots_c[parity, k]
                dots_p[parity, me_p, 0:2, :] = total[0:2]
                dots_p[parity, me_p, 2:3, :] = jnp.sum(energy, axis=0, keepdims=True)
                dots_p[parity, me_p, 3:4, :] = jnp.sum(energy, axis=0, keepdims=True)
                dp_args = (
                    lambda peer: dots_p.at[parity, me_p],
                    lambda slot: dots_p.at[parity, slot],
                    dp_s,
                    dp_r.at[parity],
                )
                start_pts(*dp_args)

            def backward_some(c, carry):
                for k in range(UNROLL):
                    backward(UNROLL * c + k)
                return carry

            some = per_half // UNROLL
            lax.fori_loop(h * some, (h + 1) * some, backward_some, 0)

        contrib_half = contrib[...].astype(BF16)
        t_swaps = []
        for g in range(GROUPS):
            for jj in range(9 // GROUPS):
                j = g * (9 // GROUPS) + jj
                lanes = slice(j * 128, (j + 1) * 128)
                wide = jnp.dot(contrib_half, fold_t[:, lanes], preferred_element_type=F32)
                wide = (wide * mask[...]).astype(BF16)
                put = jnp.dot(place[...], wide, preferred_element_type=F32)
                for o in range(2):
                    t_send[g, o, :, jj * 128 : (jj + 1) * 128] = put[
                        o * mine : (o + 1) * mine, :
                    ].astype(BF16)
            t_swaps.append(swap(t_send.at[g, 1 - core], t_recv.at[g], t_s.at[g], t_r.at[g]))
            t_swaps[g].start()

        def w_args(g):
            return (
                w_all.at[parity, g, me_z],
                lambda slot: w_all.at[parity, g, slot],
                w_s.at[g],
                w_r.at[parity, g],
            )

        for g in range(GROUPS):
            t_swaps[g].wait()
            w_all[parity, g, me_z] = (
                t_send[g, core].astype(F32) + t_recv[g].astype(F32)
            ).astype(BF16)
            for k in range(1, n_z):
                along_z(k, me_z, *w_args(g)).start()
        if it == 0:
            to_dense_blocks(pre_nat, first_block, pre_d)

        wait_pts(*dp_args)
        total = dots_p[parity, 0]
        for k in range(1, n_pts):
            total = total + dots_p[parity, k]
        energy_now = jnp.sum(total[2:3], axis=1, keepdims=True)
        total = dots_p[parity, 0] + dots_p[parity, 1]
        total = jnp.sum(total, axis=1, keepdims=True)
        gamma_now = total[0:1]
        curve_now = total[1:2] - energy_now
        if it == 0:
            alpha = gamma_now / curve_now
        else:
            beta = gamma_now / gamma_old
            alpha = gamma_now / (curve_now - beta * gamma_now / alpha_old)
            beta_all = jnp.broadcast_to(beta, (8, 128))
        gamma_old, alpha_old = gamma_now, alpha
        alpha_all = jnp.broadcast_to(alpha, (8, 128))

        def early(step, carry):
            for j in range(9):
                at_j = at_rows(j, step)
                d = z_ref[at_j, :]
                q = cz_ref[at_j, :]
                if it > 0:
                    d = d + beta_all * d_ref[at_j, :]
                    q = q + beta_all * q_ref[at_j, :]
                s = alpha_all * d
                if it > 0:
                    s = s_ref[at_j, :] + s
                if not last:
                    d_ref[at_j, :] = d
                q_ref[at_j, :] = q
                s_ref[at_j, :] = s
            return carry

        lax.fori_loop(0, mine // 8, early, 0)

        def to_native(src, out):
            def body(b, carry):
                lanes = pl.ds(pl.multiple_of((first_block + b) * 128, 128), 128)
                out[:, lanes] = src[pl.ds(b, 9, stride=mine), :]
                return carry

            lax.fori_loop(0, mine, body, 0, unroll=4)

        def out_swap(which, out):
            half = out.at[:, lanes_here]
            return swap(half, half, out_sem.at[which, 0], out_sem.at[which, 1])

        if last:
            to_native(s_ref, sol_out)
            out_swap(0, sol_out).start()

        for g in range(GROUPS):
            for k in range(1, n_z):
                copy = along_z(k, z_peer(k), *w_args(g))
                copy.wait_recv()
                copy.wait_send()

        def late(step, carry):
            r = []
            for j in range(9):
                g, jj = j // (9 // GROUPS), j % (9 // GROUPS)
                here_j = pl.ds(pl.multiple_of(step * 16, 16), 16)
                term = w_all[parity, g, 0, here_j, jj * 128 : (jj + 1) * 128].astype(F32)
                for k in range(1, n_z):
                    term = term + w_all[
                        parity, g, k, here_j, jj * 128 : (jj + 1) * 128
                    ].astype(F32)
                rr = []
                for e in range(2):
                    at_e = at_rows(j, 2 * step + e)
                    q = q_ref[at_e, :] - term[8 * e : 8 * e + 8]
                    q_ref[at_e, :] = q
                    value = r_ref[at_e, :] - alpha_all * q
                    r_ref[at_e, :] = value
                    rr.append(value)
                r.append(rr)
            if not last:
                for i in range(9):
                    zz = []
                    for e in range(2):
                        z = apply_row(pre_d, [r[j][e] for j in range(9)], i, 2 * step + e)
                        z_ref[at_rows(i, 2 * step + e), :] = z
                        zz.append(z)
                    z_all[
                        core, pl.ds(pl.multiple_of(step * 16, 16), 16), 128 * i : 128 * i + 128
                    ] = jnp.concatenate(zz, axis=0).astype(BF16)
            return carry

        lax.fori_loop(0, mine // 16, late, 0)
        if not last:
            z_swap.start()
        else:
            to_native(r_ref, res_out)
            out_swap(1, res_out).start()
            out_swap(0, sol_out).wait()
            out_swap(1, res_out).wait()


def per_device(n_cam, n_pts, rhs, cam_block, coupling, point_inverse, precond, tile_index, tile_count):
    tiles, slots = tile_index.shape
    cams = rhs.shape[1]
    blocks = cams // 128
    mine = blocks // 2
    pairs = tiles * slots
    half = tiles // 2 // HALVES
    vec = pltpu.VMEM((9 * mine, 128), F32)
    whole = pl.BlockSpec(memory_space=pltpu.VMEM)
    hbm = pl.BlockSpec(memory_space=pltpu.HBM)
    dma = pltpu.SemaphoreType.DMA
    group = 9 // GROUPS * 128
    return pl.pallas_call(
        functools.partial(kernel, n_cam, n_pts),
        out_shape=(jax.ShapeDtypeStruct(rhs.shape, F32), jax.ShapeDtypeStruct(rhs.shape, F32)),
        in_specs=[whole, whole, hbm, hbm, hbm, hbm, hbm],
        out_specs=(whole, whole),
        scratch_shapes=[
            pltpu.VMEM(coupling.shape, BF16),
            pltpu.VMEM((9, 9, mine * 128), F32),
            pltpu.VMEM(precond.shape, F32),
            pltpu.VMEM(rhs.shape, F32),
            pltpu.VMEM(point_inverse.shape, F32),
            pltpu.VMEM((9, 9 * mine, 128), F32),
            pltpu.VMEM((9, 9 * mine, 128), F32),
            pltpu.VMEM((3, 3 * tiles // 2, 128), F32),
            pltpu.VMEM((9 * blocks, 128), F32),
            vec, vec, vec, vec, vec, vec,
            pltpu.VMEM((pairs, blocks), BF16),
            pltpu.VMEM((blocks, pairs), BF16),
            pltpu.VMEM((pairs, 128), F32),
            pltpu.VMEM((9 * 128, 144), BF16),
            pltpu.VMEM((144, 9 * 128), BF16),
            pltpu.VMEM((2 * half, 8 * half), BF16),
            pltpu.VMEM((pairs, 9 * 128), BF16),
            pltpu.VMEM((pairs, 144), F32),
            pltpu.VMEM((8 * half, 384), F32),
            pltpu.VMEM((pairs, 144), F32),
            pltpu.VMEM((tiles // 2, 384), F32),
            pltpu.VMEM((tiles // 2, 384), F32),
            pltpu.VMEM((HALVES, half, 384), BF16),
            pltpu.VMEM((2, HALVES, n_cam, half, 384), BF16),
            pltpu.VMEM((2, mine, 9 * 128), BF16),
            pltpu.VMEM((GROUPS, 2, mine, group), BF16),
            pltpu.VMEM((GROUPS, mine, group), BF16),
            pltpu.VMEM((2, GROUPS, n_pts // 2, mine, group), BF16),
            pltpu.VMEM((2, n_cam, 2, 128), F32),
            pltpu.VMEM((2, n_pts, 4, 128), F32),
            dma((CHUNKS,)), dma, dma, dma, dma,
            dma((HALVES, n_cam)), dma((2, HALVES, n_cam)),
            dma((2,)),
            dma((GROUPS,)), dma((GROUPS,)),
            dma((GROUPS, n_pts // 2)), dma((2, GROUPS, n_pts // 2)),
            dma((n_cam,)), dma((2, n_cam)),
            dma((n_pts,)), dma((2, n_pts)),
            dma((2, 2)),
        ],
        compiler_params=pltpu.CompilerParams(
            collective_id=0, has_side_effects=True, vmem_limit_bytes=56 * 2**20
        ),
    )(tile_index.T, tile_count.T, rhs, point_inverse, cam_block, precond, coupling)


def solution(mesh):
    in_specs = (
        P(None, "cam"),
        P(None, None, "cam"),
        P("pts", None, "cam"),
        P(None, None, "pts"),
        P(None, None, "cam"),
        P("pts", "cam"),
        P("pts", "cam"),
    )
    out_specs = (P(None, "cam"), P(None, "cam"))
    body = functools.partial(per_device, mesh.shape["cam"], mesh.shape["pts"])
    return jax.shard_map(body, mesh=mesh, in_specs=in_specs, out_specs=out_specs, check_vma=False)
```

```python
import functools

import jax
import jax.numpy as jnp
from jax import lax
from jax.experimental import pallas as pl
from jax.experimental.pallas import tpu as pltpu
from jax.sharding import PartitionSpec as P

ITERS = 3
F32 = jnp.float32
BF16 = jnp.bfloat16
CHUNKS = 16
PIECES = 4
UNROLL = 8
GROUPS = 3
MESH = pl.DeviceIdType.MESH


def iota(shape, axis):
    return lax.broadcasted_iota(jnp.int32, shape, axis)


def one_hot(where):
    return jnp.where(where, 1.0, 0.0).astype(BF16)


def kernel(
    n_cam, n_pts,
    idx_ref, count_ref, rhs_hbm, inv_hbm, cam_hbm, pre_hbm, blk_hbm,
    sol_out, res_out,
    blk, cam_nat, pre_nat, rhs_nat, inv_nat, cam_d, pre_d, inv_d,
    z_first, r_ref, z_ref, d_ref, s_ref, q_ref, cz_ref,
    pick, place, mask, fold, fold_t, group,
    gath, rows, mid, contrib, even, odd,
    p_recv, z_all, t_send, t_recv, w_all, dots_c, dots_p,
    blk_sem, cam_sem, pre_sem, rhs_sem, inv_sem,
    ps_s, ps_r, z_sem, t_s, t_r, w_s, w_r, dc_s, dc_r, dp_s, dp_r, out_sem,
):
    me_c = lax.axis_index("cam")
    me_p = lax.axis_index("pts")
    tiles = blk.shape[0]
    pairs = tiles // 2
    slots = 4 * tiles
    per_piece = pairs // PIECES
    per_chunk = tiles // CHUNKS
    blocks = place.shape[0]
    core = lax.rem(me_p, 2)
    me_z = me_p // 2
    n_z = n_pts // 2
    mine = blocks // 2
    first_block = core * mine
    lanes_here = pl.ds(pl.multiple_of(first_block * 128, mine * 128), mine * 128)

    pre_copy = pltpu.make_async_copy(pre_hbm, pre_nat, pre_sem)
    cam_copy = pltpu.make_async_copy(cam_hbm.at[:, :, lanes_here], cam_nat, cam_sem)
    rhs_copy = pltpu.make_async_copy(rhs_hbm, rhs_nat, rhs_sem)
    inv_copy = pltpu.make_async_copy(inv_hbm, inv_nat, inv_sem)

    def blk_copy(c):
        part = pl.ds(c * per_chunk, per_chunk)
        return pltpu.make_async_copy(blk_hbm.at[part], blk.at[part], blk_sem.at[c])

    rhs_copy.start()
    pre_copy.start()

    def start_chunk(c, carry):
        blk_copy(c).start()
        return carry

    lax.fori_loop(0, CHUNKS, start_chunk, 0)
    inv_copy.start()
    cam_copy.start()

    barrier = pltpu.get_barrier_semaphore()

    def cam_peer(k):
        return lax.rem(me_c + k, n_cam)

    def pts_peer(k):
        return lax.rem(me_p + k, n_pts)

    def greet_cam(k, carry):
        pl.semaphore_signal(barrier, inc=1, device_id=(cam_peer(k), me_p), device_id_type=MESH)
        return carry

    def greet_pts(k, carry):
        pl.semaphore_signal(barrier, inc=1, device_id=(me_c, pts_peer(k)), device_id_type=MESH)
        return carry

    lax.fori_loop(1, n_cam, greet_cam, 0)
    lax.fori_loop(1, n_pts, greet_pts, 0)

    def cam_copy_to(peer, slot, src, dst, ssem, rsem):
        return pltpu.make_async_remote_copy(
            src_ref=src(peer), dst_ref=dst(slot), send_sem=ssem.at[peer],
            recv_sem=rsem.at[slot], device_id=(peer, me_p), device_id_type=MESH,
        )

    def pts_copy_to(peer, slot, src, dst, ssem, rsem):
        return pltpu.make_async_remote_copy(
            src_ref=src(peer), dst_ref=dst(slot), send_sem=ssem.at[peer],
            recv_sem=rsem.at[slot], device_id=(me_c, peer), device_id_type=MESH,
        )

    def start_cam(*args):
        def body(k, carry):
            cam_copy_to(cam_peer(k), me_c, *args).start()
            return carry

        lax.fori_loop(1, n_cam, body, 0)

    def arrive_cam(*args):
        def body(k, carry):
            cam_copy_to(cam_peer(k), cam_peer(k), *args).wait_recv()
            return carry

        lax.fori_loop(1, n_cam, body, 0)

    def left_cam(*args):
        def body(k, carry):
            cam_copy_to(cam_peer(k), cam_peer(k), *args).wait_send()
            return carry

        lax.fori_loop(1, n_cam, body, 0)

    def start_pts(*args):
        def body(k, carry):
            pts_copy_to(pts_peer(k), me_p, *args).start()
            return carry

        lax.fori_loop(1, n_pts, body, 0)

    def wait_pts(*args):
        def body(k, carry):
            copy = pts_copy_to(pts_peer(k), pts_peer(k), *args)
            copy.wait_recv()
            copy.wait_send()
            return carry

        lax.fori_loop(1, n_pts, body, 0)

    def swap(src, dst, ssem, rsem):
        return pltpu.make_async_remote_copy(
            src_ref=src, dst_ref=dst, send_sem=ssem, recv_sem=rsem,
            device_id=(me_c, me_z * 2 + 1 - core), device_id_type=MESH,
        )

    def z_peer(k):
        return lax.rem(me_z + k, n_z)

    def along_z(k, slot, src, dst, ssem, rsem):
        return pltpu.make_async_remote_copy(
            src_ref=src, dst_ref=dst(slot), send_sem=ssem.at[k], recv_sem=rsem.at[slot],
            device_id=(me_c, z_peer(k) * 2 + core), device_id_type=MESH,
        )

    def at_rows(j, step):
        return pl.ds(pl.multiple_of(j * mine + step * 8, 8), 8)

    def to_dense_blocks(src, start, dst):
        def body(b, carry):
            lanes = pl.ds(pl.multiple_of((start + b) * 128, 128), 128)
            for i in range(9):
                dst[i, pl.ds(b, 9, stride=mine), :] = src[i, :, lanes]
            return carry

        lax.fori_loop(0, mine, body, 0)

    def apply_row(mat, vec, i, step):
        total = mat[i, at_rows(0, step), :] * vec[0]
        for j in range(1, 9):
            total = total + mat[i, at_rows(j, step), :] * vec[j]
        return total

    z_swap = swap(z_all.at[core], z_all.at[core], z_sem.at[0], z_sem.at[1])

    index = idx_ref[...]
    used = iota((4, tiles), 0) < count_ref[...]
    spread = one_hot(iota((slots, tiles), 0) // 4 == iota((slots, tiles), 1))
    here = iota((slots, 4), 1) == lax.rem(iota((slots, 4), 0), 4)

    def column(value):
        wide = lax.dot_general(
            spread, value.astype(F32).astype(BF16), (((1,), (1,)), ((), ())),
            preferred_element_type=F32,
        )
        return jnp.sum(jnp.where(here, wide, 0.0), axis=1, keepdims=True)

    chosen = jnp.where(
        iota((slots, blocks), 1).astype(F32) == column(jnp.where(used, index // 8, -1)), 1.0, 0.0
    )
    pick[...] = chosen.astype(BF16)
    place[...] = jnp.transpose(chosen).astype(BF16)
    mask[...] = jnp.where(
        (iota((slots, 128), 1) // 16).astype(F32) == column(lax.rem(index, 8)), 1.0, 0.0
    )
    at = iota((9 * 128, 144), 0)
    fold[...] = one_hot(iota((9 * 128, 144), 1) == (at // 128) * 16 + lax.rem(at, 16))
    at = iota((144, 9 * 128), 1)
    fold_t[...] = one_hot(iota((144, 9 * 128), 0) == (at // 128) * 16 + lax.rem(at, 16))
    row = iota((2 * per_piece, 8 * per_piece), 0)
    col = iota((2 * per_piece, 8 * per_piece), 1)
    group[...] = one_hot(
        (col // 8 == lax.rem(row, per_piece)) & (lax.rem(col, 8) // 4 == row // per_piece)
    )

    rhs_copy.wait()
    pre_copy.wait()

    def first(b, carry):
        lanes = pl.ds(pl.multiple_of(b * 128, 128), 128)
        total = pre_nat[0, :, lanes] * rhs_nat[pl.ds(0, 1), lanes]
        for j in range(1, 9):
            total = total + pre_nat[j, :, lanes] * rhs_nat[pl.ds(j, 1), lanes]
        z_first[pl.ds(b, 9, stride=blocks), :] = total
        return carry

    lax.fori_loop(0, blocks, first, 0, unroll=2)
    for j in range(9):
        for o in range(2):
            at = j * blocks + o * mine
            z_all[o, :, 128 * j : 128 * j + 128] = z_first[at : at + mine, :].astype(BF16)

    row8 = iota((8, 768), 0)
    diag = iota((8, 768), 1) // 192 == lax.rem(row8, 4)
    upper = row8 < 4
    first_tile = lax.rem(iota((per_piece, 384), 1), 128) < 64
    order = (0, 2, 1)

    gamma_old = None
    alpha_old = None
    for it in range(ITERS):
        last = it + 1 == ITERS
        parity = it % 2
        if it > 0:
            z_swap.wait()
        for j in range(9):
            wide = z_all[:, :, 128 * j : 128 * j + 128].astype(F32).reshape(blocks, 128)
            picked = jnp.dot(pick[...], wide.astype(BF16), preferred_element_type=F32)
            gath[:, 128 * j : 128 * j + 128] = (picked * mask[...]).astype(BF16)
        rows[...] = jnp.dot(gath[...], fold[...], preferred_element_type=F32)

        def forward(j, h):
            left = rows[pl.ds(pl.multiple_of(8 * j, 8), 8), :].astype(BF16)
            one = jnp.dot(left, blk[2 * j], preferred_element_type=F32)
            two = jnp.dot(left, blk[2 * j + 1], preferred_element_type=F32)
            both = jnp.where(diag, jnp.where(upper, one, two), 0.0)
            mid[pl.ds(pl.multiple_of(8 * (j - h * per_piece), 8), 8), :] = (
                both[:, :384] + both[:, 384:]
            )

        def p_args(h):
            return (
                lambda peer: p_recv.at[parity, h, me_c],
                lambda slot: p_recv.at[parity, h, slot],
                ps_s.at[h],
                ps_r.at[parity, h],
            )

        for h in range(PIECES):
            if it == 0:

                def forward_chunk(c, carry):
                    blk_copy(c).wait()
                    for k in range(per_chunk // 2):
                        forward(c * (per_chunk // 2) + k, h)
                    return carry

                some = CHUNKS // PIECES
                lax.fori_loop(h * some, (h + 1) * some, forward_chunk, 0)
            else:

                def forward_some(c, carry):
                    for k in range(UNROLL):
                        forward(UNROLL * c + k, h)
                    return carry

                some = per_piece // UNROLL
                lax.fori_loop(h * some, (h + 1) * some, forward_some, 0)
            full = mid[...]
            high = full.astype(BF16)
            low = (full - high.astype(F32)).astype(BF16)
            summed = jnp.dot(group[...], high, preferred_element_type=F32) + jnp.dot(
                group[...], low, preferred_element_type=F32
            )
            summed = summed + pltpu.roll(summed, 192, 1)
            p_recv[parity, h, me_c] = jnp.where(
                first_tile, summed[:per_piece], pltpu.roll(summed[per_piece:], 64, 1)
            ).astype(BF16)
            if it == 0 and h == 0:
                pl.semaphore_wait(barrier, n_cam + n_pts - 2)
            start_cam(*p_args(h))

        if it == 0:

            def inv_dense(b, carry):
                for i in range(3):
                    inv_d[i, pl.ds(b, 3, stride=pairs), :] = inv_nat[
                        i, :, pl.ds(pl.multiple_of(b * 128, 128), 128)
                    ]
                return carry

            inv_copy.wait()
            lax.fori_loop(0, pairs, inv_dense, 0, unroll=4)
            for j in range(9):
                rows_j = pl.ds(pl.multiple_of(j * blocks + first_block, 8), mine)
                z_ref[j * mine : (j + 1) * mine, :] = z_first[rows_j, :]

            def rhs_dense(b, carry):
                lanes = pl.ds(pl.multiple_of((first_block + b) * 128, 128), 128)
                r_ref[pl.ds(b, 9, stride=mine), :] = rhs_nat[:, lanes]
                return carry

            lax.fori_loop(0, mine, rhs_dense, 0, unroll=4)
            cam_copy.wait()
            to_dense_blocks(cam_nat, 0, cam_d)

        def shares(step, carry):
            gamma, curve = carry
            z = [z_ref[at_rows(j, step), :] for j in range(9)]
            for i in range(9):
                cz = apply_row(cam_d, z, i, step)
                cz_ref[at_rows(i, step), :] = cz
                curve = curve + z[i] * cz
                gamma = gamma + z[i] * r_ref[at_rows(i, step), :]
            return gamma, curve

        zero = jnp.zeros((8, 128), F32)
        gamma, curve = lax.fori_loop(0, mine // 8, shares, (zero, zero))
        dots_c[parity, me_c, 0:1, :] = jnp.sum(gamma, axis=0, keepdims=True)
        dots_c[parity, me_c, 1:2, :] = jnp.sum(curve, axis=0, keepdims=True)
        dc_args = (
            lambda peer: dots_c.at[parity, me_c],
            lambda slot: dots_c.at[parity, slot],
            dc_s,
            dc_r.at[parity],
        )
        start_cam(*dc_args)

        def backward(j):
            both = jnp.where(
                upper[:, :384],
                jnp.broadcast_to(even[pl.ds(j, 1), :], (8, 384)),
                jnp.broadcast_to(odd[pl.ds(j, 1), :], (8, 384)),
            )
            left = jnp.where(diag, jnp.concatenate([both, both], axis=1), 0.0).astype(BF16)
            contract = (((1,), (1,)), ((), ()))
            one = lax.dot_general(left, blk[2 * j], contract, preferred_element_type=F32)
            two = lax.dot_general(left, blk[2 * j + 1], contract, preferred_element_type=F32)
            contrib[pl.ds(pl.multiple_of(8 * j, 8), 8), :] = jnp.where(upper[:, :144], one, two)

        energy = jnp.zeros((per_piece, 128), F32)
        for h in range(PIECES):
            arrive_cam(*p_args(h))
            total = p_recv[parity, h, 0].astype(F32)
            for k in range(1, n_cam):
                total = total + p_recv[parity, h, k].astype(F32)
            sums = [None] * 3
            for place_i, i in enumerate(order):
                sums[i] = total[:, 128 * place_i : 128 * place_i + 128]
            here_h = slice(h * per_piece, (h + 1) * per_piece)
            answers = []
            for i in order:
                answer = jnp.zeros((per_piece, 128), F32)
                for j in range(3):
                    at_j = slice(j * pairs + h * per_piece, j * pairs + (h + 1) * per_piece)
                    answer = answer + inv_d[i, at_j, :] * sums[j]
                answer = answer.astype(BF16).astype(F32)
                energy = energy + answer * sums[i]
                answers.append(answer)
            answer = jnp.concatenate(answers, axis=1)
            a = jnp.where(first_tile, answer, 0.0)
            even[here_h, :] = a + pltpu.roll(a, 192, 1)
            a = pltpu.roll(jnp.where(first_tile, 0.0, answer), 320, 1)
            odd[here_h, :] = a + pltpu.roll(a, 192, 1)
            if h + 1 == PIECES:
                arrive_cam(*dc_args)
                total = dots_c[parity, 0]
                for k in range(1, n_cam):
                    total = total + dots_c[parity, k]
                dots_p[parity, me_p, 0:2, :] = total[0:2]
                dots_p[parity, me_p, 2:3, :] = jnp.sum(energy, axis=0, keepdims=True)
                dots_p[parity, me_p, 3:4, :] = jnp.sum(energy, axis=0, keepdims=True)
                dp_args = (
                    lambda peer: dots_p.at[parity, me_p],
                    lambda slot: dots_p.at[parity, slot],
                    dp_s,
                    dp_r.at[parity],
                )
                start_pts(*dp_args)

            def backward_some(c, carry):
                for k in range(UNROLL):
                    backward(UNROLL * c + k)
                return carry

            some = per_piece // UNROLL
            lax.fori_loop(h * some, (h + 1) * some, backward_some, 0)

        contrib_half = contrib[...].astype(BF16)
        width = 9 // GROUPS * 128
        mask_wide = jnp.concatenate([mask[...]] * (9 // GROUPS), axis=1)
        t_swaps = []
        for g in range(GROUPS):
            lanes = slice(g * width, (g + 1) * width)
            wide = jnp.dot(contrib_half, fold_t[:, lanes], preferred_element_type=F32)
            wide = (wide * mask_wide).astype(BF16)
            put = jnp.dot(place[...], wide, preferred_element_type=F32)
            for o in range(2):
                t_send[g, o] = put[o * mine : (o + 1) * mine, :].astype(BF16)
            t_swaps.append(swap(t_send.at[g, 1 - core], t_recv.at[g], t_s.at[g], t_r.at[g]))
            t_swaps[g].start()

        def w_args(g):
            return (
                w_all.at[parity, g, me_z],
                lambda slot: w_all.at[parity, g, slot],
                w_s.at[g],
                w_r.at[parity, g],
            )

        for g in range(GROUPS):
            t_swaps[g].wait()
            w_all[parity, g, me_z] = (
                t_send[g, core].astype(F32) + t_recv[g].astype(F32)
            ).astype(BF16)
            for k in range(1, n_z):
                along_z(k, me_z, *w_args(g)).start()
        if it == 0:
            to_dense_blocks(pre_nat, first_block, pre_d)

        wait_pts(*dp_args)
        total = dots_p[parity, 0]
        for k in range(1, n_pts):
            total = total + dots_p[parity, k]
        energy_now = jnp.sum(total[2:3], axis=1, keepdims=True)
        total = dots_p[parity, 0] + dots_p[parity, 1]
        total = jnp.sum(total, axis=1, keepdims=True)
        gamma_now = total[0:1]
        curve_now = total[1:2] - energy_now
        if it == 0:
            alpha = gamma_now / curve_now
        else:
            beta = gamma_now / gamma_old
            alpha = gamma_now / (curve_now - beta * gamma_now / alpha_old)
            beta_all = jnp.broadcast_to(beta, (8, 128))
        gamma_old, alpha_old = gamma_now, alpha
        alpha_all = jnp.broadcast_to(alpha, (8, 128))

        def early(step, carry):
            for j in range(9):
                at_j = at_rows(j, step)
                d = z_ref[at_j, :]
                q = cz_ref[at_j, :]
                if it > 0:
                    d = d + beta_all * d_ref[at_j, :]
                    q = q + beta_all * q_ref[at_j, :]
                s = alpha_all * d
                if it > 0:
                    s = s_ref[at_j, :] + s
                if not last:
                    d_ref[at_j, :] = d
                q_ref[at_j, :] = q
                s_ref[at_j, :] = s
            return carry

        lax.fori_loop(0, mine // 8, early, 0)
        for h in range(PIECES):
            left_cam(*p_args(h))
        left_cam(*dc_args)

        def to_native(src, out):
            def body(b, carry):
                lanes = pl.ds(pl.multiple_of((first_block + b) * 128, 128), 128)
                out[:, lanes] = src[pl.ds(b, 9, stride=mine), :]
                return carry

            lax.fori_loop(0, mine, body, 0, unroll=4)

        def out_swap(which, out):
            half = out.at[:, lanes_here]
            return swap(half, half, out_sem.at[which, 0], out_sem.at[which, 1])

        if last:
            to_native(s_ref, sol_out)
            out_swap(0, sol_out).start()

        for g in range(GROUPS):
            for k in range(1, n_z):
                copy = along_z(k, z_peer(k), *w_args(g))
                copy.wait_recv()
                copy.wait_send()

        def late(step, carry):
            r = []
            for j in range(9):
                g, jj = j // (9 // GROUPS), j % (9 // GROUPS)
                here_j = pl.ds(pl.multiple_of(step * 16, 16), 16)
                term = w_all[parity, g, 0, here_j, jj * 128 : (jj + 1) * 128].astype(F32)
                for k in range(1, n_z):
                    term = term + w_all[
                        parity, g, k, here_j, jj * 128 : (jj + 1) * 128
                    ].astype(F32)
                rr = []
                for e in range(2):
                    at_e = at_rows(j, 2 * step + e)
                    q = q_ref[at_e, :] - term[8 * e : 8 * e + 8]
                    q_ref[at_e, :] = q
                    value = r_ref[at_e, :] - alpha_all * q
                    r_ref[at_e, :] = value
                    rr.append(value)
                r.append(rr)
            if not last:
                for i in range(9):
                    zz = []
                    for e in range(2):
                        z = apply_row(pre_d, [r[j][e] for j in range(9)], i, 2 * step + e)
                        z_ref[at_rows(i, 2 * step + e), :] = z
                        zz.append(z)
                    z_all[
                        core, pl.ds(pl.multiple_of(step * 16, 16), 16), 128 * i : 128 * i + 128
                    ] = jnp.concatenate(zz, axis=0).astype(BF16)
            return carry

        lax.fori_loop(0, mine // 16, late, 0)
        if not last:
            z_swap.start()
        else:
            to_native(r_ref, res_out)
            out_swap(1, res_out).start()
            out_swap(0, sol_out).wait()
            out_swap(1, res_out).wait()


def per_device(n_cam, n_pts, rhs, cam_block, coupling, point_inverse, precond, tile_index, tile_count):
    tiles, slots = tile_index.shape
    cams = rhs.shape[1]
    blocks = cams // 128
    mine = blocks // 2
    pairs = tiles * slots
    half = tiles // 2 // PIECES
    vec = pltpu.VMEM((9 * mine, 128), F32)
    whole = pl.BlockSpec(memory_space=pltpu.VMEM)
    hbm = pl.BlockSpec(memory_space=pltpu.HBM)
    dma = pltpu.SemaphoreType.DMA
    group = 9 // GROUPS * 128
    big = (rhs, point_inverse, cam_block, precond, coupling)
    big = [pltpu.with_memory_space_constraint(x, pltpu.HBM) for x in big]
    return pl.pallas_call(
        functools.partial(kernel, n_cam, n_pts),
        out_shape=(jax.ShapeDtypeStruct(rhs.shape, F32), jax.ShapeDtypeStruct(rhs.shape, F32)),
        in_specs=[whole, whole, hbm, hbm, hbm, hbm, hbm],
        out_specs=(whole, whole),
        scratch_shapes=[
            pltpu.VMEM(coupling.shape, BF16),
            pltpu.VMEM((9, 9, mine * 128), F32),
            pltpu.VMEM(precond.shape, F32),
            pltpu.VMEM(rhs.shape, F32),
            pltpu.VMEM(point_inverse.shape, F32),
            pltpu.VMEM((9, 9 * mine, 128), F32),
            pltpu.VMEM((9, 9 * mine, 128), F32),
            pltpu.VMEM((3, 3 * tiles // 2, 128), F32),
            pltpu.VMEM((9 * blocks, 128), F32),
            vec, vec, vec, vec, vec, vec,
            pltpu.VMEM((pairs, blocks), BF16),
            pltpu.VMEM((blocks, pairs), BF16),
            pltpu.VMEM((pairs, 128), F32),
            pltpu.VMEM((9 * 128, 144), BF16),
            pltpu.VMEM((144, 9 * 128), BF16),
            pltpu.VMEM((2 * half, 8 * half), BF16),
            pltpu.VMEM((pairs, 9 * 128), BF16),
            pltpu.VMEM((pairs, 144), F32),
            pltpu.VMEM((8 * half, 384), F32),
            pltpu.VMEM((pairs, 144), F32),
            pltpu.VMEM((tiles // 2, 384), F32),
            pltpu.VMEM((tiles // 2, 384), F32),
            pltpu.VMEM((2, PIECES, n_cam, half, 384), BF16),
            pltpu.VMEM((2, mine, 9 * 128), BF16),
            pltpu.VMEM((GROUPS, 2, mine, group), BF16),
            pltpu.VMEM((GROUPS, mine, group), BF16),
            pltpu.VMEM((2, GROUPS, n_pts // 2, mine, group), BF16),
            pltpu.VMEM((2, n_cam, 2, 128), F32),
            pltpu.VMEM((2, n_pts, 4, 128), F32),
            dma((CHUNKS,)), dma, dma, dma, dma,
            dma((PIECES, n_cam)), dma((2, PIECES, n_cam)),
            dma((2,)),
            dma((GROUPS,)), dma((GROUPS,)),
            dma((GROUPS, n_pts // 2)), dma((2, GROUPS, n_pts // 2)),
            dma((n_cam,)), dma((2, n_cam)),
            dma((n_pts,)), dma((2, n_pts)),
            dma((2, 2)),
        ],
        compiler_params=pltpu.CompilerParams(
            collective_id=0, has_side_effects=True, vmem_limit_bytes=52 * 2**20
        ),
    )(tile_index.T, tile_count.T, *big)


def solution(mesh):
    in_specs = (
        P(None, "cam"),
        P(None, None, "cam"),
        P("pts", None, "cam"),
        P(None, None, "pts"),
        P(None, None, "cam"),
        P("pts", "cam"),
        P("pts", "cam"),
    )
    out_specs = (P(None, "cam"), P(None, "cam"))
    body = functools.partial(per_device, mesh.shape["cam"], mesh.shape["pts"])
    return jax.shard_map(body, mesh=mesh, in_specs=in_specs, out_specs=out_specs, check_vma=False)
```

```python
import functools

import jax
import jax.numpy as jnp
from jax import lax
from jax.experimental import pallas as pl
from jax.experimental.pallas import tpu as pltpu
from jax.sharding import PartitionSpec as P

ITERS = 3
F32 = jnp.float32
BF16 = jnp.bfloat16
CHUNKS = 16
PIECES = 4
UNROLL = 8
GROUPS = 3
MESH = pl.DeviceIdType.MESH


def iota(shape, axis):
    return lax.broadcasted_iota(jnp.int32, shape, axis)


def one_hot(where):
    return jnp.where(where, 1.0, 0.0).astype(BF16)


def kernel(
    n_cam, n_pts,
    idx_hbm, count_hbm, rhs_hbm, inv_hbm, cam_hbm, pre_hbm, blk_hbm,
    sol_out, res_out,
    idx_ref, count_ref, blk, cam_nat, pre_nat, rhs_nat, inv_nat, cam_d, pre_d, inv_d,
    z_first, r_ref, z_ref, d_ref, s_ref, q_ref, cz_ref,
    pick, place, mask, fold, fold_t, group,
    gath, rows, mid, contrib, contrib_last, wide_ref, even, odd,
    p_recv, z_all, t_send, t_recv, w_all, dots_c, dots_p,
    blk_sem, cam_sem, pre_sem, rhs_sem, inv_sem, idx_sem, count_sem,
    ps_s, ps_r, z_sem, t_s, t_r, w_s, w_r, dc_s, dc_r, dp_s, dp_r, out_sem,
):
    me_c = lax.axis_index("cam")
    me_p = lax.axis_index("pts")
    tiles = blk.shape[0]
    pairs = tiles // 2
    slots = 4 * tiles
    per_piece = pairs // PIECES
    per_chunk = tiles // CHUNKS
    blocks = place.shape[0]
    core = lax.rem(me_p, 2)
    me_z = me_p // 2
    n_z = n_pts // 2
    mine = blocks // 2
    first_block = core * mine
    lanes_here = pl.ds(pl.multiple_of(first_block * 128, mine * 128), mine * 128)

    pre_copy = pltpu.make_async_copy(pre_hbm, pre_nat, pre_sem)
    cam_copy = pltpu.make_async_copy(cam_hbm.at[:, :, lanes_here], cam_nat, cam_sem)
    rhs_copy = pltpu.make_async_copy(rhs_hbm, rhs_nat, rhs_sem)
    inv_copy = pltpu.make_async_copy(inv_hbm, inv_nat, inv_sem)

    def blk_copy(c):
        part = pl.ds(c * per_chunk, per_chunk)
        return pltpu.make_async_copy(blk_hbm.at[part], blk.at[part], blk_sem.at[c])

    barrier = pltpu.get_barrier_semaphore()

    def cam_peer(k):
        return lax.rem(me_c + k, n_cam)

    def pts_peer(k):
        return lax.rem(me_p + k, n_pts)

    def greet_cam(k, carry):
        pl.semaphore_signal(barrier, inc=1, device_id=(cam_peer(k), me_p), device_id_type=MESH)
        return carry

    def greet_pts(k, carry):
        pl.semaphore_signal(barrier, inc=1, device_id=(me_c, pts_peer(k)), device_id_type=MESH)
        return carry

    lax.fori_loop(1, n_cam, greet_cam, 0)
    lax.fori_loop(1, n_pts, greet_pts, 0)

    idx_copy = pltpu.make_async_copy(idx_hbm, idx_ref, idx_sem)
    count_copy = pltpu.make_async_copy(count_hbm, count_ref, count_sem)
    idx_copy.start()
    count_copy.start()
    rhs_copy.start()
    pre_copy.start()

    def start_chunk(c, carry):
        blk_copy(c).start()
        return carry

    lax.fori_loop(0, CHUNKS, start_chunk, 0)
    inv_copy.start()
    cam_copy.start()

    def cam_copy_to(peer, slot, src, dst, ssem, rsem):
        return pltpu.make_async_remote_copy(
            src_ref=src(peer), dst_ref=dst(slot), send_sem=ssem.at[peer],
            recv_sem=rsem.at[slot], device_id=(peer, me_p), device_id_type=MESH,
        )

    def pts_copy_to(peer, slot, src, dst, ssem, rsem):
        return pltpu.make_async_remote_copy(
            src_ref=src(peer), dst_ref=dst(slot), send_sem=ssem.at[peer],
            recv_sem=rsem.at[slot], device_id=(me_c, peer), device_id_type=MESH,
        )

    def start_cam(*args):
        def body(k, carry):
            cam_copy_to(cam_peer(k), me_c, *args).start()
            return carry

        lax.fori_loop(1, n_cam, body, 0)

    def arrive_cam(*args):
        def body(k, carry):
            cam_copy_to(cam_peer(k), cam_peer(k), *args).wait_recv()
            return carry

        lax.fori_loop(1, n_cam, body, 0)

    def left_cam(*args):
        def body(k, carry):
            cam_copy_to(cam_peer(k), cam_peer(k), *args).wait_send()
            return carry

        lax.fori_loop(1, n_cam, body, 0)

    def start_pts(*args):
        def body(k, carry):
            pts_copy_to(pts_peer(k), me_p, *args).start()
            return carry

        lax.fori_loop(1, n_pts, body, 0)

    def wait_pts(*args):
        def body(k, carry):
            copy = pts_copy_to(pts_peer(k), pts_peer(k), *args)
            copy.wait_recv()
            copy.wait_send()
            return carry

        lax.fori_loop(1, n_pts, body, 0)

    def swap(src, dst, ssem, rsem):
        return pltpu.make_async_remote_copy(
            src_ref=src, dst_ref=dst, send_sem=ssem, recv_sem=rsem,
            device_id=(me_c, me_z * 2 + 1 - core), device_id_type=MESH,
        )

    def z_peer(k):
        return lax.rem(me_z + k, n_z)

    def along_z(k, slot, src, dst, ssem, rsem):
        return pltpu.make_async_remote_copy(
            src_ref=src, dst_ref=dst(slot), send_sem=ssem.at[k], recv_sem=rsem.at[slot],
            device_id=(me_c, z_peer(k) * 2 + core), device_id_type=MESH,
        )

    def at_rows(j, step):
        return pl.ds(pl.multiple_of(j * mine + step * 8, 8), 8)

    def to_dense_blocks(src, start, dst):
        def body(b, carry):
            lanes = pl.ds(pl.multiple_of((start + b) * 128, 128), 128)
            for i in range(9):
                dst[i, pl.ds(b, 9, stride=mine), :] = src[i, :, lanes]
            return carry

        lax.fori_loop(0, mine, body, 0)

    def apply_row(mat, vec, i, step):
        total = mat[i, at_rows(0, step), :] * vec[0]
        for j in range(1, 9):
            total = total + mat[i, at_rows(j, step), :] * vec[j]
        return total

    z_swap = swap(z_all.at[core], z_all.at[core], z_sem.at[0], z_sem.at[1])

    at = iota((9 * 128, 144), 0)
    fold[...] = one_hot(iota((9 * 128, 144), 1) == (at // 128) * 16 + lax.rem(at, 16))
    at = iota((144, 9 * 128), 1)
    fold_t[...] = one_hot(iota((144, 9 * 128), 0) == (at // 128) * 16 + lax.rem(at, 16))
    row = iota((2 * per_piece, 8 * per_piece), 0)
    col = iota((2 * per_piece, 8 * per_piece), 1)
    group[...] = one_hot(
        (col // 8 == lax.rem(row, per_piece)) & (lax.rem(col, 8) // 4 == row // per_piece)
    )
    idx_copy.wait()
    count_copy.wait()
    index = idx_ref[...]
    used = iota((4, tiles), 0) < count_ref[...]
    spread = one_hot(iota((slots, tiles), 0) // 4 == iota((slots, tiles), 1))
    here = iota((slots, 4), 1) == lax.rem(iota((slots, 4), 0), 4)

    def column(value):
        wide = lax.dot_general(
            spread, value.astype(F32).astype(BF16), (((1,), (1,)), ((), ())),
            preferred_element_type=F32,
        )
        return jnp.sum(jnp.where(here, wide, 0.0), axis=1, keepdims=True)

    chosen = jnp.where(
        iota((slots, blocks), 1).astype(F32) == column(jnp.where(used, index // 8, -1)), 1.0, 0.0
    )
    pick[...] = chosen.astype(BF16)
    place[...] = jnp.transpose(chosen).astype(BF16)
    mask[...] = jnp.where(
        (iota((slots, 128), 1) // 16).astype(F32) == column(lax.rem(index, 8)), 1.0, 0.0
    )

    rhs_copy.wait()
    pre_copy.wait()

    def first(b, carry):
        lanes = pl.ds(pl.multiple_of(b * 128, 128), 128)
        total = pre_nat[0, :, lanes] * rhs_nat[pl.ds(0, 1), lanes]
        for j in range(1, 9):
            total = total + pre_nat[j, :, lanes] * rhs_nat[pl.ds(j, 1), lanes]
        z_first[pl.ds(b, 9, stride=blocks), :] = total
        return carry

    lax.fori_loop(0, blocks, first, 0, unroll=2)
    for j in range(9):
        for o in range(2):
            at = j * blocks + o * mine
            z_all[o, :, 128 * j : 128 * j + 128] = z_first[at : at + mine, :].astype(BF16)

    row8 = iota((8, 768), 0)
    diag = iota((8, 768), 1) // 192 == lax.rem(row8, 4)
    upper = row8 < 4
    first_tile = lax.rem(iota((per_piece, 384), 1), 128) < 64
    order = (0, 2, 1)

    gamma_old = None
    alpha_old = None
    for it in range(ITERS):
        last = it + 1 == ITERS
        parity = it % 2
        if it > 0:
            z_swap.wait()
        for j in range(9):
            wide = z_all[:, :, 128 * j : 128 * j + 128].astype(F32).reshape(blocks, 128)
            picked = jnp.dot(pick[...], wide.astype(BF16), preferred_element_type=F32)
            gath[:, 128 * j : 128 * j + 128] = (picked * mask[...]).astype(BF16)
        rows[...] = jnp.dot(gath[...], fold[...], preferred_element_type=F32)

        def forward(j, h):
            left = rows[pl.ds(pl.multiple_of(8 * j, 8), 8), :].astype(BF16)
            one = jnp.dot(left, blk[2 * j], preferred_element_type=F32)
            two = jnp.dot(left, blk[2 * j + 1], preferred_element_type=F32)
            both = jnp.where(diag, jnp.where(upper, one, two), 0.0)
            mid[pl.ds(pl.multiple_of(8 * (j - h * per_piece), 8), 8), :] = (
                both[:, :384] + both[:, 384:]
            )

        def p_args(h):
            return (
                lambda peer: p_recv.at[parity, h, me_c],
                lambda slot: p_recv.at[parity, h, slot],
                ps_s.at[h],
                ps_r.at[parity, h],
            )

        for h in range(PIECES):
            if it == 0:

                def forward_chunk(c, carry):
                    blk_copy(c).wait()
                    for k in range(per_chunk // 2):
                        forward(c * (per_chunk // 2) + k, h)
                    return carry

                some = CHUNKS // PIECES
                lax.fori_loop(h * some, (h + 1) * some, forward_chunk, 0)
            else:

                def forward_some(c, carry):
                    for k in range(UNROLL):
                        forward(UNROLL * c + k, h)
                    return carry

                some = per_piece // UNROLL
                lax.fori_loop(h * some, (h + 1) * some, forward_some, 0)
            full = mid[...]
            high = full.astype(BF16)
            low = (full - high.astype(F32)).astype(BF16)
            summed = jnp.dot(group[...], high, preferred_element_type=F32) + jnp.dot(
                group[...], low, preferred_element_type=F32
            )
            summed = summed + pltpu.roll(summed, 192, 1)
            p_recv[parity, h, me_c] = jnp.where(
                first_tile, summed[:per_piece], pltpu.roll(summed[per_piece:], 64, 1)
            ).astype(BF16)
            if it == 0 and h == 0:
                pl.semaphore_wait(barrier, n_cam + n_pts - 2)
            start_cam(*p_args(h))

        if it == 0:

            def inv_dense(b, carry):
                for i in range(3):
                    inv_d[i, pl.ds(b, 3, stride=pairs), :] = inv_nat[
                        i, :, pl.ds(pl.multiple_of(b * 128, 128), 128)
                    ]
                return carry

            inv_copy.wait()
            lax.fori_loop(0, pairs, inv_dense, 0, unroll=4)
            for j in range(9):
                rows_j = pl.ds(pl.multiple_of(j * blocks + first_block, 8), mine)
                z_ref[j * mine : (j + 1) * mine, :] = z_first[rows_j, :]

            def rhs_dense(b, carry):
                lanes = pl.ds(pl.multiple_of((first_block + b) * 128, 128), 128)
                r_ref[pl.ds(b, 9, stride=mine), :] = rhs_nat[:, lanes]
                return carry

            lax.fori_loop(0, mine, rhs_dense, 0, unroll=4)
            cam_copy.wait()
            to_dense_blocks(cam_nat, 0, cam_d)

        def shares(step, carry):
            gamma, curve = carry
            z = [z_ref[at_rows(j, step), :] for j in range(9)]
            for i in range(9):
                cz = apply_row(cam_d, z, i, step)
                cz_ref[at_rows(i, step), :] = cz
                curve = curve + z[i] * cz
                gamma = gamma + z[i] * r_ref[at_rows(i, step), :]
            return gamma, curve

        zero = jnp.zeros((8, 128), F32)
        gamma, curve = lax.fori_loop(0, mine // 8, shares, (zero, zero))
        dots_c[parity, me_c, 0:1, :] = jnp.sum(gamma, axis=0, keepdims=True)
        dots_c[parity, me_c, 1:2, :] = jnp.sum(curve, axis=0, keepdims=True)
        dc_args = (
            lambda peer: dots_c.at[parity, me_c],
            lambda slot: dots_c.at[parity, slot],
            dc_s,
            dc_r.at[parity],
        )
        start_cam(*dc_args)

        def backward(j, lines, out, at):
            both = jnp.where(
                upper[:, :384],
                jnp.broadcast_to(even[pl.ds(j, 1), :], (8, 384)),
                jnp.broadcast_to(odd[pl.ds(j, 1), :], (8, 384)),
            )
            left = jnp.where(diag, jnp.concatenate([both, both], axis=1), 0.0).astype(BF16)
            contract = (((1,), (1,)), ((), ()))
            one = lax.dot_general(left, blk[2 * j, lines, :], contract, preferred_element_type=F32)
            two = lax.dot_general(
                left, blk[2 * j + 1, lines, :], contract, preferred_element_type=F32
            )
            out[at, :] = jnp.where(upper[:, : one.shape[1]], one, two)

        width = 9 // GROUPS * 128
        mask_wide = jnp.concatenate([mask[...]] * (9 // GROUPS), axis=1)
        early_rows = 8 * per_piece * (PIECES - 1)
        energy = jnp.zeros((per_piece, 128), F32)
        for h in range(PIECES):
            if h + 1 == PIECES:
                contrib_half = contrib[0:early_rows, :].astype(BF16)
                for g in range(GROUPS):
                    wide = jnp.dot(
                        contrib_half, fold_t[:, g * width : (g + 1) * width],
                        preferred_element_type=F32,
                    )
                    wide_ref[g, 0:early_rows, :] = (wide * mask_wide[:early_rows]).astype(BF16)
            arrive_cam(*p_args(h))
            total = p_recv[parity, h, 0].astype(F32)
            for k in range(1, n_cam):
                total = total + p_recv[parity, h, k].astype(F32)
            sums = [None] * 3
            for place_i, i in enumerate(order):
                sums[i] = total[:, 128 * place_i : 128 * place_i + 128]
            here_h = slice(h * per_piece, (h + 1) * per_piece)
            answers = []
            for i in order:
                answer = jnp.zeros((per_piece, 128), F32)
                for j in range(3):
                    at_j = slice(j * pairs + h * per_piece, j * pairs + (h + 1) * per_piece)
                    answer = answer + inv_d[i, at_j, :] * sums[j]
                answer = answer.astype(BF16).astype(F32)
                energy = energy + answer * sums[i]
                answers.append(answer)
            answer = jnp.concatenate(answers, axis=1)
            a = jnp.where(first_tile, answer, 0.0)
            even[here_h, :] = a + pltpu.roll(a, 192, 1)
            a = pltpu.roll(jnp.where(first_tile, 0.0, answer), 320, 1)
            odd[here_h, :] = a + pltpu.roll(a, 192, 1)
            if h + 1 == PIECES:
                arrive_cam(*dc_args)
                total = dots_c[parity, 0]
                for k in range(1, n_cam):
                    total = total + dots_c[parity, k]
                dots_p[parity, me_p, 0:2, :] = total[0:2]
                dots_p[parity, me_p, 2:3, :] = jnp.sum(energy, axis=0, keepdims=True)
                dots_p[parity, me_p, 3:4, :] = jnp.sum(energy, axis=0, keepdims=True)
                dp_args = (
                    lambda peer: dots_p.at[parity, me_p],
                    lambda slot: dots_p.at[parity, slot],
                    dp_s,
                    dp_r.at[parity],
                )
                start_pts(*dp_args)

            if h + 1 < PIECES:

                def backward_some(c, carry):
                    for k in range(UNROLL):
                        j = UNROLL * c + k
                        backward(j, slice(0, 144), contrib, pl.ds(pl.multiple_of(8 * j, 8), 8))
                    return carry

                some = per_piece // UNROLL
                lax.fori_loop(h * some, (h + 1) * some, backward_some, 0)

        def w_args(g):
            return (
                w_all.at[parity, g, me_z],
                lambda slot: w_all.at[parity, g, slot],
                w_s.at[g],
                w_r.at[parity, g],
            )

        def send_along_z(g):
            t_swaps[g].wait()
            w_all[parity, g, me_z] = (
                t_send[g, core].astype(F32) + t_recv[g].astype(F32)
            ).astype(BF16)
            for k in range(1, n_z):
                along_z(k, me_z, *w_args(g)).start()

        t_swaps = []
        lines = 144 // GROUPS
        for g in range(GROUPS):
            for k in range(per_piece):
                backward(
                    (PIECES - 1) * per_piece + k, slice(g * lines, (g + 1) * lines),
                    contrib_last.at[g], slice(8 * k, 8 * k + 8),
                )
            wide = jnp.dot(
                contrib_last[g].astype(BF16), fold_t[0:lines, 0:width], preferred_element_type=F32
            )
            wide_ref[g, early_rows:, :] = (wide * mask_wide[early_rows:]).astype(BF16)
            put = jnp.dot(place[...], wide_ref[g], preferred_element_type=F32)
            for o in range(2):
                t_send[g, o] = put[o * mine : (o + 1) * mine, :].astype(BF16)
            t_swaps.append(swap(t_send.at[g, 1 - core], t_recv.at[g], t_s.at[g], t_r.at[g]))
            t_swaps[g].start()
            if g > 0:
                send_along_z(g - 1)
        send_along_z(GROUPS - 1)
        if it == 0:
            to_dense_blocks(pre_nat, first_block, pre_d)

        wait_pts(*dp_args)
        total = dots_p[parity, 0]
        for k in range(1, n_pts):
            total = total + dots_p[parity, k]
        energy_now = jnp.sum(total[2:3], axis=1, keepdims=True)
        total = dots_p[parity, 0] + dots_p[parity, 1]
        total = jnp.sum(total, axis=1, keepdims=True)
        gamma_now = total[0:1]
        curve_now = total[1:2] - energy_now
        if it == 0:
            alpha = gamma_now / curve_now
        else:
            beta = gamma_now / gamma_old
            alpha = gamma_now / (curve_now - beta * gamma_now / alpha_old)
            beta_all = jnp.broadcast_to(beta, (8, 128))
        gamma_old, alpha_old = gamma_now, alpha
        alpha_all = jnp.broadcast_to(alpha, (8, 128))

        def early(step, carry):
            for j in range(9):
                at_j = at_rows(j, step)
                d = z_ref[at_j, :]
                q = cz_ref[at_j, :]
                if it > 0:
                    d = d + beta_all * d_ref[at_j, :]
                    q = q + beta_all * q_ref[at_j, :]
                s = alpha_all * d
                if it > 0:
                    s = s_ref[at_j, :] + s
                if not last:
                    d_ref[at_j, :] = d
                q_ref[at_j, :] = q
                s_ref[at_j, :] = s
            return carry

        lax.fori_loop(0, mine // 8, early, 0)
        for h in range(PIECES):
            left_cam(*p_args(h))
        left_cam(*dc_args)

        def to_native(src, out):
            def body(b, carry):
                lanes = pl.ds(pl.multiple_of((first_block + b) * 128, 128), 128)
                out[:, lanes] = src[pl.ds(b, 9, stride=mine), :]
                return carry

            lax.fori_loop(0, mine, body, 0, unroll=4)

        def out_swap(which, out):
            half = out.at[:, lanes_here]
            return swap(half, half, out_sem.at[which, 0], out_sem.at[which, 1])

        if last:
            to_native(s_ref, sol_out)
            out_swap(0, sol_out).start()

        def late(g, step):
            some = range(g * (9 // GROUPS), (g + 1) * (9 // GROUPS))
            here_j = pl.ds(pl.multiple_of(step * 16, 16), 16)
            r = {}
            for j in some:
                lanes = slice((j - some[0]) * 128, (j - some[0] + 1) * 128)
                term = w_all[parity, g, 0, here_j, lanes].astype(F32)
                for k in range(1, n_z):
                    term = term + w_all[parity, g, k, here_j, lanes].astype(F32)
                for e in range(2):
                    at_e = at_rows(j, 2 * step + e)
                    q = q_ref[at_e, :] - term[8 * e : 8 * e + 8]
                    q_ref[at_e, :] = q
                    value = r_ref[at_e, :] - alpha_all * q
                    r_ref[at_e, :] = value
                    r[j, e] = value
            if last:
                return
            for i in range(9):
                zz = []
                for e in range(2):
                    z = pre_d[i, at_rows(some[0], 2 * step + e), :] * r[some[0], e]
                    for j in some[1:]:
                        z = z + pre_d[i, at_rows(j, 2 * step + e), :] * r[j, e]
                    if g > 0:
                        z = z_ref[at_rows(i, 2 * step + e), :] + z
                    z_ref[at_rows(i, 2 * step + e), :] = z
                    zz.append(z)
                if g + 1 == GROUPS:
                    z_all[core, here_j, 128 * i : 128 * i + 128] = jnp.concatenate(
                        zz, axis=0
                    ).astype(BF16)

        for g in range(GROUPS):
            for k in range(1, n_z):
                along_z(k, z_peer(k), *w_args(g)).wait_recv()

            def late_step(step, carry):
                late(g, step)
                return carry

            lax.fori_loop(0, mine // 16, late_step, 0)

        def left_z():
            for g in range(GROUPS):
                for k in range(1, n_z):
                    along_z(k, z_peer(k), *w_args(g)).wait_send()

        if not last:
            z_swap.start()
            left_z()
        else:
            to_native(r_ref, res_out)
            out_swap(1, res_out).start()
            left_z()
            out_swap(0, sol_out).wait()
            out_swap(1, res_out).wait()


def per_device(n_cam, n_pts, rhs, cam_block, coupling, point_inverse, precond, tile_index, tile_count):
    tiles, slots = tile_index.shape
    cams = rhs.shape[1]
    blocks = cams // 128
    mine = blocks // 2
    pairs = tiles * slots
    half = tiles // 2 // PIECES
    vec = pltpu.VMEM((9 * mine, 128), F32)
    whole = pl.BlockSpec(memory_space=pltpu.VMEM)
    hbm = pl.BlockSpec(memory_space=pltpu.HBM)
    dma = pltpu.SemaphoreType.DMA
    group = 9 // GROUPS * 128
    big = (tile_index.T, tile_count.T, rhs, point_inverse, cam_block, precond, coupling)
    big = [pltpu.with_memory_space_constraint(x, pltpu.HBM) for x in big]
    return pl.pallas_call(
        functools.partial(kernel, n_cam, n_pts),
        out_shape=(jax.ShapeDtypeStruct(rhs.shape, F32), jax.ShapeDtypeStruct(rhs.shape, F32)),
        in_specs=[hbm] * 7,
        out_specs=(whole, whole),
        scratch_shapes=[
            pltpu.VMEM((slots, tiles), jnp.int32),
            pltpu.VMEM((1, tiles), jnp.int32),
            pltpu.VMEM(coupling.shape, BF16),
            pltpu.VMEM((9, 9, mine * 128), F32),
            pltpu.VMEM(precond.shape, F32),
            pltpu.VMEM(rhs.shape, F32),
            pltpu.VMEM(point_inverse.shape, F32),
            pltpu.VMEM((9, 9 * mine, 128), F32),
            pltpu.VMEM((9, 9 * mine, 128), F32),
            pltpu.VMEM((3, 3 * tiles // 2, 128), F32),
            pltpu.VMEM((9 * blocks, 128), F32),
            vec, vec, vec, vec, vec, vec,
            pltpu.VMEM((pairs, blocks), BF16),
            pltpu.VMEM((blocks, pairs), BF16),
            pltpu.VMEM((pairs, 128), F32),
            pltpu.VMEM((9 * 128, 144), BF16),
            pltpu.VMEM((144, 9 * 128), BF16),
            pltpu.VMEM((2 * half, 8 * half), BF16),
            pltpu.VMEM((pairs, 9 * 128), BF16),
            pltpu.VMEM((pairs, 144), F32),
            pltpu.VMEM((8 * half, 384), F32),
            pltpu.VMEM((pairs, 144), F32),
            pltpu.VMEM((GROUPS, 8 * half, 144 // GROUPS), F32),
            pltpu.VMEM((GROUPS, pairs, group), BF16),
            pltpu.VMEM((tiles // 2, 384), F32),
            pltpu.VMEM((tiles // 2, 384), F32),
            pltpu.VMEM((2, PIECES, n_cam, half, 384), BF16),
            pltpu.VMEM((2, mine, 9 * 128), BF16),
            pltpu.VMEM((GROUPS, 2, mine, group), BF16),
            pltpu.VMEM((GROUPS, mine, group), BF16),
            pltpu.VMEM((2, GROUPS, n_pts // 2, mine, group), BF16),
            pltpu.VMEM((2, n_cam, 2, 128), F32),
            pltpu.VMEM((2, n_pts, 4, 128), F32),
            dma((CHUNKS,)), dma, dma, dma, dma, dma, dma,
            dma((PIECES, n_cam)), dma((2, PIECES, n_cam)),
            dma((2,)),
            dma((GROUPS,)), dma((GROUPS,)),
            dma((GROUPS, n_pts // 2)), dma((2, GROUPS, n_pts // 2)),
            dma((n_cam,)), dma((2, n_cam)),
            dma((n_pts,)), dma((2, n_pts)),
            dma((2, 2)),
        ],
        compiler_params=pltpu.CompilerParams(
            collective_id=0, has_side_effects=True, vmem_limit_bytes=52 * 2**20
        ),
    )(*big)


def solution(mesh):
    in_specs = (
        P(None, "cam"),
        P(None, None, "cam"),
        P("pts", None, "cam"),
        P(None, None, "pts"),
        P(None, None, "cam"),
        P("pts", "cam"),
        P("pts", "cam"),
    )
    out_specs = (P(None, "cam"), P(None, "cam"))
    body = functools.partial(per_device, mesh.shape["cam"], mesh.shape["pts"])
    return jax.shard_map(body, mesh=mesh, in_specs=in_specs, out_specs=out_specs, check_vma=False)
```

```python
import functools

import jax
import jax.numpy as jnp
from jax import lax
from jax.experimental import pallas as pl
from jax.experimental.pallas import tpu as pltpu
from jax.sharding import PartitionSpec as P

ITERS = 3
F32 = jnp.float32
BF16 = jnp.bfloat16
CHUNKS = 16
PIECES = 4
GROUPS = 3
MESH = pl.DeviceIdType.MESH


def iota(shape, axis):
    return lax.broadcasted_iota(jnp.int32, shape, axis)


def eight(j):
    return slice(8 * j, 8 * j + 8) if isinstance(j, int) else pl.ds(pl.multiple_of(8 * j, 8), 8)


def one_hot(where):
    return jnp.where(where, 1.0, 0.0).astype(BF16)


def kernel(
    n_cam, n_pts,
    idx_hbm, count_hbm, rhs_hbm, inv_hbm, cam_hbm, pre_hbm, blk_hbm,
    sol_out, res_out,
    idx_ref, count_ref, blk, cam_nat, pre_nat, rhs_nat, inv_nat, cam_d, pre_d, inv_d,
    z_first, r_ref, z_ref, d_ref, s_ref, q_ref, cz_ref,
    pick, place, mask, fold, fold_t, group,
    gath, rows, mid, contrib, contrib_last, wide_ref, even, odd,
    p_recv, z_all, t_send, t_recv, w_all, dots_c, dots_p,
    blk_sem, cam_sem, pre_sem, rhs_sem, inv_sem, idx_sem, count_sem,
    ps_s, ps_r, z_sem, t_s, t_r, w_s, w_r, dc_s, dc_r, dp_s, dp_r, out_sem,
):
    me_c = lax.axis_index("cam")
    me_p = lax.axis_index("pts")
    tiles = blk.shape[0]
    pairs = tiles // 2
    slots = 4 * tiles
    per_piece = pairs // PIECES
    per_chunk = tiles // CHUNKS
    blocks = place.shape[0]
    core = lax.rem(me_p, 2)
    me_z = me_p // 2
    n_z = n_pts // 2
    mine = blocks // 2
    first_block = core * mine
    lanes_here = pl.ds(pl.multiple_of(first_block * 128, mine * 128), mine * 128)

    pre_copy = pltpu.make_async_copy(pre_hbm, pre_nat, pre_sem)
    cam_copy = pltpu.make_async_copy(cam_hbm.at[:, :, lanes_here], cam_nat, cam_sem)
    rhs_copy = pltpu.make_async_copy(rhs_hbm, rhs_nat, rhs_sem)
    inv_copy = pltpu.make_async_copy(inv_hbm, inv_nat, inv_sem)

    def blk_copy(c):
        part = pl.ds(c * per_chunk, per_chunk)
        return pltpu.make_async_copy(blk_hbm.at[part], blk.at[part], blk_sem.at[c])

    barrier = pltpu.get_barrier_semaphore()

    def cam_peer(k):
        return lax.rem(me_c + k, n_cam)

    def pts_peer(k):
        return lax.rem(me_p + k, n_pts)

    def greet_cam(k, carry):
        pl.semaphore_signal(barrier, inc=1, device_id=(cam_peer(k), me_p), device_id_type=MESH)
        return carry

    def greet_pts(k, carry):
        pl.semaphore_signal(barrier, inc=1, device_id=(me_c, pts_peer(k)), device_id_type=MESH)
        return carry

    lax.fori_loop(1, n_cam, greet_cam, 0)
    lax.fori_loop(1, n_pts, greet_pts, 0)

    idx_copy = pltpu.make_async_copy(idx_hbm, idx_ref, idx_sem)
    count_copy = pltpu.make_async_copy(count_hbm, count_ref, count_sem)
    idx_copy.start()
    count_copy.start()
    rhs_copy.start()
    pre_copy.start()

    def start_chunk(c, carry):
        blk_copy(c).start()
        return carry

    lax.fori_loop(0, CHUNKS, start_chunk, 0)
    inv_copy.start()
    cam_copy.start()

    def cam_copy_to(peer, slot, src, dst, ssem, rsem):
        return pltpu.make_async_remote_copy(
            src_ref=src(peer), dst_ref=dst(slot), send_sem=ssem.at[peer],
            recv_sem=rsem.at[slot], device_id=(peer, me_p), device_id_type=MESH,
        )

    def pts_copy_to(peer, slot, src, dst, ssem, rsem):
        return pltpu.make_async_remote_copy(
            src_ref=src(peer), dst_ref=dst(slot), send_sem=ssem.at[peer],
            recv_sem=rsem.at[slot], device_id=(me_c, peer), device_id_type=MESH,
        )

    def start_cam(*args):
        def body(k, carry):
            cam_copy_to(cam_peer(k), me_c, *args).start()
            return carry

        lax.fori_loop(1, n_cam, body, 0)

    def arrive_cam(*args):
        def body(k, carry):
            cam_copy_to(cam_peer(k), cam_peer(k), *args).wait_recv()
            return carry

        lax.fori_loop(1, n_cam, body, 0)

    def left_cam(*args):
        def body(k, carry):
            cam_copy_to(cam_peer(k), cam_peer(k), *args).wait_send()
            return carry

        lax.fori_loop(1, n_cam, body, 0)

    def start_pts(*args):
        def body(k, carry):
            pts_copy_to(pts_peer(k), me_p, *args).start()
            return carry

        lax.fori_loop(1, n_pts, body, 0)

    def wait_pts(*args):
        def body(k, carry):
            copy = pts_copy_to(pts_peer(k), pts_peer(k), *args)
            copy.wait_recv()
            copy.wait_send()
            return carry

        lax.fori_loop(1, n_pts, body, 0)

    def swap(src, dst, ssem, rsem):
        return pltpu.make_async_remote_copy(
            src_ref=src, dst_ref=dst, send_sem=ssem, recv_sem=rsem,
            device_id=(me_c, me_z * 2 + 1 - core), device_id_type=MESH,
        )

    def z_peer(k):
        return lax.rem(me_z + k, n_z)

    def along_z(k, slot, src, dst, ssem, rsem):
        return pltpu.make_async_remote_copy(
            src_ref=src, dst_ref=dst(slot), send_sem=ssem.at[k], recv_sem=rsem.at[slot],
            device_id=(me_c, z_peer(k) * 2 + core), device_id_type=MESH,
        )

    def at_rows(j, step):
        return pl.ds(pl.multiple_of(j * mine + step * 8, 8), 8)

    def to_dense_blocks(src, start, dst):
        def body(b, carry):
            lanes = pl.ds(pl.multiple_of((start + b) * 128, 128), 128)
            for i in range(9):
                dst[i, pl.ds(b, 9, stride=mine), :] = src[i, :, lanes]
            return carry

        lax.fori_loop(0, mine, body, 0)

    def apply_row(mat, vec, i, step):
        total = mat[i, at_rows(0, step), :] * vec[0]
        for j in range(1, 9):
            total = total + mat[i, at_rows(j, step), :] * vec[j]
        return total

    z_swap = swap(z_all.at[core], z_all.at[core], z_sem.at[0], z_sem.at[1])

    at = iota((9 * 128, 144), 0)
    fold[...] = one_hot(iota((9 * 128, 144), 1) == (at // 128) * 16 + lax.rem(at, 16))
    at = iota((144, 9 * 128), 1)
    fold_t[...] = one_hot(iota((144, 9 * 128), 0) == (at // 128) * 16 + lax.rem(at, 16))
    row = iota((2 * per_piece, 8 * per_piece), 0)
    col = iota((2 * per_piece, 8 * per_piece), 1)
    group[...] = one_hot(
        (col // 8 == lax.rem(row, per_piece)) & (lax.rem(col, 8) // 4 == row // per_piece)
    )
    idx_copy.wait()
    count_copy.wait()
    index = idx_ref[...]
    used = iota((4, tiles), 0) < count_ref[...]
    spread = one_hot(iota((slots, tiles), 0) // 4 == iota((slots, tiles), 1))
    here = iota((slots, 4), 1) == lax.rem(iota((slots, 4), 0), 4)

    def column(value):
        wide = lax.dot_general(
            spread, value.astype(F32).astype(BF16), (((1,), (1,)), ((), ())),
            preferred_element_type=F32,
        )
        return jnp.sum(jnp.where(here, wide, 0.0), axis=1, keepdims=True)

    chosen = jnp.where(
        iota((slots, blocks), 1).astype(F32) == column(jnp.where(used, index // 8, -1)), 1.0, 0.0
    )
    pick[...] = chosen.astype(BF16)
    place[...] = jnp.transpose(chosen).astype(BF16)
    mask[...] = jnp.where(
        (iota((slots, 128), 1) // 16).astype(F32) == column(lax.rem(index, 8)), 1.0, 0.0
    )

    rhs_copy.wait()
    pre_copy.wait()

    def first(b, carry):
        lanes = pl.ds(pl.multiple_of(b * 128, 128), 128)
        total = pre_nat[0, :, lanes] * rhs_nat[pl.ds(0, 1), lanes]
        for j in range(1, 9):
            total = total + pre_nat[j, :, lanes] * rhs_nat[pl.ds(j, 1), lanes]
        z_first[pl.ds(b, 9, stride=blocks), :] = total
        return carry

    lax.fori_loop(0, blocks, first, 0, unroll=2)
    for j in range(9):
        for o in range(2):
            at = j * blocks + o * mine
            z_all[o, :, 128 * j : 128 * j + 128] = z_first[at : at + mine, :].astype(BF16)

    row8 = iota((8, 768), 0)
    diag = iota((8, 768), 1) // 192 == lax.rem(row8, 4)
    upper = row8 < 4
    first_tile = lax.rem(iota((per_piece, 384), 1), 128) < 64
    order = (0, 2, 1)

    gamma_old = None
    alpha_old = None
    for it in range(ITERS):
        last = it + 1 == ITERS
        parity = it % 2
        if it > 0:
            z_swap.wait()
        def gather(h):
            some = slice(8 * per_piece * h, 8 * per_piece * (h + 1))
            for j in range(9):
                wide = z_all[:, :, 128 * j : 128 * j + 128].reshape(blocks, 128)
                picked = jnp.dot(pick[some, :], wide, preferred_element_type=F32)
                gath[some, 128 * j : 128 * j + 128] = (picked * mask[some, :]).astype(BF16)
            rows[some, :] = jnp.dot(gath[some, :], fold[...], preferred_element_type=F32)

        def forward(j, h):
            left = rows[eight(j), :].astype(BF16)
            one = jnp.dot(left, blk[2 * j], preferred_element_type=F32)
            two = jnp.dot(left, blk[2 * j + 1], preferred_element_type=F32)
            both = jnp.where(diag, jnp.where(upper, one, two), 0.0)
            mid[eight(j - h * per_piece), :] = (
                both[:, :384] + both[:, 384:]
            )

        def p_args(h):
            return (
                lambda peer: p_recv.at[parity, h, me_c],
                lambda slot: p_recv.at[parity, h, slot],
                ps_s.at[h],
                ps_r.at[parity, h],
            )

        for h in range(PIECES):
            gather(h)
            if it == 0:

                def forward_chunk(c, carry):
                    blk_copy(c).wait()
                    for k in range(per_chunk // 2):
                        forward(c * (per_chunk // 2) + k, h)
                    return carry

                some = CHUNKS // PIECES
                lax.fori_loop(h * some, (h + 1) * some, forward_chunk, 0)
            else:

                for k in range(per_piece):
                    forward(h * per_piece + k, h)
            full = mid[...]
            high = full.astype(BF16)
            low = (full - high.astype(F32)).astype(BF16)
            summed = jnp.dot(group[...], high, preferred_element_type=F32) + jnp.dot(
                group[...], low, preferred_element_type=F32
            )
            summed = summed + pltpu.roll(summed, 192, 1)
            p_recv[parity, h, me_c] = jnp.where(
                first_tile, summed[:per_piece], pltpu.roll(summed[per_piece:], 64, 1)
            ).astype(BF16)
            if it == 0 and h == 0:
                pl.semaphore_wait(barrier, n_cam + n_pts - 2)
            start_cam(*p_args(h))

        if it == 0:

            def inv_dense(b, carry):
                for i in range(3):
                    inv_d[i, pl.ds(b, 3, stride=pairs), :] = inv_nat[
                        i, :, pl.ds(pl.multiple_of(b * 128, 128), 128)
                    ]
                return carry

            inv_copy.wait()
            lax.fori_loop(0, pairs, inv_dense, 0, unroll=4)
            for j in range(9):
                rows_j = pl.ds(pl.multiple_of(j * blocks + first_block, 8), mine)
                z_ref[j * mine : (j + 1) * mine, :] = z_first[rows_j, :]

            def rhs_dense(b, carry):
                lanes = pl.ds(pl.multiple_of((first_block + b) * 128, 128), 128)
                r_ref[pl.ds(b, 9, stride=mine), :] = rhs_nat[:, lanes]
                return carry

            lax.fori_loop(0, mine, rhs_dense, 0, unroll=4)
            cam_copy.wait()
            to_dense_blocks(cam_nat, 0, cam_d)

        def shares(step, carry):
            gamma, curve = carry
            z = [z_ref[at_rows(j, step), :] for j in range(9)]
            for i in range(9):
                cz = apply_row(cam_d, z, i, step)
                cz_ref[at_rows(i, step), :] = cz
                curve = curve + z[i] * cz
                gamma = gamma + z[i] * r_ref[at_rows(i, step), :]
            return gamma, curve

        zero = jnp.zeros((8, 128), F32)
        gamma, curve = lax.fori_loop(0, mine // 8, shares, (zero, zero))
        dots_c[parity, me_c, 0:1, :] = jnp.sum(gamma, axis=0, keepdims=True)
        dots_c[parity, me_c, 1:2, :] = jnp.sum(curve, axis=0, keepdims=True)
        dc_args = (
            lambda peer: dots_c.at[parity, me_c],
            lambda slot: dots_c.at[parity, slot],
            dc_s,
            dc_r.at[parity],
        )
        start_cam(*dc_args)

        def backward(j, lines, out, at):
            both = jnp.where(
                upper[:, :384],
                jnp.broadcast_to(even[j : j + 1, :], (8, 384)),
                jnp.broadcast_to(odd[j : j + 1, :], (8, 384)),
            )
            left = jnp.where(diag, jnp.concatenate([both, both], axis=1), 0.0).astype(BF16)
            contract = (((1,), (1,)), ((), ()))
            one = lax.dot_general(left, blk[2 * j, lines, :], contract, preferred_element_type=F32)
            two = lax.dot_general(
                left, blk[2 * j + 1, lines, :], contract, preferred_element_type=F32
            )
            out[at, :] = jnp.where(upper[:, : one.shape[1]], one, two)

        width = 9 // GROUPS * 128
        mask_wide = jnp.concatenate([mask[...]] * (9 // GROUPS), axis=1)
        early_rows = 8 * per_piece * (PIECES - 1)
        energy = jnp.zeros((per_piece, 128), F32)
        for h in range(PIECES):
            if h + 1 == PIECES:
                contrib_half = contrib[0:early_rows, :].astype(BF16)
                for g in range(GROUPS):
                    wide = jnp.dot(
                        contrib_half, fold_t[:, g * width : (g + 1) * width],
                        preferred_element_type=F32,
                    )
                    wide_ref[g, 0:early_rows, :] = (wide * mask_wide[:early_rows]).astype(BF16)
            arrive_cam(*p_args(h))
            total = p_recv[parity, h, 0].astype(F32)
            for k in range(1, n_cam):
                total = total + p_recv[parity, h, k].astype(F32)
            sums = [None] * 3
            for place_i, i in enumerate(order):
                sums[i] = total[:, 128 * place_i : 128 * place_i + 128]
            here_h = slice(h * per_piece, (h + 1) * per_piece)
            answers = []
            for i in order:
                answer = jnp.zeros((per_piece, 128), F32)
                for j in range(3):
                    at_j = slice(j * pairs + h * per_piece, j * pairs + (h + 1) * per_piece)
                    answer = answer + inv_d[i, at_j, :] * sums[j]
                answer = answer.astype(BF16).astype(F32)
                energy = energy + answer * sums[i]
                answers.append(answer)
            answer = jnp.concatenate(answers, axis=1)
            a = jnp.where(first_tile, answer, 0.0)
            even[here_h, :] = a + pltpu.roll(a, 192, 1)
            a = pltpu.roll(jnp.where(first_tile, 0.0, answer), 320, 1)
            odd[here_h, :] = a + pltpu.roll(a, 192, 1)
            if h + 1 == PIECES:
                arrive_cam(*dc_args)
                total = dots_c[parity, 0]
                for k in range(1, n_cam):
                    total = total + dots_c[parity, k]
                dots_p[parity, me_p, 0:2, :] = total[0:2]
                dots_p[parity, me_p, 2:3, :] = jnp.sum(energy, axis=0, keepdims=True)
                dots_p[parity, me_p, 3:4, :] = jnp.sum(energy, axis=0, keepdims=True)
                dp_args = (
                    lambda peer: dots_p.at[parity, me_p],
                    lambda slot: dots_p.at[parity, slot],
                    dp_s,
                    dp_r.at[parity],
                )
                start_pts(*dp_args)

            if h + 1 < PIECES:

                for k in range(per_piece):
                    j = h * per_piece + k
                    backward(j, slice(0, 144), contrib, slice(8 * j, 8 * j + 8))

        def w_args(g):
            return (
                w_all.at[parity, g, me_z],
                lambda slot: w_all.at[parity, g, slot],
                w_s.at[g],
                w_r.at[parity, g],
            )

        def send_along_z(g):
            t_swaps[g].wait()
            w_all[parity, g, me_z] = (
                t_send[g, core].astype(F32) + t_recv[g].astype(F32)
            ).astype(BF16)
            for k in range(1, n_z):
                along_z(k, me_z, *w_args(g)).start()

        t_swaps = []
        lines = 144 // GROUPS
        for g in range(GROUPS):
            for k in range(per_piece):
                backward(
                    (PIECES - 1) * per_piece + k, slice(g * lines, (g + 1) * lines),
                    contrib_last.at[g], slice(8 * k, 8 * k + 8),
                )
            wide = jnp.dot(
                contrib_last[g].astype(BF16), fold_t[0:lines, 0:width], preferred_element_type=F32
            )
            wide_ref[g, early_rows:, :] = (wide * mask_wide[early_rows:]).astype(BF16)
            put = jnp.dot(place[...], wide_ref[g], preferred_element_type=F32)
            for o in range(2):
                t_send[g, o] = put[o * mine : (o + 1) * mine, :].astype(BF16)
            t_swaps.append(swap(t_send.at[g, 1 - core], t_recv.at[g], t_s.at[g], t_r.at[g]))
            t_swaps[g].start()
            if g > 0:
                send_along_z(g - 1)
        send_along_z(GROUPS - 1)
        if it == 0:
            to_dense_blocks(pre_nat, first_block, pre_d)

        wait_pts(*dp_args)
        total = dots_p[parity, 0]
        for k in range(1, n_pts):
            total = total + dots_p[parity, k]
        energy_now = jnp.sum(total[2:3], axis=1, keepdims=True)
        total = dots_p[parity, 0] + dots_p[parity, 1]
        total = jnp.sum(total, axis=1, keepdims=True)
        gamma_now = total[0:1]
        curve_now = total[1:2] - energy_now
        if it == 0:
            alpha = gamma_now / curve_now
        else:
            beta = gamma_now / gamma_old
            alpha = gamma_now / (curve_now - beta * gamma_now / alpha_old)
            beta_all = jnp.broadcast_to(beta, (8, 128))
        gamma_old, alpha_old = gamma_now, alpha
        alpha_all = jnp.broadcast_to(alpha, (8, 128))

        def early(step, carry):
            for j in range(9):
                at_j = at_rows(j, step)
                d = z_ref[at_j, :]
                q = cz_ref[at_j, :]
                if it > 0:
                    d = d + beta_all * d_ref[at_j, :]
                    q = q + beta_all * q_ref[at_j, :]
                s = alpha_all * d
                if it > 0:
                    s = s_ref[at_j, :] + s
                if not last:
                    d_ref[at_j, :] = d
                q_ref[at_j, :] = q
                s_ref[at_j, :] = s
            return carry

        lax.fori_loop(0, mine // 8, early, 0)
        for h in range(PIECES):
            left_cam(*p_args(h))
        left_cam(*dc_args)

        def to_native(src, out):
            def body(b, carry):
                lanes = pl.ds(pl.multiple_of((first_block + b) * 128, 128), 128)
                out[:, lanes] = src[pl.ds(b, 9, stride=mine), :]
                return carry

            lax.fori_loop(0, mine, body, 0, unroll=4)

        def out_swap(which, out):
            half = out.at[:, lanes_here]
            return swap(half, half, out_sem.at[which, 0], out_sem.at[which, 1])

        if last:
            to_native(s_ref, sol_out)
            out_swap(0, sol_out).start()

        def late(g, step):
            some = range(g * (9 // GROUPS), (g + 1) * (9 // GROUPS))
            here_j = pl.ds(pl.multiple_of(step * 16, 16), 16)
            r = {}
            for j in some:
                lanes = slice((j - some[0]) * 128, (j - some[0] + 1) * 128)
                term = w_all[parity, g, 0, here_j, lanes].astype(F32)
                for k in range(1, n_z):
                    term = term + w_all[parity, g, k, here_j, lanes].astype(F32)
                for e in range(2):
                    at_e = at_rows(j, 2 * step + e)
                    q = q_ref[at_e, :] - term[8 * e : 8 * e + 8]
                    q_ref[at_e, :] = q
                    value = r_ref[at_e, :] - alpha_all * q
                    r_ref[at_e, :] = value
                    r[j, e] = value
            if last:
                return
            for i in range(9):
                zz = []
                for e in range(2):
                    z = pre_d[i, at_rows(some[0], 2 * step + e), :] * r[some[0], e]
                    for j in some[1:]:
                        z = z + pre_d[i, at_rows(j, 2 * step + e), :] * r[j, e]
                    if g > 0:
                        z = z_ref[at_rows(i, 2 * step + e), :] + z
                    z_ref[at_rows(i, 2 * step + e), :] = z
                    zz.append(z)
                if g + 1 == GROUPS:
                    z_all[core, here_j, 128 * i : 128 * i + 128] = jnp.concatenate(
                        zz, axis=0
                    ).astype(BF16)

        for g in range(GROUPS):
            for k in range(1, n_z):
                along_z(k, z_peer(k), *w_args(g)).wait_recv()

            def late_step(step, carry):
                late(g, step)
                return carry

            lax.fori_loop(0, mine // 16, late_step, 0)

        def left_z():
            for g in range(GROUPS):
                for k in range(1, n_z):
                    along_z(k, z_peer(k), *w_args(g)).wait_send()

        if not last:
            z_swap.start()
            left_z()
        else:
            to_native(r_ref, res_out)
            out_swap(1, res_out).start()
            left_z()
            out_swap(0, sol_out).wait()
            out_swap(1, res_out).wait()


def hand_out(sol, res, sol_out, res_out, sem):
    copies = [
        pltpu.make_async_copy(sol, sol_out, sem.at[0]),
        pltpu.make_async_copy(res, res_out, sem.at[1]),
    ]
    for copy in copies:
        copy.start()
    for copy in copies:
        copy.wait()


def per_device(n_cam, n_pts, rhs, cam_block, coupling, point_inverse, precond, tile_index, tile_count):
    tiles, slots = tile_index.shape
    cams = rhs.shape[1]
    blocks = cams // 128
    mine = blocks // 2
    pairs = tiles * slots
    half = tiles // 2 // PIECES
    vec = pltpu.VMEM((9 * mine, 128), F32)
    whole = pl.BlockSpec(memory_space=pltpu.VMEM)
    hbm = pl.BlockSpec(memory_space=pltpu.HBM)
    dma = pltpu.SemaphoreType.DMA
    group = 9 // GROUPS * 128
    big = (tile_index.T, tile_count.T, rhs, point_inverse, cam_block, precond, coupling)
    big = [pltpu.with_memory_space_constraint(x, pltpu.HBM) for x in big]
    results = pl.pallas_call(
        functools.partial(kernel, n_cam, n_pts),
        out_shape=(jax.ShapeDtypeStruct(rhs.shape, F32), jax.ShapeDtypeStruct(rhs.shape, F32)),
        in_specs=[hbm] * 7,
        out_specs=(whole, whole),
        scratch_shapes=[
            pltpu.VMEM((slots, tiles), jnp.int32),
            pltpu.VMEM((1, tiles), jnp.int32),
            pltpu.VMEM(coupling.shape, BF16),
            pltpu.VMEM((9, 9, mine * 128), F32),
            pltpu.VMEM(precond.shape, F32),
            pltpu.VMEM(rhs.shape, F32),
            pltpu.VMEM(point_inverse.shape, F32),
            pltpu.VMEM((9, 9 * mine, 128), F32),
            pltpu.VMEM((9, 9 * mine, 128), F32),
            pltpu.VMEM((3, 3 * tiles // 2, 128), F32),
            pltpu.VMEM((9 * blocks, 128), F32),
            vec, vec, vec, vec, vec, vec,
            pltpu.VMEM((pairs, blocks), BF16),
            pltpu.VMEM((blocks, pairs), BF16),
            pltpu.VMEM((pairs, 128), F32),
            pltpu.VMEM((9 * 128, 144), BF16),
            pltpu.VMEM((144, 9 * 128), BF16),
            pltpu.VMEM((2 * half, 8 * half), BF16),
            pltpu.VMEM((pairs, 9 * 128), BF16),
            pltpu.VMEM((pairs, 144), F32),
            pltpu.VMEM((8 * half, 384), F32),
            pltpu.VMEM((pairs, 144), F32),
            pltpu.VMEM((GROUPS, 8 * half, 144 // GROUPS), F32),
            pltpu.VMEM((GROUPS, pairs, group), BF16),
            pltpu.VMEM((tiles // 2, 384), F32),
            pltpu.VMEM((tiles // 2, 384), F32),
            pltpu.VMEM((2, PIECES, n_cam, half, 384), BF16),
            pltpu.VMEM((2, mine, 9 * 128), BF16),
            pltpu.VMEM((GROUPS, 2, mine, group), BF16),
            pltpu.VMEM((GROUPS, mine, group), BF16),
            pltpu.VMEM((2, GROUPS, n_pts // 2, mine, group), BF16),
            pltpu.VMEM((2, n_cam, 2, 128), F32),
            pltpu.VMEM((2, n_pts, 4, 128), F32),
            dma((CHUNKS,)), dma, dma, dma, dma, dma, dma,
            dma((PIECES, n_cam)), dma((2, PIECES, n_cam)),
            dma((2,)),
            dma((GROUPS,)), dma((GROUPS,)),
            dma((GROUPS, n_pts // 2)), dma((2, GROUPS, n_pts // 2)),
            dma((n_cam,)), dma((2, n_cam)),
            dma((n_pts,)), dma((2, n_pts)),
            dma((2, 2)),
        ],
        compiler_params=pltpu.CompilerParams(
            collective_id=0, has_side_effects=True, vmem_limit_bytes=52 * 2**20
        ),
    )(*big)
    return pl.pallas_call(
        hand_out,
        out_shape=(jax.ShapeDtypeStruct(rhs.shape, F32), jax.ShapeDtypeStruct(rhs.shape, F32)),
        in_specs=[pl.BlockSpec(memory_space=pl.ANY)] * 2,
        out_specs=(hbm, hbm),
        scratch_shapes=[dma((2,))],
        compiler_params=pltpu.CompilerParams(vmem_limit_bytes=2**20),
    )(*results)


def solution(mesh):
    in_specs = (
        P(None, "cam"),
        P(None, None, "cam"),
        P("pts", None, "cam"),
        P(None, None, "pts"),
        P(None, None, "cam"),
        P("pts", "cam"),
        P("pts", "cam"),
    )
    out_specs = (P(None, "cam"), P(None, "cam"))
    body = functools.partial(per_device, mesh.shape["cam"], mesh.shape["pts"])
    return jax.shard_map(body, mesh=mesh, in_specs=in_specs, out_specs=out_specs, check_vma=False)
```

```python
import functools

import jax
import jax.numpy as jnp
from jax import lax
from jax.experimental import pallas as pl
from jax.experimental.pallas import tpu as pltpu
from jax.sharding import PartitionSpec as P

ITERS = 3
F32 = jnp.float32
BF16 = jnp.bfloat16
CHUNKS = 16
PIECES = 4
UNROLL = 8
GROUPS = 3
MESH = pl.DeviceIdType.MESH


def iota(shape, axis):
    return lax.broadcasted_iota(jnp.int32, shape, axis)


def one_hot(where):
    return jnp.where(where, 1.0, 0.0).astype(BF16)


def kernel(
    n_cam, n_pts,
    idx_hbm, count_hbm, rhs_hbm, inv_hbm, cam_hbm, pre_hbm, blk_hbm,
    sol_out, res_out,
    idx_ref, count_ref, blk, cam_nat, pre_nat, rhs_nat, inv_nat, cam_d, pre_d, inv_d,
    z_first, r_ref, z_ref, d_ref, s_ref, q_ref, cz_ref,
    pick, place, mask, fold, fold_t, group,
    gath, rows, mid, contrib, contrib_last, wide_ref, even, odd,
    p_recv, z_all, t_send, t_recv, w_all, dots_c, dots_p,
    blk_sem, cam_sem, pre_sem, rhs_sem, inv_sem, idx_sem, count_sem,
    ps_s, ps_r, z_sem, t_s, t_r, w_s, w_r, dc_s, dc_r, dp_s, dp_r, out_sem,
):
    me_c = lax.axis_index("cam")
    me_p = lax.axis_index("pts")
    tiles = blk.shape[0]
    pairs = tiles // 2
    slots = 4 * tiles
    per_piece = pairs // PIECES
    per_chunk = tiles // CHUNKS
    blocks = place.shape[0]
    core = lax.rem(me_p, 2)
    me_z = me_p // 2
    n_z = n_pts // 2
    mine = blocks // 2
    first_block = core * mine
    lanes_here = pl.ds(pl.multiple_of(first_block * 128, mine * 128), mine * 128)

    pre_copy = pltpu.make_async_copy(pre_hbm, pre_nat, pre_sem)
    cam_copy = pltpu.make_async_copy(cam_hbm.at[:, :, lanes_here], cam_nat, cam_sem)
    rhs_copy = pltpu.make_async_copy(rhs_hbm, rhs_nat, rhs_sem)
    inv_copy = pltpu.make_async_copy(inv_hbm, inv_nat, inv_sem)

    def blk_copy(c):
        part = pl.ds(c * per_chunk, per_chunk)
        return pltpu.make_async_copy(blk_hbm.at[part], blk.at[part], blk_sem.at[c])

    barrier = pltpu.get_barrier_semaphore()

    def cam_peer(k):
        return lax.rem(me_c + k, n_cam)

    def pts_peer(k):
        return lax.rem(me_p + k, n_pts)

    def greet_cam(k, carry):
        pl.semaphore_signal(barrier, inc=1, device_id=(cam_peer(k), me_p), device_id_type=MESH)
        return carry

    def greet_pts(k, carry):
        pl.semaphore_signal(barrier, inc=1, device_id=(me_c, pts_peer(k)), device_id_type=MESH)
        return carry

    lax.fori_loop(1, n_cam, greet_cam, 0)
    lax.fori_loop(1, n_pts, greet_pts, 0)

    idx_copy = pltpu.make_async_copy(idx_hbm, idx_ref, idx_sem)
    count_copy = pltpu.make_async_copy(count_hbm, count_ref, count_sem)
    idx_copy.start()
    count_copy.start()
    rhs_copy.start()
    pre_copy.start()

    def start_chunk(c, carry):
        blk_copy(c).start()
        return carry

    lax.fori_loop(0, CHUNKS, start_chunk, 0)
    inv_copy.start()
    cam_copy.start()

    def cam_copy_to(peer, slot, src, dst, ssem, rsem):
        return pltpu.make_async_remote_copy(
            src_ref=src(peer), dst_ref=dst(slot), send_sem=ssem.at[peer],
            recv_sem=rsem.at[slot], device_id=(peer, me_p), device_id_type=MESH,
        )

    def pts_copy_to(peer, slot, src, dst, ssem, rsem):
        return pltpu.make_async_remote_copy(
            src_ref=src(peer), dst_ref=dst(slot), send_sem=ssem.at[peer],
            recv_sem=rsem.at[slot], device_id=(me_c, peer), device_id_type=MESH,
        )

    side = 4
    far = [(dy, dx) for dy in range(n_cam // side) for dx in range(side)][1:]
    far.sort(key=lambda at: -min(at[0], n_cam // side - at[0]) - min(at[1], side - at[1]))
    far = [
        lax.rem(me_c // side + dy, n_cam // side) * side + lax.rem(lax.rem(me_c, side) + dx, side)
        for dy, dx in far
    ]

    def start_cam(*args):
        for peer in far:
            cam_copy_to(peer, me_c, *args).start()

    def arrive_cam(*args):
        def body(k, carry):
            cam_copy_to(cam_peer(k), cam_peer(k), *args).wait_recv()
            return carry

        lax.fori_loop(1, n_cam, body, 0)

    def left_cam(*args):
        def body(k, carry):
            cam_copy_to(cam_peer(k), cam_peer(k), *args).wait_send()
            return carry

        lax.fori_loop(1, n_cam, body, 0)

    def start_pts(*args):
        def body(k, carry):
            pts_copy_to(pts_peer(k), me_p, *args).start()
            return carry

        lax.fori_loop(1, n_pts, body, 0)

    def wait_pts(*args):
        def body(k, carry):
            copy = pts_copy_to(pts_peer(k), pts_peer(k), *args)
            copy.wait_recv()
            copy.wait_send()
            return carry

        lax.fori_loop(1, n_pts, body, 0)

    def swap(src, dst, ssem, rsem):
        return pltpu.make_async_remote_copy(
            src_ref=src, dst_ref=dst, send_sem=ssem, recv_sem=rsem,
            device_id=(me_c, me_z * 2 + 1 - core), device_id_type=MESH,
        )

    def z_peer(k):
        return lax.rem(me_z + k, n_z)

    def along_z(k, slot, src, dst, ssem, rsem):
        return pltpu.make_async_remote_copy(
            src_ref=src, dst_ref=dst(slot), send_sem=ssem.at[k], recv_sem=rsem.at[slot],
            device_id=(me_c, z_peer(k) * 2 + core), device_id_type=MESH,
        )

    def at_rows(j, step):
        return pl.ds(pl.multiple_of(j * mine + step * 8, 8), 8)

    def to_dense_blocks(src, start, dst):
        def body(b, carry):
            lanes = pl.ds(pl.multiple_of((start + b) * 128, 128), 128)
            for i in range(9):
                dst[i, pl.ds(b, 9, stride=mine), :] = src[i, :, lanes]
            return carry

        lax.fori_loop(0, mine, body, 0)

    def apply_row(mat, vec, i, step):
        total = mat[i, at_rows(0, step), :] * vec[0]
        for j in range(1, 9):
            total = total + mat[i, at_rows(j, step), :] * vec[j]
        return total

    z_swap = swap(z_all.at[core], z_all.at[core], z_sem.at[0], z_sem.at[1])

    at = iota((9 * 128, 144), 0)
    fold[...] = one_hot(iota((9 * 128, 144), 1) == (at // 128) * 16 + lax.rem(at, 16))
    at = iota((144, 9 * 128), 1)
    fold_t[...] = one_hot(iota((144, 9 * 128), 0) == (at // 128) * 16 + lax.rem(at, 16))
    row = iota((2 * per_piece, 8 * per_piece), 0)
    col = iota((2 * per_piece, 8 * per_piece), 1)
    group[...] = one_hot(
        (col // 8 == lax.rem(row, per_piece)) & (lax.rem(col, 8) // 4 == row // per_piece)
    )
    idx_copy.wait()
    count_copy.wait()
    index = idx_ref[...]
    used = iota((4, tiles), 0) < count_ref[...]
    spread = one_hot(iota((slots, tiles), 0) // 4 == iota((slots, tiles), 1))
    here = iota((slots, 4), 1) == lax.rem(iota((slots, 4), 0), 4)

    def column(value):
        wide = lax.dot_general(
            spread, value.astype(F32).astype(BF16), (((1,), (1,)), ((), ())),
            preferred_element_type=F32,
        )
        return jnp.sum(jnp.where(here, wide, 0.0), axis=1, keepdims=True)

    chosen = jnp.where(
        iota((slots, blocks), 1).astype(F32) == column(jnp.where(used, index // 8, -1)), 1.0, 0.0
    )
    pick[...] = chosen.astype(BF16)
    place[...] = jnp.transpose(chosen).astype(BF16)
    mask[...] = jnp.where(
        (iota((slots, 128), 1) // 16).astype(F32) == column(lax.rem(index, 8)), 1.0, 0.0
    )

    rhs_copy.wait()
    pre_copy.wait()

    def first(b, carry):
        lanes = pl.ds(pl.multiple_of(b * 128, 128), 128)
        total = pre_nat[0, :, lanes] * rhs_nat[pl.ds(0, 1), lanes]
        for j in range(1, 9):
            total = total + pre_nat[j, :, lanes] * rhs_nat[pl.ds(j, 1), lanes]
        z_first[pl.ds(b, 9, stride=blocks), :] = total
        return carry

    lax.fori_loop(0, blocks, first, 0, unroll=2)
    for j in range(9):
        for o in range(2):
            at = j * blocks + o * mine
            z_all[o, :, 128 * j : 128 * j + 128] = z_first[at : at + mine, :].astype(BF16)

    row8 = iota((8, 768), 0)
    diag = iota((8, 768), 1) // 192 == lax.rem(row8, 4)
    upper = row8 < 4
    first_tile = lax.rem(iota((per_piece, 384), 1), 128) < 64
    order = (0, 2, 1)

    gamma_old = None
    alpha_old = None
    for it in range(ITERS):
        last = it + 1 == ITERS
        parity = it % 2
        if it > 0:
            z_swap.wait()
        for j in range(9):
            wide = z_all[:, :, 128 * j : 128 * j + 128].astype(F32).reshape(blocks, 128)
            picked = jnp.dot(pick[...], wide.astype(BF16), preferred_element_type=F32)
            gath[:, 128 * j : 128 * j + 128] = (picked * mask[...]).astype(BF16)
        rows[...] = jnp.dot(gath[...], fold[...], preferred_element_type=F32)

        def forward(j, h):
            left = rows[pl.ds(pl.multiple_of(8 * j, 8), 8), :].astype(BF16)
            one = jnp.dot(left, blk[2 * j], preferred_element_type=F32)
            two = jnp.dot(left, blk[2 * j + 1], preferred_element_type=F32)
            both = jnp.where(diag, jnp.where(upper, one, two), 0.0)
            mid[pl.ds(pl.multiple_of(8 * (j - h * per_piece), 8), 8), :] = (
                both[:, :384] + both[:, 384:]
            )

        def p_args(h):
            return (
                lambda peer: p_recv.at[parity, h, me_c],
                lambda slot: p_recv.at[parity, h, slot],
                ps_s.at[h],
                ps_r.at[parity, h],
            )

        for h in range(PIECES):
            if it == 0:

                def forward_chunk(c, carry):
                    blk_copy(c).wait()
                    for k in range(per_chunk // 2):
                        forward(c * (per_chunk // 2) + k, h)
                    return carry

                some = CHUNKS // PIECES
                lax.fori_loop(h * some, (h + 1) * some, forward_chunk, 0)
            else:

                def forward_some(c, carry):
                    for k in range(UNROLL):
                        forward(UNROLL * c + k, h)
                    return carry

                some = per_piece // UNROLL
                lax.fori_loop(h * some, (h + 1) * some, forward_some, 0)
            full = mid[...]
            high = full.astype(BF16)
            low = (full - high.astype(F32)).astype(BF16)
            summed = jnp.dot(group[...], high, preferred_element_type=F32) + jnp.dot(
                group[...], low, preferred_element_type=F32
            )
            summed = summed + pltpu.roll(summed, 192, 1)
            p_recv[parity, h, me_c] = jnp.where(
                first_tile, summed[:per_piece], pltpu.roll(summed[per_piece:], 64, 1)
            ).astype(BF16)
            if it == 0 and h == 0:
                pl.semaphore_wait(barrier, n_cam + n_pts - 2)
            start_cam(*p_args(h))

        if it == 0:

            def inv_dense(b, carry):
                for i in range(3):
                    inv_d[i, pl.ds(b, 3, stride=pairs), :] = inv_nat[
                        i, :, pl.ds(pl.multiple_of(b * 128, 128), 128)
                    ]
                return carry

            inv_copy.wait()
            lax.fori_loop(0, pairs, inv_dense, 0, unroll=4)
            for j in range(9):
                rows_j = pl.ds(pl.multiple_of(j * blocks + first_block, 8), mine)
                z_ref[j * mine : (j + 1) * mine, :] = z_first[rows_j, :]

            def rhs_dense(b, carry):
                lanes = pl.ds(pl.multiple_of((first_block + b) * 128, 128), 128)
                r_ref[pl.ds(b, 9, stride=mine), :] = rhs_nat[:, lanes]
                return carry

            lax.fori_loop(0, mine, rhs_dense, 0, unroll=4)
            cam_copy.wait()
            to_dense_blocks(cam_nat, 0, cam_d)

        def shares(step, carry):
            gamma, curve = carry
            z = [z_ref[at_rows(j, step), :] for j in range(9)]
            for i in range(9):
                cz = apply_row(cam_d, z, i, step)
                cz_ref[at_rows(i, step), :] = cz
                curve = curve + z[i] * cz
                gamma = gamma + z[i] * r_ref[at_rows(i, step), :]
            return gamma, curve

        zero = jnp.zeros((8, 128), F32)
        gamma, curve = lax.fori_loop(0, mine // 8, shares, (zero, zero))
        dots_c[parity, me_c, 0:1, :] = jnp.sum(gamma, axis=0, keepdims=True)
        dots_c[parity, me_c, 1:2, :] = jnp.sum(curve, axis=0, keepdims=True)
        dc_args = (
            lambda peer: dots_c.at[parity, me_c],
            lambda slot: dots_c.at[parity, slot],
            dc_s,
            dc_r.at[parity],
        )
        start_cam(*dc_args)

        def backward(j, lines, out, at):
            both = jnp.where(
                upper[:, :384],
                jnp.broadcast_to(even[pl.ds(j, 1), :], (8, 384)),
                jnp.broadcast_to(odd[pl.ds(j, 1), :], (8, 384)),
            )
            left = jnp.where(diag, jnp.concatenate([both, both], axis=1), 0.0).astype(BF16)
            contract = (((1,), (1,)), ((), ()))
            one = lax.dot_general(left, blk[2 * j, lines, :], contract, preferred_element_type=F32)
            two = lax.dot_general(
                left, blk[2 * j + 1, lines, :], contract, preferred_element_type=F32
            )
            out[at, :] = jnp.where(upper[:, : one.shape[1]], one, two)

        width = 9 // GROUPS * 128
        mask_wide = jnp.concatenate([mask[...]] * (9 // GROUPS), axis=1)
        early_rows = 8 * per_piece * (PIECES - 1)
        energy = jnp.zeros((per_piece, 128), F32)
        for h in range(PIECES):
            if h + 1 == PIECES:
                contrib_half = contrib[0:early_rows, :].astype(BF16)
                for g in range(GROUPS):
                    wide = jnp.dot(
                        contrib_half, fold_t[:, g * width : (g + 1) * width],
                        preferred_element_type=F32,
                    )
                    wide_ref[g, 0:early_rows, :] = (wide * mask_wide[:early_rows]).astype(BF16)
            arrive_cam(*p_args(h))
            total = p_recv[parity, h, 0].astype(F32)
            for k in range(1, n_cam):
                total = total + p_recv[parity, h, k].astype(F32)
            sums = [None] * 3
            for place_i, i in enumerate(order):
                sums[i] = total[:, 128 * place_i : 128 * place_i + 128]
            here_h = slice(h * per_piece, (h + 1) * per_piece)
            answers = []
            for i in order:
                answer = jnp.zeros((per_piece, 128), F32)
                for j in range(3):
                    at_j = slice(j * pairs + h * per_piece, j * pairs + (h + 1) * per_piece)
                    answer = answer + inv_d[i, at_j, :] * sums[j]
                answer = answer.astype(BF16).astype(F32)
                energy = energy + answer * sums[i]
                answers.append(answer)
            answer = jnp.concatenate(answers, axis=1)
            a = jnp.where(first_tile, answer, 0.0)
            even[here_h, :] = a + pltpu.roll(a, 192, 1)
            a = pltpu.roll(jnp.where(first_tile, 0.0, answer), 320, 1)
            odd[here_h, :] = a + pltpu.roll(a, 192, 1)
            if h + 1 == PIECES:
                arrive_cam(*dc_args)
                total = dots_c[parity, 0]
                for k in range(1, n_cam):
                    total = total + dots_c[parity, k]
                dots_p[parity, me_p, 0:2, :] = total[0:2]
                dots_p[parity, me_p, 2:3, :] = jnp.sum(energy, axis=0, keepdims=True)
                dots_p[parity, me_p, 3:4, :] = jnp.sum(energy, axis=0, keepdims=True)
                dp_args = (
                    lambda peer: dots_p.at[parity, me_p],
                    lambda slot: dots_p.at[parity, slot],
                    dp_s,
                    dp_r.at[parity],
                )
                start_pts(*dp_args)

            if h + 1 < PIECES:

                def backward_some(c, carry):
                    for k in range(UNROLL):
                        j = UNROLL * c + k
                        backward(j, slice(0, 144), contrib, pl.ds(pl.multiple_of(8 * j, 8), 8))
                    return carry

                some = per_piece // UNROLL
                lax.fori_loop(h * some, (h + 1) * some, backward_some, 0)

        def w_args(g):
            return (
                w_all.at[parity, g, me_z],
                lambda slot: w_all.at[parity, g, slot],
                w_s.at[g],
                w_r.at[parity, g],
            )

        def send_along_z(g):
            t_swaps[g].wait()
            w_all[parity, g, me_z] = (
                t_send[g, core].astype(F32) + t_recv[g].astype(F32)
            ).astype(BF16)
            for k in (2, 1, 3):
                along_z(k, me_z, *w_args(g)).start()

        t_swaps = []
        lines = 144 // GROUPS
        for g in range(GROUPS):
            for k in range(per_piece):
                backward(
                    (PIECES - 1) * per_piece + k, slice(g * lines, (g + 1) * lines),
                    contrib_last.at[g], slice(8 * k, 8 * k + 8),
                )
            wide = jnp.dot(
                contrib_last[g].astype(BF16), fold_t[0:lines, 0:width], preferred_element_type=F32
            )
            wide_ref[g, early_rows:, :] = (wide * mask_wide[early_rows:]).astype(BF16)
            put = jnp.dot(place[...], wide_ref[g], preferred_element_type=F32)
            for o in range(2):
                t_send[g, o] = put[o * mine : (o + 1) * mine, :].astype(BF16)
            t_swaps.append(swap(t_send.at[g, 1 - core], t_recv.at[g], t_s.at[g], t_r.at[g]))
            t_swaps[g].start()
            if g > 0:
                send_along_z(g - 1)
        send_along_z(GROUPS - 1)
        if it == 0:
            to_dense_blocks(pre_nat, first_block, pre_d)

        wait_pts(*dp_args)
        total = dots_p[parity, 0]
        for k in range(1, n_pts):
            total = total + dots_p[parity, k]
        energy_now = jnp.sum(total[2:3], axis=1, keepdims=True)
        total = dots_p[parity, 0] + dots_p[parity, 1]
        total = jnp.sum(total, axis=1, keepdims=True)
        gamma_now = total[0:1]
        curve_now = total[1:2] - energy_now
        if it == 0:
            alpha = gamma_now / curve_now
        else:
            beta = gamma_now / gamma_old
            alpha = gamma_now / (curve_now - beta * gamma_now / alpha_old)
            beta_all = jnp.broadcast_to(beta, (8, 128))
        gamma_old, alpha_old = gamma_now, alpha
        alpha_all = jnp.broadcast_to(alpha, (8, 128))

        def early(step, carry):
            for j in range(9):
                at_j = at_rows(j, step)
                d = z_ref[at_j, :]
                q = cz_ref[at_j, :]
                if it > 0:
                    d = d + beta_all * d_ref[at_j, :]
                    q = q + beta_all * q_ref[at_j, :]
                s = alpha_all * d
                if it > 0:
                    s = s_ref[at_j, :] + s
                if not last:
                    d_ref[at_j, :] = d
                q_ref[at_j, :] = q
                s_ref[at_j, :] = s
            return carry

        lax.fori_loop(0, mine // 8, early, 0)
        for h in range(PIECES):
            left_cam(*p_args(h))
        left_cam(*dc_args)

        def to_native(src, out):
            def body(b, carry):
                lanes = pl.ds(pl.multiple_of((first_block + b) * 128, 128), 128)
                out[:, lanes] = src[pl.ds(b, 9, stride=mine), :]
                return carry

            lax.fori_loop(0, mine, body, 0, unroll=4)

        def out_swap(which, out):
            half = out.at[:, lanes_here]
            return swap(half, half, out_sem.at[which, 0], out_sem.at[which, 1])

        if last:
            to_native(s_ref, sol_out)
            out_swap(0, sol_out).start()

        def late(g, step):
            some = range(g * (9 // GROUPS), (g + 1) * (9 // GROUPS))
            here_j = pl.ds(pl.multiple_of(step * 16, 16), 16)
            r = {}
            for j in some:
                lanes = slice((j - some[0]) * 128, (j - some[0] + 1) * 128)
                term = w_all[parity, g, 0, here_j, lanes].astype(F32)
                for k in range(1, n_z):
                    term = term + w_all[parity, g, k, here_j, lanes].astype(F32)
                for e in range(2):
                    at_e = at_rows(j, 2 * step + e)
                    q = q_ref[at_e, :] - term[8 * e : 8 * e + 8]
                    q_ref[at_e, :] = q
                    value = r_ref[at_e, :] - alpha_all * q
                    r_ref[at_e, :] = value
                    r[j, e] = value
            if last:
                return
            for i in range(9):
                zz = []
                for e in range(2):
                    z = pre_d[i, at_rows(some[0], 2 * step + e), :] * r[some[0], e]
                    for j in some[1:]:
                        z = z + pre_d[i, at_rows(j, 2 * step + e), :] * r[j, e]
                    if g > 0:
                        z = z_ref[at_rows(i, 2 * step + e), :] + z
                    z_ref[at_rows(i, 2 * step + e), :] = z
                    zz.append(z)
                if g + 1 == GROUPS:
                    z_all[core, here_j, 128 * i : 128 * i + 128] = jnp.concatenate(
                        zz, axis=0
                    ).astype(BF16)

        for g in range(GROUPS):
            for k in range(1, n_z):
                along_z(k, z_peer(k), *w_args(g)).wait_recv()

            def late_step(step, carry):
                late(g, step)
                return carry

            lax.fori_loop(0, mine // 16, late_step, 0)

        def left_z():
            for g in range(GROUPS):
                for k in range(1, n_z):
                    along_z(k, z_peer(k), *w_args(g)).wait_send()

        if not last:
            z_swap.start()
            left_z()
        else:
            to_native(r_ref, res_out)
            out_swap(1, res_out).start()
            left_z()
            out_swap(0, sol_out).wait()
            out_swap(1, res_out).wait()


def hand_out(sol, res, sol_out, res_out, sem):
    copies = [
        pltpu.make_async_copy(sol, sol_out, sem.at[0]),
        pltpu.make_async_copy(res, res_out, sem.at[1]),
    ]
    for copy in copies:
        copy.start()
    for copy in copies:
        copy.wait()


def per_device(n_cam, n_pts, rhs, cam_block, coupling, point_inverse, precond, tile_index, tile_count):
    tiles, slots = tile_index.shape
    cams = rhs.shape[1]
    blocks = cams // 128
    mine = blocks // 2
    pairs = tiles * slots
    half = tiles // 2 // PIECES
    vec = pltpu.VMEM((9 * mine, 128), F32)
    whole = pl.BlockSpec(memory_space=pltpu.VMEM)
    hbm = pl.BlockSpec(memory_space=pltpu.HBM)
    dma = pltpu.SemaphoreType.DMA
    group = 9 // GROUPS * 128
    big = (tile_index.T, tile_count.T, rhs, point_inverse, cam_block, precond, coupling)
    big = [pltpu.with_memory_space_constraint(x, pltpu.HBM) for x in big]
    results = pl.pallas_call(
        functools.partial(kernel, n_cam, n_pts),
        out_shape=(jax.ShapeDtypeStruct(rhs.shape, F32), jax.ShapeDtypeStruct(rhs.shape, F32)),
        in_specs=[hbm] * 7,
        out_specs=(whole, whole),
        scratch_shapes=[
            pltpu.VMEM((slots, tiles), jnp.int32),
            pltpu.VMEM((1, tiles), jnp.int32),
            pltpu.VMEM(coupling.shape, BF16),
            pltpu.VMEM((9, 9, mine * 128), F32),
            pltpu.VMEM(precond.shape, F32),
            pltpu.VMEM(rhs.shape, F32),
            pltpu.VMEM(point_inverse.shape, F32),
            pltpu.VMEM((9, 9 * mine, 128), F32),
            pltpu.VMEM((9, 9 * mine, 128), F32),
            pltpu.VMEM((3, 3 * tiles // 2, 128), F32),
            pltpu.VMEM((9 * blocks, 128), F32),
            vec, vec, vec, vec, vec, vec,
            pltpu.VMEM((pairs, blocks), BF16),
            pltpu.VMEM((blocks, pairs), BF16),
            pltpu.VMEM((pairs, 128), F32),
            pltpu.VMEM((9 * 128, 144), BF16),
            pltpu.VMEM((144, 9 * 128), BF16),
            pltpu.VMEM((2 * half, 8 * half), BF16),
            pltpu.VMEM((pairs, 9 * 128), BF16),
            pltpu.VMEM((pairs, 144), F32),
            pltpu.VMEM((8 * half, 384), F32),
            pltpu.VMEM((pairs, 144), F32),
            pltpu.VMEM((GROUPS, 8 * half, 144 // GROUPS), F32),
            pltpu.VMEM((GROUPS, pairs, group), BF16),
            pltpu.VMEM((tiles // 2, 384), F32),
            pltpu.VMEM((tiles // 2, 384), F32),
            pltpu.VMEM((2, PIECES, n_cam, half, 384), BF16),
            pltpu.VMEM((2, mine, 9 * 128), BF16),
            pltpu.VMEM((GROUPS, 2, mine, group), BF16),
            pltpu.VMEM((GROUPS, mine, group), BF16),
            pltpu.VMEM((2, GROUPS, n_pts // 2, mine, group), BF16),
            pltpu.VMEM((2, n_cam, 2, 128), F32),
            pltpu.VMEM((2, n_pts, 4, 128), F32),
            dma((CHUNKS,)), dma, dma, dma, dma, dma, dma,
            dma((PIECES, n_cam)), dma((2, PIECES, n_cam)),
            dma((2,)),
            dma((GROUPS,)), dma((GROUPS,)),
            dma((GROUPS, n_pts // 2)), dma((2, GROUPS, n_pts // 2)),
            dma((n_cam,)), dma((2, n_cam)),
            dma((n_pts,)), dma((2, n_pts)),
            dma((2, 2)),
        ],
        compiler_params=pltpu.CompilerParams(
            collective_id=0, has_side_effects=True, vmem_limit_bytes=52 * 2**20
        ),
    )(*big)
    return pl.pallas_call(
        hand_out,
        out_shape=(jax.ShapeDtypeStruct(rhs.shape, F32), jax.ShapeDtypeStruct(rhs.shape, F32)),
        in_specs=[pl.BlockSpec(memory_space=pl.ANY)] * 2,
        out_specs=(hbm, hbm),
        scratch_shapes=[dma((2,))],
        compiler_params=pltpu.CompilerParams(vmem_limit_bytes=2**20),
    )(*results)


def solution(mesh):
    in_specs = (
        P(None, "cam"),
        P(None, None, "cam"),
        P("pts", None, "cam"),
        P(None, None, "pts"),
        P(None, None, "cam"),
        P("pts", "cam"),
        P("pts", "cam"),
    )
    out_specs = (P(None, "cam"), P(None, "cam"))
    body = functools.partial(per_device, mesh.shape["cam"], mesh.shape["pts"])
    return jax.shard_map(body, mesh=mesh, in_specs=in_specs, out_specs=out_specs, check_vma=False)
```

```python
import functools

import jax
import jax.numpy as jnp
from jax import lax
from jax.experimental import pallas as pl
from jax.experimental.pallas import tpu as pltpu
from jax.sharding import PartitionSpec as P

ITERS = 3
F32 = jnp.float32
BF16 = jnp.bfloat16
CHUNKS = 16
PIECES = 4
UNROLL = 8
GROUPS = 3
MESH = pl.DeviceIdType.MESH


def iota(shape, axis):
    return lax.broadcasted_iota(jnp.int32, shape, axis)


def one_hot(where):
    return jnp.where(where, 1.0, 0.0).astype(BF16)


def kernel(
    n_cam, n_pts,
    idx_hbm, count_hbm, rhs_hbm, inv_hbm, cam_hbm, pre_hbm, blk_hbm,
    sol_out, res_out,
    idx_ref, count_ref, blk, cam_nat, pre_nat, rhs_nat, inv_nat, cam_d, pre_d, inv_d,
    z_first, r_ref, z_ref, d_ref, s_ref, q_ref, cz_ref,
    pick, place, mask, fold, fold_t, group,
    gath, rows, mid, contrib, contrib_last, wide_ref, even, odd,
    p_recv, z_all, t_send, t_recv, w_all, dots_c, dots_p,
    blk_sem, cam_sem, pre_sem, rhs_sem, inv_sem, idx_sem, count_sem,
    ps_s, ps_r, z_sem, t_s, t_r, w_s, w_r, dc_s, dc_r, dp_s, dp_r, out_sem,
):
    me_c = lax.axis_index("cam")
    me_p = lax.axis_index("pts")
    tiles = blk.shape[0]
    pairs = tiles // 2
    slots = 4 * tiles
    per_piece = pairs // PIECES
    per_chunk = tiles // CHUNKS
    blocks = place.shape[0]
    core = lax.rem(me_p, 2)
    me_z = me_p // 2
    n_z = n_pts // 2
    mine = blocks // 2
    first_block = core * mine
    lanes_here = pl.ds(pl.multiple_of(first_block * 128, mine * 128), mine * 128)

    pre_copy = pltpu.make_async_copy(pre_hbm, pre_nat, pre_sem)
    cam_copy = pltpu.make_async_copy(cam_hbm.at[:, :, lanes_here], cam_nat, cam_sem)
    rhs_copy = pltpu.make_async_copy(rhs_hbm, rhs_nat, rhs_sem)
    inv_copy = pltpu.make_async_copy(inv_hbm, inv_nat, inv_sem)

    def blk_copy(c):
        part = pl.ds(c * per_chunk, per_chunk)
        return pltpu.make_async_copy(blk_hbm.at[part], blk.at[part], blk_sem.at[c])

    barrier = pltpu.get_barrier_semaphore()

    def cam_peer(k):
        return lax.rem(me_c + k, n_cam)

    def pts_peer(k):
        return lax.rem(me_p + k, n_pts)

    def greet_cam(k, carry):
        pl.semaphore_signal(barrier, inc=1, device_id=(cam_peer(k), me_p), device_id_type=MESH)
        return carry

    def greet_pts(k, carry):
        pl.semaphore_signal(barrier, inc=1, device_id=(me_c, pts_peer(k)), device_id_type=MESH)
        return carry

    lax.fori_loop(1, n_cam, greet_cam, 0)
    lax.fori_loop(1, n_pts, greet_pts, 0)

    idx_copy = pltpu.make_async_copy(idx_hbm, idx_ref, idx_sem)
    count_copy = pltpu.make_async_copy(count_hbm, count_ref, count_sem)
    idx_copy.start()
    count_copy.start()
    rhs_copy.start()
    pre_copy.start()

    def start_chunk(c, carry):
        blk_copy(c).start()
        return carry

    lax.fori_loop(0, CHUNKS, start_chunk, 0)
    inv_copy.start()
    cam_copy.start()

    def cam_copy_to(peer, slot, src, dst, ssem, rsem):
        return pltpu.make_async_remote_copy(
            src_ref=src(peer), dst_ref=dst(slot), send_sem=ssem.at[peer],
            recv_sem=rsem.at[slot], device_id=(peer, me_p), device_id_type=MESH,
        )

    def pts_copy_to(peer, slot, src, dst, ssem, rsem):
        return pltpu.make_async_remote_copy(
            src_ref=src(peer), dst_ref=dst(slot), send_sem=ssem.at[peer],
            recv_sem=rsem.at[slot], device_id=(me_c, peer), device_id_type=MESH,
        )

    side = 4
    far = [(dy, dx) for dy in range(n_cam // side) for dx in range(side)][1:]
    far.sort(key=lambda at: -min(at[0], n_cam // side - at[0]) - min(at[1], side - at[1]))
    far = [
        lax.rem(me_c // side + dy, n_cam // side) * side + lax.rem(lax.rem(me_c, side) + dx, side)
        for dy, dx in far
    ]

    others = [pts_peer(k) for k in range(1, n_pts)]

    def start_cam(*args):
        for peer in far:
            cam_copy_to(peer, me_c, *args).start()

    def arrive_cam(*args):
        for peer in far[::-1]:
            cam_copy_to(peer, peer, *args).wait_recv()

    def left_cam(*args):
        for peer in far:
            cam_copy_to(peer, peer, *args).wait_send()

    def start_pts(*args):
        for peer in others:
            pts_copy_to(peer, me_p, *args).start()

    def wait_pts(*args):
        for peer in others:
            copy = pts_copy_to(peer, peer, *args)
            copy.wait_recv()
            copy.wait_send()

    def swap(src, dst, ssem, rsem):
        return pltpu.make_async_remote_copy(
            src_ref=src, dst_ref=dst, send_sem=ssem, recv_sem=rsem,
            device_id=(me_c, me_z * 2 + 1 - core), device_id_type=MESH,
        )

    def z_peer(k):
        return lax.rem(me_z + k, n_z)

    def along_z(k, slot, src, dst, ssem, rsem):
        return pltpu.make_async_remote_copy(
            src_ref=src, dst_ref=dst(slot), send_sem=ssem.at[k], recv_sem=rsem.at[slot],
            device_id=(me_c, z_peer(k) * 2 + core), device_id_type=MESH,
        )

    def at_rows(j, step):
        return pl.ds(pl.multiple_of(j * mine + step * 8, 8), 8)

    def to_dense_blocks(src, start, dst):
        def body(b, carry):
            lanes = pl.ds(pl.multiple_of((start + b) * 128, 128), 128)
            for i in range(9):
                dst[i, pl.ds(b, 9, stride=mine), :] = src[i, :, lanes]
            return carry

        lax.fori_loop(0, mine, body, 0)

    def apply_row(mat, vec, i, step):
        total = mat[i, at_rows(0, step), :] * vec[0]
        for j in range(1, 9):
            total = total + mat[i, at_rows(j, step), :] * vec[j]
        return total

    z_swap = swap(z_all.at[core], z_all.at[core], z_sem.at[0], z_sem.at[1])

    at = iota((9 * 128, 144), 0)
    fold[...] = one_hot(iota((9 * 128, 144), 1) == (at // 128) * 16 + lax.rem(at, 16))
    at = iota((144, 9 * 128), 1)
    fold_t[...] = one_hot(iota((144, 9 * 128), 0) == (at // 128) * 16 + lax.rem(at, 16))
    row = iota((2 * per_piece, 8 * per_piece), 0)
    col = iota((2 * per_piece, 8 * per_piece), 1)
    group[...] = one_hot(
        (col // 8 == lax.rem(row, per_piece)) & (lax.rem(col, 8) // 4 == row // per_piece)
    )
    idx_copy.wait()
    count_copy.wait()
    index = idx_ref[...]
    used = iota((4, tiles), 0) < count_ref[...]
    spread = one_hot(iota((slots, tiles), 0) // 4 == iota((slots, tiles), 1))
    here = iota((slots, 4), 1) == lax.rem(iota((slots, 4), 0), 4)

    def column(value):
        wide = lax.dot_general(
            spread, value.astype(F32).astype(BF16), (((1,), (1,)), ((), ())),
            preferred_element_type=F32,
        )
        return jnp.sum(jnp.where(here, wide, 0.0), axis=1, keepdims=True)

    chosen = jnp.where(
        iota((slots, blocks), 1).astype(F32) == column(jnp.where(used, index // 8, -1)), 1.0, 0.0
    )
    pick[...] = chosen.astype(BF16)
    place[...] = jnp.transpose(chosen).astype(BF16)
    mask[...] = jnp.where(
        (iota((slots, 128), 1) // 16).astype(F32) == column(lax.rem(index, 8)), 1.0, 0.0
    )

    rhs_copy.wait()
    pre_copy.wait()

    def first(b, carry):
        lanes = pl.ds(pl.multiple_of(b * 128, 128), 128)
        total = pre_nat[0, :, lanes] * rhs_nat[pl.ds(0, 1), lanes]
        for j in range(1, 9):
            total = total + pre_nat[j, :, lanes] * rhs_nat[pl.ds(j, 1), lanes]
        z_first[pl.ds(b, 9, stride=blocks), :] = total
        return carry

    lax.fori_loop(0, blocks, first, 0, unroll=2)
    for j in range(9):
        for o in range(2):
            at = j * blocks + o * mine
            z_all[o, :, 128 * j : 128 * j + 128] = z_first[at : at + mine, :].astype(BF16)

    row8 = iota((8, 768), 0)
    diag = iota((8, 768), 1) // 192 == lax.rem(row8, 4)
    upper = row8 < 4
    first_tile = lax.rem(iota((per_piece, 384), 1), 128) < 64
    order = (0, 2, 1)

    gamma_old = None
    alpha_old = None
    for it in range(ITERS):
        last = it + 1 == ITERS
        parity = it % 2
        if it > 0:
            z_swap.wait()
        for j in range(9):
            wide = z_all[:, :, 128 * j : 128 * j + 128].astype(F32).reshape(blocks, 128)
            picked = jnp.dot(pick[...], wide.astype(BF16), preferred_element_type=F32)
            gath[:, 128 * j : 128 * j + 128] = (picked * mask[...]).astype(BF16)
        rows[...] = jnp.dot(gath[...], fold[...], preferred_element_type=F32)

        def forward(j, h):
            left = rows[pl.ds(pl.multiple_of(8 * j, 8), 8), :].astype(BF16)
            one = jnp.dot(left, blk[2 * j], preferred_element_type=F32)
            two = jnp.dot(left, blk[2 * j + 1], preferred_element_type=F32)
            both = jnp.where(diag, jnp.where(upper, one, two), 0.0)
            mid[pl.ds(pl.multiple_of(8 * (j - h * per_piece), 8), 8), :] = (
                both[:, :384] + both[:, 384:]
            )

        def p_args(h):
            return (
                lambda peer: p_recv.at[parity, h, me_c],
                lambda slot: p_recv.at[parity, h, slot],
                ps_s.at[h],
                ps_r.at[parity, h],
            )

        for h in range(PIECES):
            if it == 0:

                def forward_chunk(c, carry):
                    blk_copy(c).wait()
                    for k in range(per_chunk // 2):
                        forward(c * (per_chunk // 2) + k, h)
                    return carry

                some = CHUNKS // PIECES
                lax.fori_loop(h * some, (h + 1) * some, forward_chunk, 0)
            else:

                def forward_some(c, carry):
                    for k in range(UNROLL):
                        forward(UNROLL * c + k, h)
                    return carry

                some = per_piece // UNROLL
                lax.fori_loop(h * some, (h + 1) * some, forward_some, 0)
            full = mid[...]
            high = full.astype(BF16)
            low = (full - high.astype(F32)).astype(BF16)
            summed = jnp.dot(group[...], high, preferred_element_type=F32) + jnp.dot(
                group[...], low, preferred_element_type=F32
            )
            summed = summed + pltpu.roll(summed, 192, 1)
            p_recv[parity, h, me_c] = jnp.where(
                first_tile, summed[:per_piece], pltpu.roll(summed[per_piece:], 64, 1)
            ).astype(BF16)
            if it == 0 and h == 0:
                pl.semaphore_wait(barrier, n_cam + n_pts - 2)
            start_cam(*p_args(h))

        if it == 0:

            def inv_dense(b, carry):
                for i in range(3):
                    inv_d[i, pl.ds(b, 3, stride=pairs), :] = inv_nat[
                        i, :, pl.ds(pl.multiple_of(b * 128, 128), 128)
                    ]
                return carry

            inv_copy.wait()
            lax.fori_loop(0, pairs, inv_dense, 0, unroll=4)
            for j in range(9):
                rows_j = pl.ds(pl.multiple_of(j * blocks + first_block, 8), mine)
                z_ref[j * mine : (j + 1) * mine, :] = z_first[rows_j, :]

            def rhs_dense(b, carry):
                lanes = pl.ds(pl.multiple_of((first_block + b) * 128, 128), 128)
                r_ref[pl.ds(b, 9, stride=mine), :] = rhs_nat[:, lanes]
                return carry

            lax.fori_loop(0, mine, rhs_dense, 0, unroll=4)
            cam_copy.wait()
            to_dense_blocks(cam_nat, 0, cam_d)

        def shares(step, carry):
            gamma, curve = carry
            z = [z_ref[at_rows(j, step), :] for j in range(9)]
            for i in range(9):
                cz = apply_row(cam_d, z, i, step)
                cz_ref[at_rows(i, step), :] = cz
                curve = curve + z[i] * cz
                gamma = gamma + z[i] * r_ref[at_rows(i, step), :]
            return gamma, curve

        zero = jnp.zeros((8, 128), F32)
        gamma, curve = lax.fori_loop(0, mine // 8, shares, (zero, zero))
        dots_c[parity, me_c, 0:1, :] = jnp.sum(gamma, axis=0, keepdims=True)
        dots_c[parity, me_c, 1:2, :] = jnp.sum(curve, axis=0, keepdims=True)
        dc_args = (
            lambda peer: dots_c.at[parity, me_c],
            lambda slot: dots_c.at[parity, slot],
            dc_s,
            dc_r.at[parity],
        )
        start_cam(*dc_args)

        def backward(j, lines, out, at):
            both = jnp.where(
                upper[:, :384],
                jnp.broadcast_to(even[pl.ds(j, 1), :], (8, 384)),
                jnp.broadcast_to(odd[pl.ds(j, 1), :], (8, 384)),
            )
            left = jnp.where(diag, jnp.concatenate([both, both], axis=1), 0.0).astype(BF16)
            contract = (((1,), (1,)), ((), ()))
            one = lax.dot_general(left, blk[2 * j, lines, :], contract, preferred_element_type=F32)
            two = lax.dot_general(
                left, blk[2 * j + 1, lines, :], contract, preferred_element_type=F32
            )
            out[at, :] = jnp.where(upper[:, : one.shape[1]], one, two)

        width = 9 // GROUPS * 128
        mask_wide = jnp.concatenate([mask[...]] * (9 // GROUPS), axis=1)
        early_rows = 8 * per_piece * (PIECES - 1)
        energy = jnp.zeros((per_piece, 128), F32)
        for h in range(PIECES):
            if h + 1 == PIECES:
                contrib_half = contrib[0:early_rows, :].astype(BF16)
                for g in range(GROUPS):
                    wide = jnp.dot(
                        contrib_half, fold_t[:, g * width : (g + 1) * width],
                        preferred_element_type=F32,
                    )
                    wide_ref[g, 0:early_rows, :] = (wide * mask_wide[:early_rows]).astype(BF16)
            arrive_cam(*p_args(h))
            total = p_recv[parity, h, 0].astype(F32)
            for k in range(1, n_cam):
                total = total + p_recv[parity, h, k].astype(F32)
            sums = [None] * 3
            for place_i, i in enumerate(order):
                sums[i] = total[:, 128 * place_i : 128 * place_i + 128]
            here_h = slice(h * per_piece, (h + 1) * per_piece)
            answers = []
            for i in order:
                answer = jnp.zeros((per_piece, 128), F32)
                for j in range(3):
                    at_j = slice(j * pairs + h * per_piece, j * pairs + (h + 1) * per_piece)
                    answer = answer + inv_d[i, at_j, :] * sums[j]
                answer = answer.astype(BF16).astype(F32)
                energy = energy + answer * sums[i]
                answers.append(answer)
            answer = jnp.concatenate(answers, axis=1)
            a = jnp.where(first_tile, answer, 0.0)
            even[here_h, :] = a + pltpu.roll(a, 192, 1)
            a = pltpu.roll(jnp.where(first_tile, 0.0, answer), 320, 1)
            odd[here_h, :] = a + pltpu.roll(a, 192, 1)
            if h + 1 == PIECES:
                arrive_cam(*dc_args)
                total = dots_c[parity, 0]
                for k in range(1, n_cam):
                    total = total + dots_c[parity, k]
                dots_p[parity, me_p, 0:2, :] = total[0:2]
                dots_p[parity, me_p, 2:3, :] = jnp.sum(energy, axis=0, keepdims=True)
                dots_p[parity, me_p, 3:4, :] = jnp.sum(energy, axis=0, keepdims=True)
                dp_args = (
                    lambda peer: dots_p.at[parity, me_p],
                    lambda slot: dots_p.at[parity, slot],
                    dp_s,
                    dp_r.at[parity],
                )
                start_pts(*dp_args)

            if h + 1 < PIECES:

                def backward_some(c, carry):
                    for k in range(UNROLL):
                        j = UNROLL * c + k
                        backward(j, slice(0, 144), contrib, pl.ds(pl.multiple_of(8 * j, 8), 8))
                    return carry

                some = per_piece // UNROLL
                lax.fori_loop(h * some, (h + 1) * some, backward_some, 0)

        def w_args(g):
            return (
                w_all.at[parity, g, me_z],
                lambda slot: w_all.at[parity, g, slot],
                w_s.at[g],
                w_r.at[parity, g],
            )

        def send_along_z(g):
            t_swaps[g].wait()
            w_all[parity, g, me_z] = (
                t_send[g, core].astype(F32) + t_recv[g].astype(F32)
            ).astype(BF16)
            for k in (2, 1, 3):
                along_z(k, me_z, *w_args(g)).start()

        t_swaps = []
        lines = 144 // GROUPS
        for g in range(GROUPS):
            for k in range(per_piece):
                backward(
                    (PIECES - 1) * per_piece + k, slice(g * lines, (g + 1) * lines),
                    contrib_last.at[g], slice(8 * k, 8 * k + 8),
                )
            wide = jnp.dot(
                contrib_last[g].astype(BF16), fold_t[0:lines, 0:width], preferred_element_type=F32
            )
            wide_ref[g, early_rows:, :] = (wide * mask_wide[early_rows:]).astype(BF16)
            put = jnp.dot(place[...], wide_ref[g], preferred_element_type=F32)
            for o in range(2):
                t_send[g, o] = put[o * mine : (o + 1) * mine, :].astype(BF16)
            t_swaps.append(swap(t_send.at[g, 1 - core], t_recv.at[g], t_s.at[g], t_r.at[g]))
            t_swaps[g].start()
            if g > 0:
                send_along_z(g - 1)
        send_along_z(GROUPS - 1)
        if it == 0:
            to_dense_blocks(pre_nat, first_block, pre_d)

        wait_pts(*dp_args)
        total = dots_p[parity, 0]
        for k in range(1, n_pts):
            total = total + dots_p[parity, k]
        energy_now = jnp.sum(total[2:3], axis=1, keepdims=True)
        total = dots_p[parity, 0] + dots_p[parity, 1]
        total = jnp.sum(total, axis=1, keepdims=True)
        gamma_now = total[0:1]
        curve_now = total[1:2] - energy_now
        if it == 0:
            alpha = gamma_now / curve_now
        else:
            beta = gamma_now / gamma_old
            alpha = gamma_now / (curve_now - beta * gamma_now / alpha_old)
            beta_all = jnp.broadcast_to(beta, (8, 128))
        gamma_old, alpha_old = gamma_now, alpha
        alpha_all = jnp.broadcast_to(alpha, (8, 128))

        def early(step, carry):
            for j in range(9):
                at_j = at_rows(j, step)
                d = z_ref[at_j, :]
                q = cz_ref[at_j, :]
                if it > 0:
                    d = d + beta_all * d_ref[at_j, :]
                    q = q + beta_all * q_ref[at_j, :]
                s = alpha_all * d
                if it > 0:
                    s = s_ref[at_j, :] + s
                if not last:
                    d_ref[at_j, :] = d
                q_ref[at_j, :] = q
                s_ref[at_j, :] = s
            return carry

        lax.fori_loop(0, mine // 8, early, 0)
        for h in range(PIECES):
            left_cam(*p_args(h))
        left_cam(*dc_args)

        def to_native(src, out):
            def body(b, carry):
                lanes = pl.ds(pl.multiple_of((first_block + b) * 128, 128), 128)
                out[:, lanes] = src[pl.ds(b, 9, stride=mine), :]
                return carry

            lax.fori_loop(0, mine, body, 0, unroll=4)

        def out_swap(which, out):
            half = out.at[:, lanes_here]
            return swap(half, half, out_sem.at[which, 0], out_sem.at[which, 1])

        if last:
            to_native(s_ref, sol_out)
            out_swap(0, sol_out).start()

        def late(g, step):
            some = range(g * (9 // GROUPS), (g + 1) * (9 // GROUPS))
            here_j = pl.ds(pl.multiple_of(step * 16, 16), 16)
            r = {}
            for j in some:
                lanes = slice((j - some[0]) * 128, (j - some[0] + 1) * 128)
                term = w_all[parity, g, 0, here_j, lanes].astype(F32)
                for k in range(1, n_z):
                    term = term + w_all[parity, g, k, here_j, lanes].astype(F32)
                for e in range(2):
                    at_e = at_rows(j, 2 * step + e)
                    q = q_ref[at_e, :] - term[8 * e : 8 * e + 8]
                    q_ref[at_e, :] = q
                    value = r_ref[at_e, :] - alpha_all * q
                    r_ref[at_e, :] = value
                    r[j, e] = value
            if last:
                return
            for i in range(9):
                zz = []
                for e in range(2):
                    z = pre_d[i, at_rows(some[0], 2 * step + e), :] * r[some[0], e]
                    for j in some[1:]:
                        z = z + pre_d[i, at_rows(j, 2 * step + e), :] * r[j, e]
                    if g > 0:
                        z = z_ref[at_rows(i, 2 * step + e), :] + z
                    z_ref[at_rows(i, 2 * step + e), :] = z
                    zz.append(z)
                if g + 1 == GROUPS:
                    z_all[core, here_j, 128 * i : 128 * i + 128] = jnp.concatenate(
                        zz, axis=0
                    ).astype(BF16)

        for g in range(GROUPS):
            for k in range(1, n_z):
                along_z(k, z_peer(k), *w_args(g)).wait_recv()

            def late_step(step, carry):
                late(g, step)
                return carry

            lax.fori_loop(0, mine // 16, late_step, 0)

        def left_z():
            for g in range(GROUPS):
                for k in range(1, n_z):
                    along_z(k, z_peer(k), *w_args(g)).wait_send()

        if not last:
            z_swap.start()
            left_z()
        else:
            to_native(r_ref, res_out)
            out_swap(1, res_out).start()
            left_z()
            out_swap(0, sol_out).wait()
            out_swap(1, res_out).wait()


def hand_out(sol, res, sol_out, res_out, sem):
    copies = [
        pltpu.make_async_copy(sol, sol_out, sem.at[0]),
        pltpu.make_async_copy(res, res_out, sem.at[1]),
    ]
    for copy in copies:
        copy.start()
    for copy in copies:
        copy.wait()


def per_device(n_cam, n_pts, rhs, cam_block, coupling, point_inverse, precond, tile_index, tile_count):
    tiles, slots = tile_index.shape
    cams = rhs.shape[1]
    blocks = cams // 128
    mine = blocks // 2
    pairs = tiles * slots
    half = tiles // 2 // PIECES
    vec = pltpu.VMEM((9 * mine, 128), F32)
    whole = pl.BlockSpec(memory_space=pltpu.VMEM)
    hbm = pl.BlockSpec(memory_space=pltpu.HBM)
    dma = pltpu.SemaphoreType.DMA
    group = 9 // GROUPS * 128
    big = (tile_index.T, tile_count.T, rhs, point_inverse, cam_block, precond, coupling)
    big = [pltpu.with_memory_space_constraint(x, pltpu.HBM) for x in big]
    results = pl.pallas_call(
        functools.partial(kernel, n_cam, n_pts),
        out_shape=(jax.ShapeDtypeStruct(rhs.shape, F32), jax.ShapeDtypeStruct(rhs.shape, F32)),
        in_specs=[hbm] * 7,
        out_specs=(whole, whole),
        scratch_shapes=[
            pltpu.VMEM((slots, tiles), jnp.int32),
            pltpu.VMEM((1, tiles), jnp.int32),
            pltpu.VMEM(coupling.shape, BF16),
            pltpu.VMEM((9, 9, mine * 128), F32),
            pltpu.VMEM(precond.shape, F32),
            pltpu.VMEM(rhs.shape, F32),
            pltpu.VMEM(point_inverse.shape, F32),
            pltpu.VMEM((9, 9 * mine, 128), F32),
            pltpu.VMEM((9, 9 * mine, 128), F32),
            pltpu.VMEM((3, 3 * tiles // 2, 128), F32),
            pltpu.VMEM((9 * blocks, 128), F32),
            vec, vec, vec, vec, vec, vec,
            pltpu.VMEM((pairs, blocks), BF16),
            pltpu.VMEM((blocks, pairs), BF16),
            pltpu.VMEM((pairs, 128), F32),
            pltpu.VMEM((9 * 128, 144), BF16),
            pltpu.VMEM((144, 9 * 128), BF16),
            pltpu.VMEM((2 * half, 8 * half), BF16),
            pltpu.VMEM((pairs, 9 * 128), BF16),
            pltpu.VMEM((pairs, 144), F32),
            pltpu.VMEM((8 * half, 384), F32),
            pltpu.VMEM((pairs, 144), F32),
            pltpu.VMEM((GROUPS, 8 * half, 144 // GROUPS), F32),
            pltpu.VMEM((GROUPS, pairs, group), BF16),
            pltpu.VMEM((tiles // 2, 384), F32),
            pltpu.VMEM((tiles // 2, 384), F32),
            pltpu.VMEM((2, PIECES, n_cam, half, 384), BF16),
            pltpu.VMEM((2, mine, 9 * 128), BF16),
            pltpu.VMEM((GROUPS, 2, mine, group), BF16),
            pltpu.VMEM((GROUPS, mine, group), BF16),
            pltpu.VMEM((2, GROUPS, n_pts // 2, mine, group), BF16),
            pltpu.VMEM((2, n_cam, 2, 128), F32),
            pltpu.VMEM((2, n_pts, 4, 128), F32),
            dma((CHUNKS,)), dma, dma, dma, dma, dma, dma,
            dma((PIECES, n_cam)), dma((2, PIECES, n_cam)),
            dma((2,)),
            dma((GROUPS,)), dma((GROUPS,)),
            dma((GROUPS, n_pts // 2)), dma((2, GROUPS, n_pts // 2)),
            dma((n_cam,)), dma((2, n_cam)),
            dma((n_pts,)), dma((2, n_pts)),
            dma((2, 2)),
        ],
        compiler_params=pltpu.CompilerParams(
            collective_id=0, has_side_effects=True, vmem_limit_bytes=52 * 2**20
        ),
    )(*big)
    return pl.pallas_call(
        hand_out,
        out_shape=(jax.ShapeDtypeStruct(rhs.shape, F32), jax.ShapeDtypeStruct(rhs.shape, F32)),
        in_specs=[pl.BlockSpec(memory_space=pl.ANY)] * 2,
        out_specs=(hbm, hbm),
        scratch_shapes=[dma((2,))],
        compiler_params=pltpu.CompilerParams(vmem_limit_bytes=2**20),
    )(*results)


def solution(mesh):
    in_specs = (
        P(None, "cam"),
        P(None, None, "cam"),
        P("pts", None, "cam"),
        P(None, None, "pts"),
        P(None, None, "cam"),
        P("pts", "cam"),
        P("pts", "cam"),
    )
    out_specs = (P(None, "cam"), P(None, "cam"))
    body = functools.partial(per_device, mesh.shape["cam"], mesh.shape["pts"])
    return jax.shard_map(body, mesh=mesh, in_specs=in_specs, out_specs=out_specs, check_vma=False)
```

```python
import functools

import jax
import jax.numpy as jnp
from jax import lax
from jax.experimental import pallas as pl
from jax.experimental.pallas import tpu as pltpu
from jax.sharding import PartitionSpec as P

ITERS = 3
F32 = jnp.float32
BF16 = jnp.bfloat16
CHUNKS = 16
PIECES = 4
UNROLL = 8
GROUPS = 3
MESH = pl.DeviceIdType.MESH


def iota(shape, axis):
    return lax.broadcasted_iota(jnp.int32, shape, axis)


def one_hot(where):
    return jnp.where(where, 1.0, 0.0).astype(BF16)


def kernel(
    n_cam, n_pts,
    idx_hbm, count_hbm, rhs_hbm, inv_hbm, cam_hbm, pre_hbm, blk_hbm,
    sol_out, res_out,
    idx_ref, count_ref, blk, cam_nat, pre_nat, rhs_nat, inv_nat, cam_d, pre_d, inv_d,
    z_first, r_ref, z_ref, d_ref, s_ref, q_ref, cz_ref,
    pick, place, mask, fold, fold_t, group,
    gath, rows, mid, contrib, contrib_last, wide_ref, even, odd,
    p_recv, z_all, t_send, t_recv, w_all, dots_c, dots_p,
    blk_sem, cam_sem, pre_sem, rhs_sem, inv_sem, idx_sem, count_sem,
    ps_s, ps_r, z_sem, t_s, t_r, w_s, w_r, dc_s, dc_r, dp_s, dp_r, out_sem,
):
    me_c = lax.axis_index("cam")
    me_p = lax.axis_index("pts")
    tiles = blk.shape[0]
    pairs = tiles // 2
    slots = 4 * tiles
    per_piece = pairs // PIECES
    per_chunk = tiles // CHUNKS
    blocks = place.shape[0]
    core = lax.rem(me_p, 2)
    me_z = me_p // 2
    n_z = n_pts // 2
    mine = blocks // 2
    first_block = core * mine
    lanes_here = pl.ds(pl.multiple_of(first_block * 128, mine * 128), mine * 128)

    pre_copy = pltpu.make_async_copy(pre_hbm, pre_nat, pre_sem)
    cam_copy = pltpu.make_async_copy(cam_hbm.at[:, :, lanes_here], cam_nat, cam_sem)
    rhs_copy = pltpu.make_async_copy(rhs_hbm, rhs_nat, rhs_sem)
    inv_copy = pltpu.make_async_copy(inv_hbm, inv_nat, inv_sem)

    def blk_copy(c):
        part = pl.ds(c * per_chunk, per_chunk)
        return pltpu.make_async_copy(blk_hbm.at[part], blk.at[part], blk_sem.at[c])

    barrier = pltpu.get_barrier_semaphore()

    def pts_peer(k):
        return lax.rem(me_p + k, n_pts)

    side = 4
    far = [(dy, dx) for dy in range(n_cam // side) for dx in range(side)][1:]
    far.sort(key=lambda at: -min(at[0], n_cam // side - at[0]) - min(at[1], side - at[1]))
    far = [
        lax.rem(me_c // side + dy, n_cam // side) * side + lax.rem(lax.rem(me_c, side) + dx, side)
        for dy, dx in far
    ]

    others = [pts_peer(k) for k in range(1, n_pts)]

    for peer in far:
        pl.semaphore_signal(barrier, inc=1, device_id=(peer, me_p), device_id_type=MESH)
    for peer in others:
        pl.semaphore_signal(barrier, inc=1, device_id=(me_c, peer), device_id_type=MESH)

    idx_copy = pltpu.make_async_copy(idx_hbm, idx_ref, idx_sem)
    count_copy = pltpu.make_async_copy(count_hbm, count_ref, count_sem)
    idx_copy.start()
    count_copy.start()
    rhs_copy.start()
    pre_copy.start()

    def start_chunk(c, carry):
        blk_copy(c).start()
        return carry

    lax.fori_loop(0, CHUNKS, start_chunk, 0)
    inv_copy.start()
    cam_copy.start()

    def cam_copy_to(peer, slot, src, dst, ssem, rsem):
        return pltpu.make_async_remote_copy(
            src_ref=src(peer), dst_ref=dst(slot), send_sem=ssem.at[peer],
            recv_sem=rsem.at[slot], device_id=(peer, me_p), device_id_type=MESH,
        )

    def pts_copy_to(peer, slot, src, dst, ssem, rsem):
        return pltpu.make_async_remote_copy(
            src_ref=src(peer), dst_ref=dst(slot), send_sem=ssem.at[peer],
            recv_sem=rsem.at[slot], device_id=(me_c, peer), device_id_type=MESH,
        )

    def start_cam(*args):
        for peer in far:
            cam_copy_to(peer, me_c, *args).start()

    def arrive_cam(*args):
        for peer in far[::-1]:
            cam_copy_to(peer, peer, *args).wait_recv()

    def left_cam(*args):
        for peer in far:
            cam_copy_to(peer, peer, *args).wait_send()

    def start_pts(*args):
        for peer in others:
            pts_copy_to(peer, me_p, *args).start()

    def wait_pts(*args):
        for peer in others:
            copy = pts_copy_to(peer, peer, *args)
            copy.wait_recv()
            copy.wait_send()

    def swap(src, dst, ssem, rsem):
        return pltpu.make_async_remote_copy(
            src_ref=src, dst_ref=dst, send_sem=ssem, recv_sem=rsem,
            device_id=(me_c, me_z * 2 + 1 - core), device_id_type=MESH,
        )

    def z_peer(k):
        return lax.rem(me_z + k, n_z)

    def along_z(k, slot, src, dst, ssem, rsem):
        return pltpu.make_async_remote_copy(
            src_ref=src, dst_ref=dst(slot), send_sem=ssem.at[k], recv_sem=rsem.at[slot],
            device_id=(me_c, z_peer(k) * 2 + core), device_id_type=MESH,
        )

    def at_rows(j, step):
        return pl.ds(pl.multiple_of(j * mine + step * 8, 8), 8)

    def to_dense_blocks(src, start, dst):
        def body(b, carry):
            lanes = pl.ds(pl.multiple_of((start + b) * 128, 128), 128)
            for i in range(9):
                dst[i, pl.ds(b, 9, stride=mine), :] = src[i, :, lanes]
            return carry

        lax.fori_loop(0, mine, body, 0)

    def apply_row(mat, vec, i, step):
        total = mat[i, at_rows(0, step), :] * vec[0]
        for j in range(1, 9):
            total = total + mat[i, at_rows(j, step), :] * vec[j]
        return total

    z_swap = swap(z_all.at[core], z_all.at[core], z_sem.at[0], z_sem.at[1])

    at = iota((9 * 128, 144), 0)
    fold[...] = one_hot(iota((9 * 128, 144), 1) == (at // 128) * 16 + lax.rem(at, 16))
    at = iota((144, 9 * 128), 1)
    fold_t[...] = one_hot(iota((144, 9 * 128), 0) == (at // 128) * 16 + lax.rem(at, 16))
    row = iota((2 * per_piece, 8 * per_piece), 0)
    col = iota((2 * per_piece, 8 * per_piece), 1)
    group[...] = one_hot(
        (col // 8 == lax.rem(row, per_piece)) & (lax.rem(col, 8) // 4 == row // per_piece)
    )
    idx_copy.wait()
    count_copy.wait()
    index = idx_ref[...]
    used = iota((4, tiles), 0) < count_ref[...]
    spread = one_hot(iota((slots, tiles), 0) // 4 == iota((slots, tiles), 1))
    here = iota((slots, 4), 1) == lax.rem(iota((slots, 4), 0), 4)

    def column(value):
        wide = lax.dot_general(
            spread, value.astype(F32).astype(BF16), (((1,), (1,)), ((), ())),
            preferred_element_type=F32,
        )
        return jnp.sum(jnp.where(here, wide, 0.0), axis=1, keepdims=True)

    chosen = jnp.where(
        iota((slots, blocks), 1).astype(F32) == column(jnp.where(used, index // 8, -1)), 1.0, 0.0
    )
    pick[...] = chosen.astype(BF16)
    place[...] = jnp.transpose(chosen).astype(BF16)
    mask[...] = jnp.where(
        (iota((slots, 128), 1) // 16).astype(F32) == column(lax.rem(index, 8)), 1.0, 0.0
    )

    rhs_copy.wait()
    pre_copy.wait()

    def first(b, carry):
        lanes = pl.ds(pl.multiple_of(b * 128, 128), 128)
        total = pre_nat[0, :, lanes] * rhs_nat[pl.ds(0, 1), lanes]
        for j in range(1, 9):
            total = total + pre_nat[j, :, lanes] * rhs_nat[pl.ds(j, 1), lanes]
        z_first[pl.ds(b, 9, stride=blocks), :] = total
        return carry

    lax.fori_loop(0, blocks, first, 0, unroll=2)
    for j in range(9):
        for o in range(2):
            at = j * blocks + o * mine
            z_all[o, :, 128 * j : 128 * j + 128] = z_first[at : at + mine, :].astype(BF16)

    row8 = iota((8, 768), 0)
    diag = iota((8, 768), 1) // 192 == lax.rem(row8, 4)
    upper = row8 < 4
    first_tile = lax.rem(iota((per_piece, 384), 1), 128) < 64
    order = (0, 2, 1)

    gamma_old = None
    alpha_old = None
    for it in range(ITERS):
        last = it + 1 == ITERS
        parity = it % 2
        if it > 0:
            z_swap.wait()
        for j in range(9):
            wide = z_all[:, :, 128 * j : 128 * j + 128].astype(F32).reshape(blocks, 128)
            picked = jnp.dot(pick[...], wide.astype(BF16), preferred_element_type=F32)
            gath[:, 128 * j : 128 * j + 128] = (picked * mask[...]).astype(BF16)
        rows[...] = jnp.dot(gath[...], fold[...], preferred_element_type=F32)

        def forward(j, h):
            left = rows[pl.ds(pl.multiple_of(8 * j, 8), 8), :].astype(BF16)
            one = jnp.dot(left, blk[2 * j], preferred_element_type=F32)
            two = jnp.dot(left, blk[2 * j + 1], preferred_element_type=F32)
            both = jnp.where(diag, jnp.where(upper, one, two), 0.0)
            mid[pl.ds(pl.multiple_of(8 * (j - h * per_piece), 8), 8), :] = (
                both[:, :384] + both[:, 384:]
            )

        def p_args(h):
            return (
                lambda peer: p_recv.at[parity, h, me_c],
                lambda slot: p_recv.at[parity, h, slot],
                ps_s.at[h],
                ps_r.at[parity, h],
            )

        for h in range(PIECES):
            if it == 0:

                def forward_chunk(c, carry):
                    blk_copy(c).wait()
                    for k in range(per_chunk // 2):
                        forward(c * (per_chunk // 2) + k, h)
                    return carry

                some = CHUNKS // PIECES
                lax.fori_loop(h * some, (h + 1) * some, forward_chunk, 0)
            else:

                def forward_some(c, carry):
                    for k in range(UNROLL):
                        forward(UNROLL * c + k, h)
                    return carry

                some = per_piece // UNROLL
                lax.fori_loop(h * some, (h + 1) * some, forward_some, 0)
            full = mid[...]
            high = full.astype(BF16)
            low = (full - high.astype(F32)).astype(BF16)
            summed = jnp.dot(group[...], high, preferred_element_type=F32) + jnp.dot(
                group[...], low, preferred_element_type=F32
            )
            summed = summed + pltpu.roll(summed, 192, 1)
            p_recv[parity, h, me_c] = jnp.where(
                first_tile, summed[:per_piece], pltpu.roll(summed[per_piece:], 64, 1)
            ).astype(BF16)
            if it == 0 and h == 0:
                pl.semaphore_wait(barrier, n_cam + n_pts - 2)
            start_cam(*p_args(h))

        if it == 0:

            def inv_dense(b, carry):
                for i in range(3):
                    inv_d[i, pl.ds(b, 3, stride=pairs), :] = inv_nat[
                        i, :, pl.ds(pl.multiple_of(b * 128, 128), 128)
                    ]
                return carry

            inv_copy.wait()
            lax.fori_loop(0, pairs, inv_dense, 0, unroll=4)
            for j in range(9):
                rows_j = pl.ds(pl.multiple_of(j * blocks + first_block, 8), mine)
                z_ref[j * mine : (j + 1) * mine, :] = z_first[rows_j, :]

            def rhs_dense(b, carry):
                lanes = pl.ds(pl.multiple_of((first_block + b) * 128, 128), 128)
                r_ref[pl.ds(b, 9, stride=mine), :] = rhs_nat[:, lanes]
                return carry

            lax.fori_loop(0, mine, rhs_dense, 0, unroll=4)
            cam_copy.wait()
            to_dense_blocks(cam_nat, 0, cam_d)

        def shares(step, carry):
            gamma, curve = carry
            z = [z_ref[at_rows(j, step), :] for j in range(9)]
            for i in range(9):
                cz = apply_row(cam_d, z, i, step)
                cz_ref[at_rows(i, step), :] = cz
                curve = curve + z[i] * cz
                gamma = gamma + z[i] * r_ref[at_rows(i, step), :]
            return gamma, curve

        zero = jnp.zeros((8, 128), F32)
        gamma, curve = lax.fori_loop(0, mine // 8, shares, (zero, zero))
        dots_c[parity, me_c, 0:1, :] = jnp.sum(gamma, axis=0, keepdims=True)
        dots_c[parity, me_c, 1:2, :] = jnp.sum(curve, axis=0, keepdims=True)
        dc_args = (
            lambda peer: dots_c.at[parity, me_c],
            lambda slot: dots_c.at[parity, slot],
            dc_s,
            dc_r.at[parity],
        )
        start_cam(*dc_args)

        def backward(j, lines, out, at):
            both = jnp.where(
                upper[:, :384],
                jnp.broadcast_to(even[pl.ds(j, 1), :], (8, 384)),
                jnp.broadcast_to(odd[pl.ds(j, 1), :], (8, 384)),
            )
            left = jnp.where(diag, jnp.concatenate([both, both], axis=1), 0.0).astype(BF16)
            contract = (((1,), (1,)), ((), ()))
            one = lax.dot_general(left, blk[2 * j, lines, :], contract, preferred_element_type=F32)
            two = lax.dot_general(
                left, blk[2 * j + 1, lines, :], contract, preferred_element_type=F32
            )
            out[at, :] = jnp.where(upper[:, : one.shape[1]], one, two)

        width = 9 // GROUPS * 128
        mask_wide = jnp.concatenate([mask[...]] * (9 // GROUPS), axis=1)
        early_rows = 8 * per_piece * (PIECES - 1)
        energy = jnp.zeros((per_piece, 128), F32)
        for h in range(PIECES):
            if h + 1 == PIECES:
                contrib_half = contrib[0:early_rows, :].astype(BF16)
                for g in range(GROUPS):
                    wide = jnp.dot(
                        contrib_half, fold_t[:, g * width : (g + 1) * width],
                        preferred_element_type=F32,
                    )
                    wide_ref[g, 0:early_rows, :] = (wide * mask_wide[:early_rows]).astype(BF16)
            arrive_cam(*p_args(h))
            total = p_recv[parity, h, 0].astype(F32)
            for k in range(1, n_cam):
                total = total + p_recv[parity, h, k].astype(F32)
            sums = [None] * 3
            for place_i, i in enumerate(order):
                sums[i] = total[:, 128 * place_i : 128 * place_i + 128]
            here_h = slice(h * per_piece, (h + 1) * per_piece)
            answers = []
            for i in order:
                answer = jnp.zeros((per_piece, 128), F32)
                for j in range(3):
                    at_j = slice(j * pairs + h * per_piece, j * pairs + (h + 1) * per_piece)
                    answer = answer + inv_d[i, at_j, :] * sums[j]
                answer = answer.astype(BF16).astype(F32)
                energy = energy + answer * sums[i]
                answers.append(answer)
            answer = jnp.concatenate(answers, axis=1)
            a = jnp.where(first_tile, answer, 0.0)
            even[here_h, :] = a + pltpu.roll(a, 192, 1)
            a = pltpu.roll(jnp.where(first_tile, 0.0, answer), 320, 1)
            odd[here_h, :] = a + pltpu.roll(a, 192, 1)
            if h + 1 == PIECES:
                arrive_cam(*dc_args)
                total = dots_c[parity, 0]
                for k in range(1, n_cam):
                    total = total + dots_c[parity, k]
                dots_p[parity, me_p, 0:2, :] = total[0:2]
                dots_p[parity, me_p, 2:3, :] = jnp.sum(energy, axis=0, keepdims=True)
                dots_p[parity, me_p, 3:4, :] = jnp.sum(energy, axis=0, keepdims=True)
                dp_args = (
                    lambda peer: dots_p.at[parity, me_p],
                    lambda slot: dots_p.at[parity, slot],
                    dp_s,
                    dp_r.at[parity],
                )
                start_pts(*dp_args)

            if h + 1 < PIECES:

                def backward_some(c, carry):
                    for k in range(UNROLL):
                        j = UNROLL * c + k
                        backward(j, slice(0, 144), contrib, pl.ds(pl.multiple_of(8 * j, 8), 8))
                    return carry

                some = per_piece // UNROLL
                lax.fori_loop(h * some, (h + 1) * some, backward_some, 0)

        def w_args(g):
            return (
                w_all.at[parity, g, me_z],
                lambda slot: w_all.at[parity, g, slot],
                w_s.at[g],
                w_r.at[parity, g],
            )

        def send_along_z(g):
            t_swaps[g].wait()
            w_all[parity, g, me_z] = (
                t_send[g, core].astype(F32) + t_recv[g].astype(F32)
            ).astype(BF16)
            for k in (2, 1, 3):
                along_z(k, me_z, *w_args(g)).start()

        t_swaps = []
        lines = 144 // GROUPS
        for g in range(GROUPS):
            for k in range(per_piece):
                backward(
                    (PIECES - 1) * per_piece + k, slice(g * lines, (g + 1) * lines),
                    contrib_last.at[g], slice(8 * k, 8 * k + 8),
                )
            wide = jnp.dot(
                contrib_last[g].astype(BF16), fold_t[0:lines, 0:width], preferred_element_type=F32
            )
            wide_ref[g, early_rows:, :] = (wide * mask_wide[early_rows:]).astype(BF16)
            put = jnp.dot(place[...], wide_ref[g], preferred_element_type=F32)
            for o in range(2):
                t_send[g, o] = put[o * mine : (o + 1) * mine, :].astype(BF16)
            t_swaps.append(swap(t_send.at[g, 1 - core], t_recv.at[g], t_s.at[g], t_r.at[g]))
            t_swaps[g].start()
            if g > 0:
                send_along_z(g - 1)
        send_along_z(GROUPS - 1)
        if it == 0:
            to_dense_blocks(pre_nat, first_block, pre_d)

        wait_pts(*dp_args)
        total = dots_p[parity, 0]
        for k in range(1, n_pts):
            total = total + dots_p[parity, k]
        energy_now = jnp.sum(total[2:3], axis=1, keepdims=True)
        total = dots_p[parity, 0] + dots_p[parity, 1]
        total = jnp.sum(total, axis=1, keepdims=True)
        gamma_now = total[0:1]
        curve_now = total[1:2] - energy_now
        if it == 0:
            alpha = gamma_now / curve_now
        else:
            beta = gamma_now / gamma_old
            alpha = gamma_now / (curve_now - beta * gamma_now / alpha_old)
            beta_all = jnp.broadcast_to(beta, (8, 128))
        gamma_old, alpha_old = gamma_now, alpha
        alpha_all = jnp.broadcast_to(alpha, (8, 128))

        def early(step, carry):
            for j in range(9):
                at_j = at_rows(j, step)
                d = z_ref[at_j, :]
                q = cz_ref[at_j, :]
                if it > 0:
                    d = d + beta_all * d_ref[at_j, :]
                    q = q + beta_all * q_ref[at_j, :]
                s = alpha_all * d
                if it > 0:
                    s = s_ref[at_j, :] + s
                if not last:
                    d_ref[at_j, :] = d
                q_ref[at_j, :] = q
                s_ref[at_j, :] = s
            return carry

        lax.fori_loop(0, mine // 8, early, 0)
        for h in range(PIECES):
            left_cam(*p_args(h))
        left_cam(*dc_args)

        def to_native(src, out):
            def body(b, carry):
                lanes = pl.ds(pl.multiple_of((first_block + b) * 128, 128), 128)
                out[:, lanes] = src[pl.ds(b, 9, stride=mine), :]
                return carry

            lax.fori_loop(0, mine, body, 0, unroll=4)

        def out_swap(which, out):
            half = out.at[:, lanes_here]
            return swap(half, half, out_sem.at[which, 0], out_sem.at[which, 1])

        if last:
            to_native(s_ref, sol_out)
            out_swap(0, sol_out).start()

        def late(g, step):
            some = range(g * (9 // GROUPS), (g + 1) * (9 // GROUPS))
            here_j = pl.ds(pl.multiple_of(step * 16, 16), 16)
            r = {}
            for j in some:
                lanes = slice((j - some[0]) * 128, (j - some[0] + 1) * 128)
                term = w_all[parity, g, 0, here_j, lanes].astype(F32)
                for k in range(1, n_z):
                    term = term + w_all[parity, g, k, here_j, lanes].astype(F32)
                for e in range(2):
                    at_e = at_rows(j, 2 * step + e)
                    q = q_ref[at_e, :] - term[8 * e : 8 * e + 8]
                    q_ref[at_e, :] = q
                    value = r_ref[at_e, :] - alpha_all * q
                    r_ref[at_e, :] = value
                    r[j, e] = value
            if last:
                return
            for i in range(9):
                zz = []
                for e in range(2):
                    z = pre_d[i, at_rows(some[0], 2 * step + e), :] * r[some[0], e]
                    for j in some[1:]:
                        z = z + pre_d[i, at_rows(j, 2 * step + e), :] * r[j, e]
                    if g > 0:
                        z = z_ref[at_rows(i, 2 * step + e), :] + z
                    z_ref[at_rows(i, 2 * step + e), :] = z
                    zz.append(z)
                if g + 1 == GROUPS:
                    z_all[core, here_j, 128 * i : 128 * i + 128] = jnp.concatenate(
                        zz, axis=0
                    ).astype(BF16)

        for g in range(GROUPS):
            for k in range(1, n_z):
                along_z(k, z_peer(k), *w_args(g)).wait_recv()

            def late_step(step, carry):
                late(g, step)
                return carry

            lax.fori_loop(0, mine // 16, late_step, 0)

        def left_z():
            for g in range(GROUPS):
                for k in range(1, n_z):
                    along_z(k, z_peer(k), *w_args(g)).wait_send()

        if not last:
            z_swap.start()
            left_z()
        else:
            to_native(r_ref, res_out)
            out_swap(1, res_out).start()
            left_z()
            out_swap(0, sol_out).wait()
            out_swap(1, res_out).wait()


def hand_out(sol, res, sol_out, res_out, sem):
    copies = [
        pltpu.make_async_copy(sol, sol_out, sem.at[0]),
        pltpu.make_async_copy(res, res_out, sem.at[1]),
    ]
    for copy in copies:
        copy.start()
    for copy in copies:
        copy.wait()


def per_device(n_cam, n_pts, rhs, cam_block, coupling, point_inverse, precond, tile_index, tile_count):
    tiles, slots = tile_index.shape
    cams = rhs.shape[1]
    blocks = cams // 128
    mine = blocks // 2
    pairs = tiles * slots
    half = tiles // 2 // PIECES
    vec = pltpu.VMEM((9 * mine, 128), F32)
    whole = pl.BlockSpec(memory_space=pltpu.VMEM)
    hbm = pl.BlockSpec(memory_space=pltpu.HBM)
    dma = pltpu.SemaphoreType.DMA
    group = 9 // GROUPS * 128
    big = (tile_index.T, tile_count.T, rhs, point_inverse, cam_block, precond, coupling)
    big = [pltpu.with_memory_space_constraint(x, pltpu.HBM) for x in big]
    results = pl.pallas_call(
        functools.partial(kernel, n_cam, n_pts),
        out_shape=(jax.ShapeDtypeStruct(rhs.shape, F32), jax.ShapeDtypeStruct(rhs.shape, F32)),
        in_specs=[hbm] * 7,
        out_specs=(whole, whole),
        scratch_shapes=[
            pltpu.VMEM((slots, tiles), jnp.int32),
            pltpu.VMEM((1, tiles), jnp.int32),
            pltpu.VMEM(coupling.shape, BF16),
            pltpu.VMEM((9, 9, mine * 128), F32),
            pltpu.VMEM(precond.shape, F32),
            pltpu.VMEM(rhs.shape, F32),
            pltpu.VMEM(point_inverse.shape, F32),
            pltpu.VMEM((9, 9 * mine, 128), F32),
            pltpu.VMEM((9, 9 * mine, 128), F32),
            pltpu.VMEM((3, 3 * tiles // 2, 128), F32),
            pltpu.VMEM((9 * blocks, 128), F32),
            vec, vec, vec, vec, vec, vec,
            pltpu.VMEM((pairs, blocks), BF16),
            pltpu.VMEM((blocks, pairs), BF16),
            pltpu.VMEM((pairs, 128), F32),
            pltpu.VMEM((9 * 128, 144), BF16),
            pltpu.VMEM((144, 9 * 128), BF16),
            pltpu.VMEM((2 * half, 8 * half), BF16),
            pltpu.VMEM((pairs, 9 * 128), BF16),
            pltpu.VMEM((pairs, 144), F32),
            pltpu.VMEM((8 * half, 384), F32),
            pltpu.VMEM((pairs, 144), F32),
            pltpu.VMEM((GROUPS, 8 * half, 144 // GROUPS), F32),
            pltpu.VMEM((GROUPS, pairs, group), BF16),
            pltpu.VMEM((tiles // 2, 384), F32),
            pltpu.VMEM((tiles // 2, 384), F32),
            pltpu.VMEM((2, PIECES, n_cam, half, 384), BF16),
            pltpu.VMEM((2, mine, 9 * 128), BF16),
            pltpu.VMEM((GROUPS, 2, mine, group), BF16),
            pltpu.VMEM((GROUPS, mine, group), BF16),
            pltpu.VMEM((2, GROUPS, n_pts // 2, mine, group), BF16),
            pltpu.VMEM((2, n_cam, 2, 128), F32),
            pltpu.VMEM((2, n_pts, 4, 128), F32),
            dma((CHUNKS,)), dma, dma, dma, dma, dma, dma,
            dma((PIECES, n_cam)), dma((2, PIECES, n_cam)),
            dma((2,)),
            dma((GROUPS,)), dma((GROUPS,)),
            dma((GROUPS, n_pts // 2)), dma((2, GROUPS, n_pts // 2)),
            dma((n_cam,)), dma((2, n_cam)),
            dma((n_pts,)), dma((2, n_pts)),
            dma((2, 2)),
        ],
        compiler_params=pltpu.CompilerParams(
            collective_id=0, has_side_effects=True, vmem_limit_bytes=52 * 2**20
        ),
    )(*big)
    return pl.pallas_call(
        hand_out,
        out_shape=(jax.ShapeDtypeStruct(rhs.shape, F32), jax.ShapeDtypeStruct(rhs.shape, F32)),
        in_specs=[pl.BlockSpec(memory_space=pl.ANY)] * 2,
        out_specs=(hbm, hbm),
        scratch_shapes=[dma((2,))],
        compiler_params=pltpu.CompilerParams(vmem_limit_bytes=2**20),
    )(*results)


def solution(mesh):
    in_specs = (
        P(None, "cam"),
        P(None, None, "cam"),
        P("pts", None, "cam"),
        P(None, None, "pts"),
        P(None, None, "cam"),
        P("pts", "cam"),
        P("pts", "cam"),
    )
    out_specs = (P(None, "cam"), P(None, "cam"))
    body = functools.partial(per_device, mesh.shape["cam"], mesh.shape["pts"])
    return jax.shard_map(body, mesh=mesh, in_specs=in_specs, out_specs=out_specs, check_vma=False)
```
